256 devices in a mesh: lat: 8 (over x, y_hi), lon: 32 (over y_lo, z, core).
Axes of the slice: x: 4, y: 4 (y_hi: 2, y_lo: 2; y = y_hi * 2 + y_lo), z: 8, core: 2. Of those that a mesh axis runs over, the one named last changes fastest.
Arguments:
- field: bfloat16 [192, 768, 384], P('lat', 'lon'), may hold values from -6 to 6
- cotangent: bfloat16 [192, 768, 384], P('lat', 'lon'), may hold values from -6 to 6
- mix_weight: bfloat16 [3, 384, 384], replicated, may hold values from -0.1875 to 0.1875
- taps: float32 [192, 3, 3, 8], replicated, may hold values from -1.8 to 1.8
- offsets: int32 [192, 3, 8], replicated, may hold values from -8 to 8, as said below
- counts: int32 [192], replicated, may hold values from 1 to 8, as said below
Outputs:
- grad_field: bfloat16 [192, 768, 384], P('lat', 'lon')
- grad_spectra: float32 [2, 384, 384, 384], P(None, 'lat', 'lon')
- grad_mix: float32 [3, 384, 384], replicated
The draws below stay inside these ranges and needn't reach their ends.
Inputs may be any that keep to these rules, and one draw needn't show every extreme that they name: For every row and latitude offset the 8 longitude offsets are distinct. Tap slots of a row at or beyond counts are inactive; the polar rows use all 8.
All inputs are finite; a program needn't handle non-finite values.
Results may differ from the reference program's by a relative error of at most 0.0061.
Values may be sent and summed in bfloat16 or wider, within the bound.
No kernel may reach another device: no remote copies, remote signals or barrier semaphores. Data moves between devices by JAX's collectives and lax.ppermute only.
A program may use at most 64 MiB of HBM per device.

```python
import math
import jax
import jax.numpy as jnp
from jax import lax

C = 384
M = 384
L = 384
K = 3
R = 8
S = 8
LB = 32
NLAT = 192
NLON = 768


def reach_rows(row_total):
    row_ids = jnp.arange(row_total, dtype=jnp.int32)
    distance = jnp.minimum(row_ids, row_total - 1 - row_ids)
    return jnp.maximum(1, jnp.minimum(R, 2 * R // (distance + 1)))


def draw_offsets(key, part):
    reach_row = reach_rows(NLAT)
    candidates = jnp.arange(2 * R + 1, dtype=jnp.int32) - R
    scores = jax.random.randint(jax.random.fold_in(key, 11), (NLAT, 3, 2 * R + 1), 0, 1000, dtype=jnp.int32)
    scores = scores * (2 * R + 1) + candidates[None, None, :] + R
    outside = jnp.abs(candidates)[None, None, :] > reach_row[:, None, None]
    scores = jnp.where(outside, scores + 4000 * (2 * R + 1), scores)
    scores = jnp.where(candidates[None, None, :] == reach_row[:, None, None], -2, scores)
    scores = jnp.where(candidates[None, None, :] == -reach_row[:, None, None], -1, scores)
    ranked = jnp.argsort(scores, axis=-1)
    return (ranked[:, :, :S] - R).astype(jnp.int32)


def draw_counts(key, part):
    reach_row = reach_rows(NLAT)
    extra_taps = jax.random.randint(jax.random.fold_in(key, 23), (NLAT,), 0, 3, dtype=jnp.int32)
    return jnp.minimum(jnp.minimum(S, 1 + reach_row + extra_taps), 2 * reach_row + 1).astype(jnp.int32)


def level_of(rng, dims, shards, low, largest):
    def one(position, parts):
        heights = jax.random.uniform(jax.random.fold_in(jax.random.fold_in(rng, 6), position), (parts,), jnp.float32, low / len(shards), largest / len(shards))
        return jnp.repeat(jnp.exp(heights), dims[position] // parts).reshape((-1,) + (1,) * (len(dims) - position - 1))

    loudness = one(*shards[0])
    for cut in shards[1:]:
        loudness = loudness * one(*cut)
    return loudness


def bell_draw(own_key, dims, spread, reach, cuts=(), kind=jnp.bfloat16):
    drawn = spread * jax.random.normal(own_key, dims, jnp.float32)
    if cuts:
        drawn = drawn * level_of(own_key, dims, cuts, -0.22, 0.18)
    return jnp.clip(drawn, -reach, reach).astype(kind)


def setup_inputs(seed: int = 0) -> dict:
    key_of = jax.random.split(jax.random.key(seed), 7)
    field = bell_draw(key_of[0], (NLAT, NLON, C), 1.0, 6.0, ((0, 8), (1, 32)))
    cotangent = bell_draw(key_of[1], (NLAT, NLON, C), 1.0, 6.0, ((0, 8), (1, 32)))
    mix_weight = bell_draw(key_of[2], (K, C, C), (K * C) ** -0.5, 0.1875)
    taps = bell_draw(key_of[3], (NLAT, K, 3, S), 0.3, 1.8, (), jnp.float32)
    offsets = draw_offsets(jax.random.fold_in(key_of[6], 71), 0)
    counts = draw_counts(jax.random.fold_in(key_of[6], 71), 0)
    return dict(field=field, cotangent=cotangent, mix_weight=mix_weight, taps=taps, offsets=offsets, counts=counts)


def live_taps(taps, counts):
    slot_ids = lax.broadcasted_iota(jnp.int32, taps.shape, 3)
    keep_mask = slot_ids < counts[:, None, None, None]
    return jnp.where(keep_mask, taps, jnp.float32(0.0)).astype(jnp.bfloat16)

def dft_table(lon_total, orders):
    columns = lax.broadcasted_iota(jnp.int32, (lon_total,), 0)
    phases = orders[:, None] * columns[None, :] % lon_total
    angles = 2.0 * math.pi / lon_total * phases.astype(jnp.float32)
    return jnp.stack([jnp.cos(angles), -jnp.sin(angles)]).astype(jnp.bfloat16)

def colatitudes(lat_total):
    angles = (lax.broadcasted_iota(jnp.int32, (lat_total,), 0).astype(jnp.float32) + 0.5) * (math.pi / lat_total)
    return (jnp.cos(angles), jnp.log(jnp.sin(angles)))

def seed_logs(order_total):
    degrees = lax.broadcasted_iota(jnp.int32, (order_total,), 0).astype(jnp.float32)
    step_logs = jnp.log((2.0 * degrees + 1.0) / (2.0 * degrees + 2.0))
    prefix = jnp.concatenate([jnp.zeros((1,), jnp.float32), jnp.cumsum(step_logs)[:-1]])
    return 0.5 * jnp.log((2.0 * degrees + 1.0) / (4.0 * math.pi)) + 0.5 * prefix

def advance(degree, previous, earlier, orders, cosines):
    deg_f = jnp.asarray(degree).astype(jnp.float32)
    ord_f = orders.astype(jnp.float32)[:, None]
    higher = (degree > orders)[:, None]
    lower_a = jnp.where(higher, deg_f * deg_f - ord_f * ord_f, 1.0)
    factor_a = jnp.sqrt((4.0 * deg_f * deg_f - 1.0) / lower_a)
    upper_b = jnp.maximum((deg_f - 1.0) * (deg_f - 1.0) - ord_f * ord_f, 0.0)
    lower_b = jnp.maximum(4.0 * (deg_f - 1.0) * (deg_f - 1.0) - 1.0, 1.0)
    factor_b = jnp.sqrt(upper_b / lower_b)
    grown = factor_a * (cosines[None, :] * previous - factor_b * earlier)
    seeded = jnp.where((degree == orders)[:, None], jnp.float32(1.0), jnp.float32(0.0))
    return jnp.where(higher, grown, seeded)

def rescale(previous, earlier, scales):
    biggest = jnp.maximum(jnp.abs(previous), jnp.abs(earlier))
    divisor = jnp.where(biggest > 0.0, biggest, jnp.float32(1.0))
    return (previous / divisor, earlier / divisor, scales + jnp.log(divisor))

def legendre_range(start_block, orders, cosines, logscale, spec_part, result, row_offset, leg_scale):
    state_zero = jnp.zeros(logscale.shape, jnp.float32)

    def block_step(block_idx, loop_state):
        previous, earlier, scales, summed = loop_state
        factor = jnp.exp(scales)
        levels = []
        for inner_step in range(LB):
            degree = block_idx * LB + inner_step
            fresh = advance(degree, previous, earlier, orders, cosines)
            levels.append(fresh * factor)
            earlier, previous = (previous, fresh)
        contrib = jnp.einsum('lmt,pmct->pmcl', jnp.stack(levels), spec_part, precision=lax.Precision.HIGHEST) * leg_scale
        level_start = (block_idx * LB).astype(jnp.int32)
        zero_index = jnp.zeros((), jnp.int32)
        summed = lax.dynamic_update_slice(summed, contrib, (zero_index, jnp.asarray(row_offset).astype(jnp.int32), zero_index, level_start))
        previous, earlier, scales = rescale(previous, earlier, scales)
        return (previous, earlier, scales, summed)
    return lax.fori_loop(start_block, L // LB, block_step, (state_zero, state_zero, logscale, result))[3]

def reference(field, cotangent, mix_weight, taps, offsets, counts):
    live_table = live_taps(taps, counts)
    field_pad = jnp.pad(field, ((1, 1), (0, 0), (0, 0)))
    columns = jnp.arange(NLON, dtype=jnp.int32)
    row_ids = jnp.arange(NLAT, dtype=jnp.int32)

    def forward_row(mix_total, row_id):
        rows_three = lax.dynamic_slice_in_dim(field_pad, row_id, 3, 0)
        row_taps = live_table[row_id]
        row_shifts = offsets[row_id]
        summed = jnp.zeros((NLON, K, C), jnp.float32)
        for lat_step in range(3):
            for tap_slot in range(S):
                index_map = (columns + row_shifts[lat_step, tap_slot]) % NLON
                moved_rows = jnp.take(rows_three[lat_step], index_map, axis=0).astype(jnp.float32)
                summed = summed + moved_rows[:, None, :] * row_taps[:, lat_step, tap_slot].astype(jnp.float32)[None, :, None]
        response = lax.optimization_barrier(summed.astype(jnp.bfloat16)).astype(jnp.float32)
        grad_row = cotangent[row_id].astype(jnp.float32)
        mix_total = mix_total + jnp.einsum('fkc,fd->kcd', response, grad_row)
        return (mix_total, None)
    mix_total, ignored = lax.scan(forward_row, jnp.zeros((K, C, C), jnp.float32), row_ids)
    grad_mix = mix_total * (1.0 / math.sqrt(NLAT * NLON))
    weight_mat = jnp.transpose(mix_weight, (2, 0, 1)).reshape(C, K * C)

    def basis_row(row_vals):
        return jnp.dot(row_vals, weight_mat, preferred_element_type=jnp.float32).reshape(NLON, K, C).astype(jnp.bfloat16)
    grad_basis = lax.map(basis_row, cotangent)
    live_pad = jnp.pad(live_table, ((1, 1), (0, 0), (0, 0), (0, 0)))
    shift_pad = jnp.pad(offsets, ((1, 1), (0, 0), (0, 0)))

    def backward_row(row_id):
        summed = cotangent[row_id].astype(jnp.float32)
        for lat_step in range(3):
            source = row_id - lat_step + 1
            basis_one = grad_basis[jnp.clip(source, 0, NLAT - 1)]
            row_taps = live_pad[source + 1]
            row_shifts = shift_pad[source + 1]
            for tap_slot in range(S):
                index_map = (columns - row_shifts[lat_step, tap_slot]) % NLON
                moved_rows = jnp.take(basis_one, index_map, axis=0).astype(jnp.float32)
                summed = summed + jnp.einsum('fkc,k->fc', moved_rows, row_taps[:, lat_step, tap_slot].astype(jnp.float32))
        return summed.astype(jnp.bfloat16)
    grad_field = lax.map(backward_row, row_ids)
    dft_rows = dft_table(NLON, jnp.arange(M, dtype=jnp.int32))
    spectra = (jnp.einsum('tfc,pmf->pmct', grad_field.astype(jnp.float32), dft_rows.astype(jnp.float32)) * (1.0 / math.sqrt(NLON))).astype(jnp.bfloat16)
    cosines, log_sines = colatitudes(NLAT)
    orders = jnp.arange(M, dtype=jnp.int32)
    logscale = seed_logs(M)[:, None] + orders.astype(jnp.float32)[:, None] * log_sines[None, :]
    grad_spectra = legendre_range(0, orders, cosines, logscale, spectra.astype(jnp.float32), jnp.zeros((2, M, C, L), jnp.float32), 0, math.sqrt(4.0 * math.pi / NLAT))
    return (grad_field, grad_spectra, grad_mix)
```

```python
import functools
import math

import jax
import jax.numpy as jnp
import ml_dtypes
import numpy as np
from jax import lax
from jax.experimental import pallas as pl
from jax.experimental.pallas import tpu as pltpu
from jax.sharding import PartitionSpec as P

C = 384
M = 384
L = 384
K = 3
R = 8
S = 8
LB = 32
NLAT = 192
NLON = 768
LATS = 8
LONS = 32
TD = NLAT // LATS
FD = NLON // LONS
CD = C // LONS
MD = M // LATS
XW = FD + 2 * R
TP = 32
QUAD = 4
F32 = jnp.float32
BF16 = jnp.bfloat16
VMEM_BYTES = 56 * 1024 * 1024


def call(kernel, out_shape, **kw):
    return pl.pallas_call(
        kernel,
        out_shape=out_shape,
        compiler_params=pltpu.CompilerParams(vmem_limit_bytes=VMEM_BYTES),
        **kw,
    )


def shape(dims, dtype):
    return jax.ShapeDtypeStruct(dims, dtype)


def swap_blocks(parts):
    lane = lax.broadcasted_iota(jnp.int32, parts[0].shape, 1)
    low = lane < 64
    even = (lane & 32) == 0
    a0, a1, a2, a3 = parts
    b0 = jnp.where(low, a0, pltpu.roll(a2, 64, 1))
    b2 = jnp.where(low, pltpu.roll(a0, 64, 1), a2)
    b1 = jnp.where(low, a1, pltpu.roll(a3, 64, 1))
    b3 = jnp.where(low, pltpu.roll(a1, 64, 1), a3)
    c0 = jnp.where(even, b0, pltpu.roll(b1, 32, 1))
    c1 = jnp.where(even, pltpu.roll(b0, 96, 1), b1)
    c2 = jnp.where(even, b2, pltpu.roll(b3, 32, 1))
    c3 = jnp.where(even, pltpu.roll(b2, 96, 1), b3)
    return c0, c1, c2, c3


def stencil_kernel(tab, cot, left, right, top, bottom, field, g_out, mix_out, ext, band):
    ext[1:TD + 1, 0:R, :] = left[...].astype(F32)
    ext[1:TD + 1, R:R + FD, :] = cot[...].astype(F32)
    ext[1:TD + 1, R + FD:XW, :] = right[...].astype(F32)
    ext[0:1] = top[...].astype(F32)
    ext[TD + 1:TD + 2] = bottom[...].astype(F32)
    lane = lax.broadcasted_iota(jnp.int32, (FD, 256), 1)
    column = lane
    for edge in range(1, QUAD + 2):
        column = column - jnp.where(lane >= edge * XW, XW, 0)
    apart = (column - lax.broadcasted_iota(jnp.int32, (FD, 256), 0)).astype(F32)
    zero = jnp.zeros((FD, 256), F32)
    for quad in range(TD // QUAD):
        for r in range(QUAD):
            t = quad * QUAD + r
            sums = [zero] * K
            for s in range(S):
                hit = apart == tab[t, K * S + s:K * S + s + 1, :]
                for k in range(K):
                    sums[k] = sums[k] + jnp.where(hit, tab[t, k * S + s:k * S + s + 1, :], 0.0)
            for k in range(K):
                row = (k * QUAD + r) * FD
                band[row:row + FD, :] = sums[k]
        slab = ext[quad * QUAD:quad * QUAD + QUAD + 2].reshape((QUAD + 2) * XW, C).astype(BF16)
        weights = band[:, :(QUAD + 2) * XW].astype(BF16)
        got = jnp.dot(weights, slab, preferred_element_type=F32).astype(BF16)
        rows = QUAD * FD
        for k in range(K):
            g_out[quad * rows:(quad + 1) * rows, k * C:(k + 1) * C] = got[k * rows:(k + 1) * rows]
    mix = lax.dot_general(
        field[...], g_out[...], (((0,), (0,)), ((), ())), preferred_element_type=F32
    )
    mix_out[...] = (mix * (1.0 / math.sqrt(NLAT * NLON))).astype(BF16)


def field_kernel(g, cot, mix, gf_out, send_out, flat, turned, send):
    total = cot[...].astype(F32)
    for k in range(K):
        total = total + lax.dot_general(
            g[:, k * C:(k + 1) * C], mix[k], (((1,), (1,)), ((), ())), preferred_element_type=F32
        )
    rounded = total.astype(BF16)
    gf_out[...] = rounded
    for h in range(C // 128):
        flat[h] = rounded[:, h * 128:(h + 1) * 128].astype(F32)
    pad = jnp.zeros((TP - TD, 128), F32)
    for fq in range(FD // 4):
        for h in range(C // 128):
            pieces = []
            for fr in range(4):
                pieces.append(flat[h, pl.ds(fq * 4 + fr, TD, stride=FD), :])
                pieces.append(pad)
            turned[fq, h * 128:(h + 1) * 128, :] = jnp.concatenate(pieces, axis=0).T
    for fq in range(FD // 4):
        for q in range(CD // 4):
            parts = [
                turned[fq, pl.ds(q * 4 + cr, LONS, stride=CD), :] for cr in range(4)
            ]
            for fr, part in enumerate(swap_blocks(parts)):
                send[q, pl.ds(fq * 4 + fr, LONS, stride=FD), :] = part
    for q in range(CD // 4):
        send_out[:, q * 128:(q + 1) * 128] = send[q].astype(BF16)


def legendre_kernel(pos, cosines, logscale, out, coef, prev_s, early_s, scale_s, rows):
    block = pl.program_id(0)
    order = pos[0] * MD + lax.broadcasted_iota(jnp.int32, (MD, 128), 0)
    order_f = order.astype(F32)

    @pl.when(block == 0)
    def _():
        prev_s[...] = jnp.zeros_like(prev_s)
        early_s[...] = jnp.zeros_like(early_s)
        scale_s[...] = logscale[...]

    lane = lax.broadcasted_iota(jnp.int32, (MD, 128), 1)
    degree = block * LB + (lane & (LB - 1))
    deg_f = degree.astype(F32)
    higher = degree > order
    lower_a = jnp.where(higher, deg_f * deg_f - order_f * order_f, 1.0)
    factor_a = jnp.where(higher, jnp.sqrt((4.0 * deg_f * deg_f - 1.0) / lower_a), 0.0)
    before = deg_f - 1.0
    upper_b = jnp.maximum(before * before - order_f * order_f, 0.0)
    lower_b = jnp.maximum(4.0 * before * before - 1.0, 1.0)
    factor_b = jnp.sqrt(upper_b / lower_b)
    coef[...] = jnp.where(lane < LB, factor_a, factor_b)

    x = [jnp.broadcast_to(cosines[0:1, h * 128:(h + 1) * 128], (MD, 128)) for h in range(2)]
    prev = [prev_s[:, h * 128:(h + 1) * 128] for h in range(2)]
    early = [early_s[:, h * 128:(h + 1) * 128] for h in range(2)]
    factor = [jnp.exp(scale_s[:, h * 128:(h + 1) * 128]) for h in range(2)]
    for step in range(LB):
        a = jnp.broadcast_to(coef[:, step:step + 1], (MD, 128))
        b = jnp.broadcast_to(coef[:, LB + step:LB + step + 1], (MD, 128))
        seed = jnp.where(order == block * LB + step, 1.0, 0.0)
        for h in range(2):
            fresh = a * (x[h] * prev[h] - b * early[h]) + seed
            rows[h, step * MD:(step + 1) * MD, :] = fresh * factor[h]
            early[h], prev[h] = prev[h], fresh
    for h in range(2):
        span = slice(h * 128, (h + 1) * 128)
        biggest = jnp.maximum(jnp.abs(prev[h]), jnp.abs(early[h]))
        divisor = jnp.where(biggest > 0.0, biggest, 1.0)
        prev_s[:, span] = prev[h] / divisor
        early_s[:, span] = early[h] / divisor
        scale_s[:, span] = scale_s[:, span] + jnp.log(divisor)
    for m in range(MD):
        for h in range(2):
            span = slice(h * 128, (h + 1) * 128)
            out[m, :, span] = rows[h, pl.ds(m, LB, stride=MD), :].astype(BF16)


MSTEP = 8


def synthesis_kernel(spec, leg, out, lined):
    step = pl.program_id(0)

    @pl.when(step == 0)
    def _():
        for g in range(2):
            for q in range(CD // 4):
                parts = [spec[4 * g + iq, :, q * 128:(q + 1) * 128].astype(F32) for iq in range(4)]
                for cr, part in enumerate(swap_blocks(parts)):
                    for p in range(2):
                        base = (p * CD + q * 4 + cr) * MD
                        lined[g, base:base + MD, :] = part[p * MD:(p + 1) * MD]

    for mm in range(MSTEP):
        halves = [lined[g, pl.ds(step * MSTEP + mm, 2 * CD, stride=MD), :] for g in range(2)]
        lhs = jnp.concatenate(halves, axis=1).astype(BF16)
        got = lax.dot_general(
            lhs, leg[mm], (((1,), (1,)), ((), ())), preferred_element_type=F32
        ) * math.sqrt(4.0 * math.pi / NLAT)
        out[0, mm] = got[:CD]
        out[1, mm] = got[CD:]


TILES = (MD // 8) * (K * C // 128)


def sum_lat_kernel(parts, out):
    total = parts[0].astype(F32)
    for i in range(1, LATS):
        total = total + parts[i].astype(F32)
    lanes = K * C // 128
    for n in range(0, 2 * LONS, 2):
        tiles = []
        for tile in (n, n + 1):
            if tile < TILES:
                row, col = divmod(tile, lanes)
                tiles.append(total[row * 8:(row + 1) * 8, col * 128:(col + 1) * 128])
            else:
                tiles.append(jnp.zeros((8, 128), F32))
        out[n // 2] = jnp.concatenate(tiles, axis=0).astype(BF16)


def sum_lon_kernel(parts, out):
    total = parts[0].astype(F32)
    for j in range(1, LONS):
        total = total + parts[j].astype(F32)
    total = total.astype(BF16)
    for j in range(LONS):
        out[j] = total


def copies_kernel(part, out):
    for i in range(LATS):
        out[i] = part[...]


def mix_kernel(parts, out):
    lanes = K * C // 128
    for i in range(LATS):
        for n in range(0, TILES, 2):
            pair = parts[i, n // 2].astype(F32)
            for half in range(2):
                row, col = divmod(n + half, lanes)
                k, d = divmod(col, C // 128)
                out[k, i * MD + row * 8:i * MD + row * 8 + 8, d * 128:(d + 1) * 128] = pair[half * 8:half * 8 + 8]


def dft_rows():
    order = np.arange(M).reshape(LATS, 1, MD)
    order = np.broadcast_to(order, (LATS, 2, MD)).reshape(-1)
    part = np.broadcast_to(np.arange(2).reshape(1, 2, 1), (LATS, 2, MD)).reshape(-1)
    angle = 2.0 * np.pi / NLON * ((order[:, None] * np.arange(NLON)[None, :]) % NLON)
    angle = angle.astype(np.float32)
    return np.where(part[:, None] == 0, np.cos(angle), -np.sin(angle)).astype(ml_dtypes.bfloat16)


def latitudes():
    angle = ((np.arange(NLAT) + 0.5) * (np.pi / NLAT)).reshape(LATS, TD)
    cosine = np.zeros((LATS, TP), np.float32)
    logsine = np.zeros((LATS, TP), np.float32)
    cosine[:, :TD] = np.cos(angle)
    logsine[:, :TD] = np.log(np.sin(angle))
    return cosine.reshape(1, -1), logsine.reshape(1, -1)


def seed_logs():
    degree = np.arange(M, dtype=np.float64)
    steps = np.log((2.0 * degree + 1.0) / (2.0 * degree + 2.0))
    prefix = np.concatenate([np.zeros(1), np.cumsum(steps)[:-1]])
    return (0.5 * np.log((2.0 * degree + 1.0) / (4.0 * np.pi)) + 0.5 * prefix).astype(np.float32)


def band_lanes():
    mark = np.zeros((TD, 3, 256), np.float32)
    for t in range(TD):
        for rr in range(3):
            start = (t % QUAD + rr) * XW
            mark[t, rr, start:start + XW] = 1.0
    return mark


def tap_table(taps, offsets, counts, first_row):
    slot_ids = lax.broadcasted_iota(jnp.int32, taps.shape, 3)
    live = jnp.where(slot_ids < counts[:, None, None, None], taps, 0.0).astype(BF16).astype(F32)
    shift = (R - offsets).astype(F32)[:, None]
    both = jnp.concatenate([live, shift], axis=1)
    both = jnp.pad(both, ((1, 1), (0, 0), (0, 0), (0, 0)))
    both = lax.dynamic_slice_in_dim(both, first_row, TD + 2, 0)
    marks = band_lanes()
    table = 0.0
    for rr in range(3):
        mine = both[rr:rr + TD, :, 2 - rr, :].reshape(TD, (K + 1) * S)
        table = table + mine[:, :, None] * marks[:, rr][:, None, :]
    return table


def on_device(field, cotangent, mix_weight, taps, offsets, counts):
    lat_pos = lax.axis_index("lat")
    up = [(i, (i + 1) % LONS) for i in range(LONS)]
    down = [(j, i) for i, j in up]
    left = lax.ppermute(cotangent[:, FD - R:], "lon", up)
    right = lax.ppermute(cotangent[:, :R], "lon", down)
    edge_rows = [
        jnp.concatenate([left[t:t + 1], cotangent[t:t + 1], right[t:t + 1]], axis=1) for t in (0, TD - 1)
    ]
    north = [(i, i + 1) for i in range(LATS - 1)]
    south = [(j, i) for i, j in north]
    top = lax.ppermute(edge_rows[1], "lat", north)
    bottom = lax.ppermute(edge_rows[0], "lat", south)

    cosine, logsine = latitudes()
    first_order = lat_pos * MD
    seeds = lax.dynamic_slice_in_dim(jnp.asarray(seed_logs()), first_order, MD, 0)
    orders = (first_order + jnp.arange(MD, dtype=jnp.int32)).astype(F32)
    logscale = seeds[:, None] + orders[:, None] * logsine
    table = call(
        legendre_kernel,
        shape((MD, L, LATS * TP), BF16),
        grid_spec=pltpu.PrefetchScalarGridSpec(
            num_scalar_prefetch=1,
            grid=(L // LB,),
            in_specs=[
                pl.BlockSpec((1, LATS * TP), lambda b, pos: (0, 0)),
                pl.BlockSpec((MD, LATS * TP), lambda b, pos: (0, 0)),
            ],
            out_specs=pl.BlockSpec((MD, LB, LATS * TP), lambda b, pos: (0, b, 0)),
            scratch_shapes=[
                pltpu.VMEM((MD, 128), F32),
                pltpu.VMEM((MD, LATS * TP), F32),
                pltpu.VMEM((MD, LATS * TP), F32),
                pltpu.VMEM((MD, LATS * TP), F32),
                pltpu.VMEM((2, LB * MD, 128), F32),
            ],
        ),
        name="legendre",
    )(jnp.reshape(lat_pos, (1,)).astype(jnp.int32), jnp.asarray(cosine), logscale)

    tab = tap_table(taps, offsets, counts, lat_pos * TD)
    cells = TD * FD
    grown, mix_part = call(
        stencil_kernel,
        (shape((cells, K * C), BF16), shape((C, K * C), BF16)),
        scratch_shapes=[pltpu.VMEM((TD + 2, XW, C), F32), pltpu.VMEM((K * QUAD * FD, 256), F32)],
        name="stencil",
    )(tab, cotangent, left, right, top, bottom, field.reshape(cells, C))
    mix_lat = lax.all_to_all(mix_part.reshape(LATS, MD, K * C), "lat", 0, 0, tiled=True)

    grad_field, send = call(
        field_kernel,
        (shape((cells, C), BF16), shape((LONS * FD, CD * TP), BF16)),
        scratch_shapes=[
            pltpu.VMEM((C // 128, cells, 128), F32),
            pltpu.VMEM((FD // 4, C, 128), F32),
            pltpu.VMEM((CD // 4, LONS * FD, 128), F32),
        ],
        name="grad_field",
    )(grown, cotangent.reshape(cells, C), mix_weight)
    columns = lax.all_to_all(send.reshape(LONS, FD, CD * TP), "lon", 0, 0, tiled=True)

    mix_lon = lax.all_to_all(
        call(sum_lat_kernel, shape((LONS, 16, 128), BF16), name="mix_sum_lat")(mix_lat), "lon", 0, 0, tiled=True
    )
    spectra = jnp.dot(
        jnp.asarray(dft_rows()), columns.reshape(NLON, CD * TP), preferred_element_type=F32
    )
    spectra = (spectra * (1.0 / math.sqrt(NLON))).astype(BF16)
    spec = lax.all_to_all(spectra.reshape(LATS, 2 * MD, CD * TP), "lat", 0, 0, tiled=True)

    mix_mine = call(sum_lon_kernel, shape((LONS, 16, 128), BF16), name="mix_sum_lon")(mix_lon)
    mix_row = lax.all_to_all(mix_mine, "lon", 0, 0, tiled=True)
    mix_copies = call(copies_kernel, shape((LATS, LONS, 16, 128), BF16), name="mix_copies")(mix_row)
    mix_all = lax.all_to_all(mix_copies, "lat", 0, 0, tiled=True)
    grad_mix = call(mix_kernel, shape((K, C, C), F32), name="mix_out")(mix_all)

    grad_spectra = call(
        synthesis_kernel,
        shape((2, MD, CD, L), F32),
        grid_spec=pltpu.PrefetchScalarGridSpec(
            num_scalar_prefetch=0,
            grid=(MD // MSTEP,),
            in_specs=[
                pl.BlockSpec((LATS, 2 * MD, CD * TP), lambda b: (0, 0, 0)),
                pl.BlockSpec((MSTEP, L, LATS * TP), lambda b: (b, 0, 0)),
            ],
            out_specs=pl.BlockSpec((2, MSTEP, CD, L), lambda b: (0, b, 0, 0)),
            scratch_shapes=[pltpu.VMEM((2, 2 * CD * MD, 128), F32)],
        ),
        name="synthesis",
    )(spec, table)
    return (grad_field.reshape(TD, FD, C), grad_spectra, grad_mix)


def solution(mesh):
    placed = (P("lat", "lon", None), P("lat", "lon", None), P(), P(), P(), P())
    return jax.shard_map(
        on_device,
        mesh=mesh,
        in_specs=placed,
        out_specs=(P("lat", "lon", None), P(None, "lat", "lon", None), P()),
        check_vma=False,
    )
```

```python
import functools
import math

import jax
import jax.numpy as jnp
import ml_dtypes
import numpy as np
from jax import lax
from jax.experimental import pallas as pl
from jax.experimental.pallas import tpu as pltpu
from jax.sharding import PartitionSpec as P

C = 384
M = 384
L = 384
K = 3
R = 8
S = 8
LB = 32
NLAT = 192
NLON = 768
LATS = 8
LONS = 32
TD = NLAT // LATS
FD = NLON // LONS
CD = C // LONS
MD = M // LATS
XW = FD + 2 * R
TP = 32
QUAD = 4
F32 = jnp.float32
BF16 = jnp.bfloat16
VMEM_BYTES = 56 * 1024 * 1024


def call(kernel, out_shape, us, **kw):
    return pl.pallas_call(
        kernel,
        out_shape=out_shape,
        cost_estimate=pl.CostEstimate(flops=int(us * 1.1e9), bytes_accessed=int(us * 3.0e6), transcendentals=0),
        compiler_params=pltpu.CompilerParams(vmem_limit_bytes=VMEM_BYTES),
        **kw,
    )


def shape(dims, dtype):
    return jax.ShapeDtypeStruct(dims, dtype)


def swap_blocks(parts):
    lane = lax.broadcasted_iota(jnp.int32, parts[0].shape, 1)
    low = lane < 64
    even = (lane & 32) == 0
    a0, a1, a2, a3 = parts
    b0 = jnp.where(low, a0, pltpu.roll(a2, 64, 1))
    b2 = jnp.where(low, pltpu.roll(a0, 64, 1), a2)
    b1 = jnp.where(low, a1, pltpu.roll(a3, 64, 1))
    b3 = jnp.where(low, pltpu.roll(a1, 64, 1), a3)
    c0 = jnp.where(even, b0, pltpu.roll(b1, 32, 1))
    c1 = jnp.where(even, pltpu.roll(b0, 96, 1), b1)
    c2 = jnp.where(even, b2, pltpu.roll(b3, 32, 1))
    c3 = jnp.where(even, pltpu.roll(b2, 96, 1), b3)
    return c0, c1, c2, c3


def stencil_kernel(tab, cot, left, right, top, bottom, field, g_out, mix_out, ext, band):
    ext[1:TD + 1, 0:R, :] = left[...].astype(F32)
    ext[1:TD + 1, R:R + FD, :] = cot[...].astype(F32)
    ext[1:TD + 1, R + FD:XW, :] = right[...].astype(F32)
    ext[0:1] = top[...].astype(F32)
    ext[TD + 1:TD + 2] = bottom[...].astype(F32)
    lane = lax.broadcasted_iota(jnp.int32, (FD, 256), 1)
    column = lane
    for edge in range(1, QUAD + 2):
        column = column - jnp.where(lane >= edge * XW, XW, 0)
    apart = (column - lax.broadcasted_iota(jnp.int32, (FD, 256), 0)).astype(F32)
    zero = jnp.zeros((FD, 256), F32)
    for quad in range(TD // QUAD):
        for r in range(QUAD):
            t = quad * QUAD + r
            sums = [zero] * K
            for s in range(S):
                hit = apart == tab[t, K * S + s:K * S + s + 1, :]
                for k in range(K):
                    sums[k] = sums[k] + jnp.where(hit, tab[t, k * S + s:k * S + s + 1, :], 0.0)
            for k in range(K):
                row = (k * QUAD + r) * FD
                band[row:row + FD, :] = sums[k]
        slab = ext[quad * QUAD:quad * QUAD + QUAD + 2].reshape((QUAD + 2) * XW, C).astype(BF16)
        weights = band[:, :(QUAD + 2) * XW].astype(BF16)
        got = jnp.dot(weights, slab, preferred_element_type=F32).astype(BF16)
        rows = QUAD * FD
        for k in range(K):
            g_out[quad * rows:(quad + 1) * rows, k * C:(k + 1) * C] = got[k * rows:(k + 1) * rows]
    mix = lax.dot_general(
        field[...], g_out[...], (((0,), (0,)), ((), ())), preferred_element_type=F32
    )
    mix_out[...] = (mix * (1.0 / math.sqrt(NLAT * NLON))).astype(BF16)


def field_kernel(pos, g, cot, mix, gf_out, send_out, flat, turned, send):
    total = cot[...].astype(F32)
    for k in range(K):
        total = total + lax.dot_general(
            g[:, k * C:(k + 1) * C], mix[k], (((1,), (1,)), ((), ())), preferred_element_type=F32
        )
    rounded = total.astype(BF16)
    gf_out[...] = rounded
    rounded = rounded.astype(F32)
    southern = pos[0] >= LATS // 2
    for t in range(TD):
        row = pl.multiple_of(jnp.where(southern, TD - 1 - t, t) * FD, FD)
        for h in range(C // 128):
            flat[h, pl.ds(row, FD), :] = rounded[t * FD:(t + 1) * FD, h * 128:(h + 1) * 128]
    pad = jnp.zeros((TP - TD, 128), F32)
    for fq in range(FD // 4):
        for h in range(C // 128):
            pieces = []
            for fr in range(4):
                pieces.append(flat[h, pl.ds(fq * 4 + fr, TD, stride=FD), :])
                pieces.append(pad)
            turned[fq, h * 128:(h + 1) * 128, :] = jnp.concatenate(pieces, axis=0).T
    for fq in range(FD // 4):
        for q in range(CD // 4):
            parts = [
                turned[fq, pl.ds(q * 4 + cr, LONS, stride=CD), :] for cr in range(4)
            ]
            for fr, part in enumerate(swap_blocks(parts)):
                send[q, pl.ds(fq * 4 + fr, LONS, stride=FD), :] = part
    for q in range(CD // 4):
        send_out[:, q * 128:(q + 1) * 128] = send[q].astype(BF16)


def dft_kernel(rows, columns, out):
    got = jnp.dot(rows[...], columns[...], preferred_element_type=F32)
    out[...] = (got * (1.0 / math.sqrt(NLON))).astype(BF16)


HALF = LATS // 2 * TP


def legendre_kernel(pos, cosines, logscale, out, coef, prev_s, early_s, scale_s, rows):
    block = pl.program_id(0)
    order = pos[0] * MD + lax.broadcasted_iota(jnp.int32, (MD, 128), 0)
    order_f = order.astype(F32)

    @pl.when(block == 0)
    def _():
        prev_s[...] = jnp.zeros_like(prev_s)
        early_s[...] = jnp.zeros_like(early_s)
        scale_s[...] = logscale[...]

    lane = lax.broadcasted_iota(jnp.int32, (MD, 128), 1)
    degree = block * LB + (lane & (LB - 1))
    deg_f = degree.astype(F32)
    higher = degree > order
    lower_a = jnp.where(higher, deg_f * deg_f - order_f * order_f, 1.0)
    factor_a = jnp.where(higher, jnp.sqrt((4.0 * deg_f * deg_f - 1.0) / lower_a), 0.0)
    before = deg_f - 1.0
    upper_b = jnp.maximum(before * before - order_f * order_f, 0.0)
    lower_b = jnp.maximum(4.0 * before * before - 1.0, 1.0)
    factor_b = jnp.sqrt(upper_b / lower_b)
    coef[...] = jnp.where(lane < LB, factor_a, factor_b)

    x = jnp.broadcast_to(cosines[...], (MD, 128))
    prev = prev_s[...]
    early = early_s[...]
    factor = jnp.exp(scale_s[...])
    for step in range(LB):
        a = jnp.broadcast_to(coef[:, step:step + 1], (MD, 128))
        b = jnp.broadcast_to(coef[:, LB + step:LB + step + 1], (MD, 128))
        seed = jnp.where(order == block * LB + step, 1.0, 0.0)
        fresh = a * (x * prev - b * early) + seed
        rows[step * MD:(step + 1) * MD, :] = fresh * factor
        early, prev = prev, fresh
    biggest = jnp.maximum(jnp.abs(prev), jnp.abs(early))
    divisor = jnp.where(biggest > 0.0, biggest, 1.0)
    prev_s[...] = prev / divisor
    early_s[...] = early / divisor
    scale_s[...] = scale_s[...] + jnp.log(divisor)
    for m in range(MD):
        side = (m % 2) * 128
        out[m // 2, :, side:side + 128] = rows[pl.ds(m, LB, stride=MD), :].astype(BF16)


MSTEP = 8


def synthesis_kernel(spec, leg, out, lined, rows):
    step = pl.program_id(0)

    @pl.when(step == 0)
    def _():
        for q in range(CD // 4):
            span = slice(q * 128, (q + 1) * 128)
            north = [spec[i, :, span].astype(F32) for i in range(LATS // 2)]
            south = [spec[LATS - 1 - i, :, span].astype(F32) for i in range(LATS // 2)]
            for odd in range(2):
                parts = [n - s if odd else n + s for n, s in zip(north, south)]
                for cr, part in enumerate(swap_blocks(parts)):
                    for p in range(2):
                        base = ((odd * 2 + p) * CD + q * 4 + cr) * MD
                        lined[base:base + MD, :] = part[p * MD:(p + 1) * MD]

    wide = 2 * CD
    odd_lane = (lax.broadcasted_iota(jnp.int32, (wide, L), 1) & 1) == 1
    zero = jnp.zeros((2 * wide, HALF), F32)
    for pair in range(MSTEP // 2):
        first = step * MSTEP + 2 * pair
        mine = [lined[pl.ds(first + side, 2 * wide, stride=MD), :] for side in range(2)]
        lhs = jnp.concatenate(
            [jnp.concatenate([mine[0], zero], axis=1), jnp.concatenate([zero, mine[1]], axis=1)], axis=0
        ).astype(BF16)
        got = lax.dot_general(
            lhs, leg[pair], (((1,), (1,)), ((), ())), preferred_element_type=F32
        ) * math.sqrt(4.0 * math.pi / NLAT)
        done = [
            jnp.where(odd_lane, got[wide:2 * wide], got[:wide]),
            jnp.where(odd_lane, got[2 * wide:3 * wide], got[3 * wide:]),
        ]
        for side in range(2):
            for h in range(L // 128):
                rows[h, pl.ds(2 * pair + side, wide, stride=MSTEP), :] = done[side][:, h * 128:(h + 1) * 128]
    for p in range(2):
        for c in range(CD):
            base = (p * CD + c) * MSTEP
            for h in range(L // 128):
                out[p, c, :, h * 128:(h + 1) * 128] = rows[h, base:base + MSTEP, :]


TILES = (MD // 8) * (K * C // 128)


def sum_lat_kernel(parts, out):
    total = parts[0].astype(F32)
    for i in range(1, LATS):
        total = total + parts[i].astype(F32)
    lanes = K * C // 128
    for n in range(0, 2 * LONS, 2):
        tiles = []
        for tile in (n, n + 1):
            if tile < TILES:
                row, col = divmod(tile, lanes)
                tiles.append(total[row * 8:(row + 1) * 8, col * 128:(col + 1) * 128])
            else:
                tiles.append(jnp.zeros((8, 128), F32))
        out[n // 2] = jnp.concatenate(tiles, axis=0).astype(BF16)


def sum_lon_kernel(parts, out):
    total = parts[0].astype(F32)
    for j in range(1, LONS):
        total = total + parts[j].astype(F32)
    total = total.astype(BF16)
    for j in range(LONS):
        out[j] = total


PAIRS = TILES // 2


def copies_kernel(part, out):
    for i in range(LATS):
        out[i] = part[:PAIRS]


def mix_kernel(parts, out):
    lanes = K * C // 128
    for n in range(0, TILES, 2):
        pair = parts[0, n // 2].astype(F32)
        for half in range(2):
            row, col = divmod(n + half, lanes)
            k, d = divmod(col, C // 128)
            out[k, row * 8:row * 8 + 8, d * 128:(d + 1) * 128] = pair[half * 8:half * 8 + 8]


def dft_rows():
    order = np.arange(M).reshape(LATS, 1, MD)
    order = np.broadcast_to(order, (LATS, 2, MD)).reshape(-1)
    part = np.broadcast_to(np.arange(2).reshape(1, 2, 1), (LATS, 2, MD)).reshape(-1)
    angle = 2.0 * np.pi / NLON * ((order[:, None] * np.arange(NLON)[None, :]) % NLON)
    angle = angle.astype(np.float32)
    return np.where(part[:, None] == 0, np.cos(angle), -np.sin(angle)).astype(ml_dtypes.bfloat16)


def latitudes():
    angle = ((np.arange(NLAT) + 0.5) * (np.pi / NLAT)).reshape(LATS, TD)
    cosine = np.zeros((LATS, TP), np.float32)
    logsine = np.zeros((LATS, TP), np.float32)
    cosine[:, :TD] = np.cos(angle)
    logsine[:, :TD] = np.log(np.sin(angle))
    half = LATS // 2
    return cosine[:half].reshape(1, -1), logsine[:half].reshape(1, -1)


def seed_logs():
    degree = np.arange(M, dtype=np.float64)
    steps = np.log((2.0 * degree + 1.0) / (2.0 * degree + 2.0))
    prefix = np.concatenate([np.zeros(1), np.cumsum(steps)[:-1]])
    return (0.5 * np.log((2.0 * degree + 1.0) / (4.0 * np.pi)) + 0.5 * prefix).astype(np.float32)


def band_lanes():
    mark = np.zeros((TD, 3, 256), np.float32)
    for t in range(TD):
        for rr in range(3):
            start = (t % QUAD + rr) * XW
            mark[t, rr, start:start + XW] = 1.0
    return mark


def tap_table(taps, offsets, counts, first_row):
    slot_ids = lax.broadcasted_iota(jnp.int32, taps.shape, 3)
    live = jnp.where(slot_ids < counts[:, None, None, None], taps, 0.0).astype(BF16).astype(F32)
    shift = (R - offsets).astype(F32)[:, None]
    both = jnp.concatenate([live, shift], axis=1)
    both = jnp.pad(both, ((1, 1), (0, 0), (0, 0), (0, 0)))
    both = lax.dynamic_slice_in_dim(both, first_row, TD + 2, 0)
    marks = band_lanes()
    table = 0.0
    for rr in range(3):
        mine = both[rr:rr + TD, :, 2 - rr, :].reshape(TD, (K + 1) * S)
        table = table + mine[:, :, None] * marks[:, rr][:, None, :]
    return table


def on_device(field, cotangent, mix_weight, taps, offsets, counts):
    lat_pos = lax.axis_index("lat")
    up = [(i, (i + 1) % LONS) for i in range(LONS)]
    down = [(j, i) for i, j in up]
    left = lax.ppermute(cotangent[:, FD - R:], "lon", up)
    right = lax.ppermute(cotangent[:, :R], "lon", down)
    edge_rows = [
        jnp.concatenate([left[t:t + 1], cotangent[t:t + 1], right[t:t + 1]], axis=1) for t in (0, TD - 1)
    ]
    north = [(i, i + 1) for i in range(LATS - 1)]
    south = [(j, i) for i, j in north]
    top = lax.ppermute(edge_rows[1], "lat", north)
    bottom = lax.ppermute(edge_rows[0], "lat", south)

    tab = tap_table(taps, offsets, counts, lat_pos * TD)
    cells = TD * FD
    grown, mix_part = call(
        stencil_kernel,
        (shape((cells, K * C), BF16), shape((C, K * C), BF16)),
        5,
        scratch_shapes=[pltpu.VMEM((TD + 2, XW, C), F32), pltpu.VMEM((K * QUAD * FD, 256), F32)],
        name="stencil",
    )(tab, cotangent, left, right, top, bottom, field.reshape(cells, C))
    mix_lat = lax.all_to_all(mix_part.reshape(LATS, MD, K * C), "lat", 0, 0, tiled=True)

    pos = jnp.reshape(lat_pos, (1,)).astype(jnp.int32)
    whole = pl.BlockSpec(memory_space=pltpu.VMEM)
    grad_field, send = call(
        field_kernel,
        (shape((cells, C), BF16), shape((LONS * FD, CD * TP), BF16)),
        5,
        in_specs=[pl.BlockSpec(memory_space=pltpu.SMEM), whole, whole, whole],
        scratch_shapes=[
            pltpu.VMEM((C // 128, cells, 128), F32),
            pltpu.VMEM((FD // 4, C, 128), F32),
            pltpu.VMEM((CD // 4, LONS * FD, 128), F32),
        ],
        name="grad_field",
    )(pos, grown, cotangent.reshape(cells, C), mix_weight)
    columns = lax.all_to_all(send.reshape(LONS, FD, CD * TP), "lon", 0, 0, tiled=True)

    mix_sum = call(sum_lat_kernel, shape((LONS, 16, 128), BF16), 2, name="mix_sum_lat")(mix_lat)
    cosine, logsine = latitudes()
    first_order = lat_pos * MD
    seeds = lax.dynamic_slice_in_dim(jnp.asarray(seed_logs()), first_order, MD, 0)
    orders = (first_order + jnp.arange(MD, dtype=jnp.int32)).astype(F32)
    logscale = seeds[:, None] + orders[:, None] * logsine
    logscale, _ = lax.optimization_barrier((logscale, send))
    table = call(
        legendre_kernel,
        shape((MD // 2, L, 2 * HALF), BF16),
        9,
        grid_spec=pltpu.PrefetchScalarGridSpec(
            num_scalar_prefetch=1,
            grid=(L // LB,),
            in_specs=[
                pl.BlockSpec((1, HALF), lambda b, pos: (0, 0)),
                pl.BlockSpec((MD, HALF), lambda b, pos: (0, 0)),
            ],
            out_specs=pl.BlockSpec((MD // 2, LB, 2 * HALF), lambda b, pos: (0, b, 0)),
            scratch_shapes=[
                pltpu.VMEM((MD, 128), F32),
                pltpu.VMEM((MD, HALF), F32),
                pltpu.VMEM((MD, HALF), F32),
                pltpu.VMEM((MD, HALF), F32),
                pltpu.VMEM((LB * MD, HALF), F32),
            ],
        ),
        name="legendre",
    )(pos, jnp.asarray(cosine), logscale)
    columns, table, mix_sum = lax.optimization_barrier((columns, table, mix_sum))

    mix_lon = lax.all_to_all(mix_sum, "lon", 0, 0, tiled=True)
    spectra = call(dft_kernel, shape((NLON, CD * TP), BF16), 2, name="dft")(
        jnp.asarray(dft_rows()), columns.reshape(NLON, CD * TP)
    )
    mix_mine = call(sum_lon_kernel, shape((LONS, 16, 128), BF16), 2, name="mix_sum_lon")(mix_lon)
    mix_row = lax.all_to_all(mix_mine, "lon", 0, 0, tiled=True)
    mix_row, spectra = lax.optimization_barrier((mix_row, spectra))

    spec = lax.all_to_all(spectra.reshape(LATS, 2 * MD, CD * TP), "lat", 0, 0, tiled=True)
    mix_copies = call(copies_kernel, shape((LATS, PAIRS, 16, 128), BF16), 2, name="mix_copies")(mix_row)
    spec, mix_copies = lax.optimization_barrier((spec, mix_copies))
    mix_all = lax.all_to_all(mix_copies, "lat", 0, 0, tiled=True)

    grad_spectra = call(
        synthesis_kernel,
        shape((2, CD, MD, L), F32),
        6,
        grid_spec=pltpu.PrefetchScalarGridSpec(
            num_scalar_prefetch=0,
            grid=(MD // MSTEP,),
            in_specs=[
                pl.BlockSpec((LATS, 2 * MD, CD * TP), lambda b: (0, 0, 0)),
                pl.BlockSpec((MSTEP // 2, L, 2 * HALF), lambda b: (b, 0, 0)),
            ],
            out_specs=pl.BlockSpec((2, CD, MSTEP, L), lambda b: (0, 0, b, 0)),
            scratch_shapes=[
                pltpu.VMEM((4 * CD * MD, HALF), F32),
                pltpu.VMEM((L // 128, 2 * CD * MSTEP, 128), F32),
            ],
        ),
        name="synthesis",
    )(spec, table)
    grad_mix = call(
        mix_kernel,
        shape((K, C, C), F32),
        2,
        grid=(LATS,),
        in_specs=[pl.BlockSpec((1, PAIRS, 16, 128), lambda i: (i, 0, 0, 0))],
        out_specs=pl.BlockSpec((K, MD, C), lambda i: (0, i, 0)),
        name="mix_out",
    )(mix_all)
    return (grad_field.reshape(TD, FD, C), jnp.transpose(grad_spectra, (0, 2, 1, 3)), grad_mix)


def solution(mesh):
    placed = (P("lat", "lon", None), P("lat", "lon", None), P(), P(), P(), P())
    return jax.shard_map(
        on_device,
        mesh=mesh,
        in_specs=placed,
        out_specs=(P("lat", "lon", None), P(None, "lat", "lon", None), P()),
        check_vma=False,
    )
```

```python
import functools
import math

import jax
import jax.numpy as jnp
import ml_dtypes
import numpy as np
from jax import lax
from jax.experimental import pallas as pl
from jax.experimental.pallas import tpu as pltpu
from jax.sharding import PartitionSpec as P

C = 384
M = 384
L = 384
K = 3
R = 8
S = 8
LB = 32
NLAT = 192
NLON = 768
LATS = 8
LONS = 32
TD = NLAT // LATS
FD = NLON // LONS
CD = C // LONS
MD = M // LATS
XW = FD + 2 * R
TP = 32
FP = FD + 8
QUAD = 4
F32 = jnp.float32
BF16 = jnp.bfloat16
VMEM_BYTES = 56 * 1024 * 1024


def call(kernel, out_shape, us, **kw):
    return pl.pallas_call(
        kernel,
        out_shape=out_shape,
        cost_estimate=pl.CostEstimate(flops=int(us * 1.1e9), bytes_accessed=int(us * 3.0e6), transcendentals=0),
        compiler_params=pltpu.CompilerParams(vmem_limit_bytes=VMEM_BYTES),
        **kw,
    )


def near(array):
    return pltpu.with_memory_space_constraint(array, pltpu.VMEM)


def shape(dims, dtype):
    return jax.ShapeDtypeStruct(dims, dtype)


def swap_blocks(parts):
    lane = lax.broadcasted_iota(jnp.int32, parts[0].shape, 1)
    low = lane < 64
    even = (lane & 32) == 0
    a0, a1, a2, a3 = parts
    b0 = jnp.where(low, a0, pltpu.roll(a2, 64, 1))
    b2 = jnp.where(low, pltpu.roll(a0, 64, 1), a2)
    b1 = jnp.where(low, a1, pltpu.roll(a3, 64, 1))
    b3 = jnp.where(low, pltpu.roll(a1, 64, 1), a3)
    c0 = jnp.where(even, b0, pltpu.roll(b1, 32, 1))
    c1 = jnp.where(even, pltpu.roll(b0, 96, 1), b1)
    c2 = jnp.where(even, b2, pltpu.roll(b3, 32, 1))
    c3 = jnp.where(even, pltpu.roll(b2, 96, 1), b3)
    return c0, c1, c2, c3


def stencil_kernel(tab, cot, left, right, top, bottom, field, g_out, mix_out, ext, band):
    ext[1:TD + 1, 0:R, :] = left[...].astype(F32)
    ext[1:TD + 1, R:R + FD, :] = cot[...].astype(F32)
    ext[1:TD + 1, R + FD:XW, :] = right[...].astype(F32)
    ext[0:1] = top[...].astype(F32)
    ext[TD + 1:TD + 2] = bottom[...].astype(F32)
    lane = lax.broadcasted_iota(jnp.int32, (FD, 256), 1)
    column = lane
    for edge in range(1, QUAD + 2):
        column = column - jnp.where(lane >= edge * XW, XW, 0)
    apart = (column - lax.broadcasted_iota(jnp.int32, (FD, 256), 0)).astype(F32)
    zero = jnp.zeros((FD, 256), F32)
    for quad in range(TD // QUAD):
        for r in range(QUAD):
            t = quad * QUAD + r
            sums = [zero] * K
            for s in range(S):
                hit = apart == tab[t, K * S + s:K * S + s + 1, :]
                for k in range(K):
                    sums[k] = sums[k] + jnp.where(hit, tab[t, k * S + s:k * S + s + 1, :], 0.0)
            for k in range(K):
                row = (k * QUAD + r) * FD
                band[row:row + FD, :] = sums[k]
        slab = ext[quad * QUAD:quad * QUAD + QUAD + 2].reshape((QUAD + 2) * XW, C).astype(BF16)
        weights = band[:, :(QUAD + 2) * XW].astype(BF16)
        got = jnp.dot(weights, slab, preferred_element_type=F32).astype(BF16)
        rows = QUAD * FD
        for k in range(K):
            g_out[quad * rows:(quad + 1) * rows, k * C:(k + 1) * C] = got[k * rows:(k + 1) * rows]
    mix = lax.dot_general(
        field[...], g_out[...], (((0,), (0,)), ((), ())), preferred_element_type=F32
    )
    mix_out[...] = (mix * (1.0 / math.sqrt(NLAT * NLON))).astype(BF16)


def field_kernel(pos, g, cot, mix, gf_out, send_out, flat, turned, send):
    total = cot[...].astype(F32)
    for k in range(K):
        total = total + lax.dot_general(
            g[:, k * C:(k + 1) * C], mix[k], (((1,), (1,)), ((), ())), preferred_element_type=F32
        )
    rounded = total.astype(BF16)
    gf_out[...] = rounded
    rounded = rounded.astype(F32)
    southern = pos[0] >= LATS // 2
    for t in range(TD):
        row = pl.multiple_of(jnp.where(southern, TD - 1 - t, t) * FD, FD)
        for h in range(C // 128):
            flat[h, pl.ds(row, FD), :] = rounded[t * FD:(t + 1) * FD, h * 128:(h + 1) * 128]
    pad = jnp.zeros((TP - TD, 128), F32)
    for fq in range(FD // 4):
        for h in range(C // 128):
            pieces = []
            for fr in range(4):
                pieces.append(flat[h, pl.ds(fq * 4 + fr, TD, stride=FD), :])
                pieces.append(pad)
            turned[fq, h * 128:(h + 1) * 128, :] = jnp.concatenate(pieces, axis=0).T
    for fq in range(FD // 4):
        for q in range(CD // 4):
            parts = [
                turned[fq, pl.ds(q * 4 + cr, LONS, stride=CD), :] for cr in range(4)
            ]
            for fr, part in enumerate(swap_blocks(parts)):
                send[q, pl.ds(fq * 4 + fr, LONS, stride=FD), :] = part
    send_out[:, FD:, :] = jnp.zeros((LONS, FP - FD, CD * TP), BF16)
    for q in range(CD // 4):
        send_out[:, :FD, q * 128:(q + 1) * 128] = send[q].reshape(LONS, FD, 128).astype(BF16)


def dft_kernel(rows, columns, out):
    got = jnp.dot(rows[...], columns[...], preferred_element_type=F32)
    got = (got * (1.0 / math.sqrt(NLON))).astype(BF16)
    total = jnp.zeros((FP - FD, 2 * 128), F32)
    for j in range(LONS):
        total = total + columns[j * FP + 16:(j + 1) * FP, :256].astype(F32)[8:]
    total = jnp.concatenate([total, jnp.zeros((FP - FD, CD * TP - 256), F32)], axis=1).astype(BF16)
    for i in range(LATS):
        out[i, :2 * MD, :] = got[i * 2 * MD:(i + 1) * 2 * MD]
        out[i, 2 * MD:, :] = total


HALF = LATS // 2 * TP


def legendre_kernel(pos, cosines, logscale, out, coef, prev_s, early_s, scale_s, rows):
    block = pl.program_id(0)
    order = pos[0] * MD + lax.broadcasted_iota(jnp.int32, (MD, 128), 0)
    order_f = order.astype(F32)

    @pl.when(block == 0)
    def _():
        prev_s[...] = jnp.zeros_like(prev_s)
        early_s[...] = jnp.zeros_like(early_s)
        scale_s[...] = logscale[...]

    lane = lax.broadcasted_iota(jnp.int32, (MD, 128), 1)
    degree = block * LB + (lane & (LB - 1))
    deg_f = degree.astype(F32)
    higher = degree > order
    lower_a = jnp.where(higher, deg_f * deg_f - order_f * order_f, 1.0)
    factor_a = jnp.where(higher, jnp.sqrt((4.0 * deg_f * deg_f - 1.0) / lower_a), 0.0)
    before = deg_f - 1.0
    upper_b = jnp.maximum(before * before - order_f * order_f, 0.0)
    lower_b = jnp.maximum(4.0 * before * before - 1.0, 1.0)
    factor_b = jnp.sqrt(upper_b / lower_b)
    coef[...] = jnp.where(lane < LB, factor_a, factor_b)

    x = jnp.broadcast_to(cosines[...], (MD, 128))
    prev = prev_s[...]
    early = early_s[...]
    factor = jnp.exp(scale_s[...])
    for step in range(LB):
        a = jnp.broadcast_to(coef[:, step:step + 1], (MD, 128))
        b = jnp.broadcast_to(coef[:, LB + step:LB + step + 1], (MD, 128))
        seed = jnp.where(order == block * LB + step, 1.0, 0.0)
        fresh = a * (x * prev - b * early) + seed
        rows[step * MD:(step + 1) * MD, :] = fresh * factor
        early, prev = prev, fresh
    biggest = jnp.maximum(jnp.abs(prev), jnp.abs(early))
    divisor = jnp.where(biggest > 0.0, biggest, 1.0)
    prev_s[...] = prev / divisor
    early_s[...] = early / divisor
    scale_s[...] = scale_s[...] + jnp.log(divisor)
    for m in range(MD):
        side = (m % 2) * 128
        out[m // 2, :, side:side + 128] = rows[pl.ds(m, LB, stride=MD), :].astype(BF16)


MSTEP = 8


def synthesis_kernel(spec, leg, out, lined, rows):
    step = pl.program_id(0)

    @pl.when(step == 0)
    def _():
        for q in range(CD // 4):
            span = slice(q * 128, (q + 1) * 128)
            north = [spec[i, :2 * MD, span].astype(F32) for i in range(LATS // 2)]
            south = [spec[LATS - 1 - i, :2 * MD, span].astype(F32) for i in range(LATS // 2)]
            for odd in range(2):
                parts = [n - s if odd else n + s for n, s in zip(north, south)]
                for cr, part in enumerate(swap_blocks(parts)):
                    for p in range(2):
                        base = ((odd * 2 + p) * CD + q * 4 + cr) * MD
                        lined[base:base + MD, :] = part[p * MD:(p + 1) * MD]

    wide = 2 * CD
    odd_lane = (lax.broadcasted_iota(jnp.int32, (wide, L), 1) & 1) == 1
    zero = jnp.zeros((2 * wide, HALF), F32)
    for pair in range(MSTEP // 2):
        first = step * MSTEP + 2 * pair
        mine = [lined[pl.ds(first + side, 2 * wide, stride=MD), :] for side in range(2)]
        lhs = jnp.concatenate(
            [jnp.concatenate([mine[0], zero], axis=1), jnp.concatenate([zero, mine[1]], axis=1)], axis=0
        ).astype(BF16)
        got = lax.dot_general(
            lhs, leg[pair], (((1,), (1,)), ((), ())), preferred_element_type=F32
        ) * math.sqrt(4.0 * math.pi / NLAT)
        done = [
            jnp.where(odd_lane, got[wide:2 * wide], got[:wide]),
            jnp.where(odd_lane, got[2 * wide:3 * wide], got[3 * wide:]),
        ]
        for side in range(2):
            for h in range(L // 128):
                rows[h, pl.ds(2 * pair + side, wide, stride=MSTEP), :] = done[side][:, h * 128:(h + 1) * 128]
    for p in range(2):
        for c in range(CD):
            base = (p * CD + c) * MSTEP
            for h in range(L // 128):
                out[p, c, :, h * 128:(h + 1) * 128] = rows[h, base:base + MSTEP, :]


TILES = (MD // 8) * (K * C // 128)
PAIRS = TILES // 2


def sum_lat_kernel(parts, send, out, rows, sem):
    total = parts[0].astype(F32)
    for i in range(1, LATS):
        total = total + parts[i].astype(F32)
    total = total.astype(BF16)
    lanes = K * C // 128
    rows[...] = jnp.zeros_like(rows)
    for tile in range(TILES):
        row, col = divmod(tile, lanes)
        side = (tile % 2) * 128
        rows[tile // 2, :, side:side + 128] = total[row * 8:(row + 1) * 8, col * 128:(col + 1) * 128]
    copy = pltpu.make_async_copy(rows, out.at[:, FD:, :], sem)
    copy.start()
    copy.wait()


def copies_kernel(spec, out):
    part = spec[:, 2 * MD:, :256]
    for j in range(LONS):
        out[j] = part


def mix_kernel(parts, out, rows, sems):
    lanes = K * C // 128
    copies = []
    for i in range(LATS):
        for tile in range(TILES):
            row, col = divmod(tile, lanes)
            k, d = divmod(col, C // 128)
            side = (tile % 2) * 128
            rows[k, i * MD + row * 8:i * MD + row * 8 + 8, d * 128:(d + 1) * 128] = parts[
                tile // 2, i, :, side:side + 128
            ].astype(F32)
        span = pl.ds(i * MD, MD)
        copies.append(pltpu.make_async_copy(rows.at[:, span], out.at[:, span], sems.at[i]))
        copies[-1].start()
    for copy in copies:
        copy.wait()


def dft_rows():
    order = np.arange(M).reshape(LATS, 1, MD)
    order = np.broadcast_to(order, (LATS, 2, MD)).reshape(-1)
    part = np.broadcast_to(np.arange(2).reshape(1, 2, 1), (LATS, 2, MD)).reshape(-1)
    angle = 2.0 * np.pi / NLON * ((order[:, None] * np.arange(NLON)[None, :]) % NLON)
    angle = angle.astype(np.float32)
    rows = np.where(part[:, None] == 0, np.cos(angle), -np.sin(angle))
    padded = np.zeros((2 * M, LONS, FP), np.float32)
    padded[:, :, :FD] = rows.reshape(2 * M, LONS, FD)
    return padded.reshape(2 * M, LONS * FP).astype(ml_dtypes.bfloat16)


def latitudes():
    angle = ((np.arange(NLAT) + 0.5) * (np.pi / NLAT)).reshape(LATS, TD)
    cosine = np.zeros((LATS, TP), np.float32)
    logsine = np.zeros((LATS, TP), np.float32)
    cosine[:, :TD] = np.cos(angle)
    logsine[:, :TD] = np.log(np.sin(angle))
    half = LATS // 2
    return cosine[:half].reshape(1, -1), logsine[:half].reshape(1, -1)


def seed_logs():
    degree = np.arange(M, dtype=np.float64)
    steps = np.log((2.0 * degree + 1.0) / (2.0 * degree + 2.0))
    prefix = np.concatenate([np.zeros(1), np.cumsum(steps)[:-1]])
    return (0.5 * np.log((2.0 * degree + 1.0) / (4.0 * np.pi)) + 0.5 * prefix).astype(np.float32)


def band_lanes():
    mark = np.zeros((TD, 3, 256), np.float32)
    for t in range(TD):
        for rr in range(3):
            start = (t % QUAD + rr) * XW
            mark[t, rr, start:start + XW] = 1.0
    return mark


def tap_table(taps, offsets, counts, first_row):
    slot_ids = lax.broadcasted_iota(jnp.int32, taps.shape, 3)
    live = jnp.where(slot_ids < counts[:, None, None, None], taps, 0.0).astype(BF16).astype(F32)
    shift = (R - offsets).astype(F32)[:, None]
    both = jnp.concatenate([live, shift], axis=1)
    both = jnp.pad(both, ((1, 1), (0, 0), (0, 0), (0, 0)))
    both = lax.dynamic_slice_in_dim(both, first_row, TD + 2, 0)
    marks = band_lanes()
    table = 0.0
    for rr in range(3):
        mine = both[rr:rr + TD, :, 2 - rr, :].reshape(TD, (K + 1) * S)
        table = table + mine[:, :, None] * marks[:, rr][:, None, :]
    return table


def on_device(field, cotangent, mix_weight, taps, offsets, counts):
    lat_pos = lax.axis_index("lat")
    up = [(i, (i + 1) % LONS) for i in range(LONS)]
    down = [(j, i) for i, j in up]
    left = lax.ppermute(cotangent[:, FD - R:], "lon", up)
    right = lax.ppermute(cotangent[:, :R], "lon", down)
    edge_rows = [
        jnp.concatenate([left[t:t + 1], cotangent[t:t + 1], right[t:t + 1]], axis=1) for t in (0, TD - 1)
    ]
    north = [(i, i + 1) for i in range(LATS - 1)]
    south = [(j, i) for i, j in north]
    top = lax.ppermute(edge_rows[1], "lat", north)
    bottom = lax.ppermute(edge_rows[0], "lat", south)

    whole = pl.BlockSpec(memory_space=pltpu.VMEM)
    tab = tap_table(taps, offsets, counts, lat_pos * TD)
    cells = TD * FD
    grown, mix_part = call(
        stencil_kernel,
        (shape((cells, K * C), BF16), shape((C, K * C), BF16)),
        5,
        in_specs=[whole] * 7,
        scratch_shapes=[pltpu.VMEM((TD + 2, XW, C), F32), pltpu.VMEM((K * QUAD * FD, 256), F32)],
        name="stencil",
    )(near(tab), cotangent, near(left), near(right), near(top), near(bottom), field.reshape(cells, C))
    mix_lat = lax.all_to_all(mix_part.reshape(LATS, MD, K * C), "lat", 0, 0, tiled=True)

    pos = jnp.reshape(lat_pos, (1,)).astype(jnp.int32)
    grad_field, send = call(
        field_kernel,
        (shape((cells, C), BF16), shape((LONS, FP, CD * TP), BF16)),
        5,
        in_specs=[pl.BlockSpec(memory_space=pltpu.SMEM), whole, whole, whole],
        scratch_shapes=[
            pltpu.VMEM((C // 128, cells, 128), F32),
            pltpu.VMEM((FD // 4, C, 128), F32),
            pltpu.VMEM((CD // 4, LONS * FD, 128), F32),
        ],
        name="grad_field",
    )(pos, grown, cotangent.reshape(cells, C), mix_weight)
    anywhere = pl.BlockSpec(memory_space=pl.ANY)
    send = call(
        sum_lat_kernel,
        shape((LONS, FP, CD * TP), BF16),
        2,
        in_specs=[whole, anywhere],
        out_specs=anywhere,
        scratch_shapes=[pltpu.VMEM((LONS, FP - FD, CD * TP), BF16), pltpu.SemaphoreType.DMA],
        input_output_aliases={1: 0},
        name="mix_sum_lat",
    )(near(mix_lat), send)
    columns = lax.all_to_all(send, "lon", 0, 0, tiled=True)

    cosine, logsine = latitudes()
    first_order = lat_pos * MD
    seeds = lax.dynamic_slice_in_dim(jnp.asarray(seed_logs()), first_order, MD, 0)
    orders = (first_order + jnp.arange(MD, dtype=jnp.int32)).astype(F32)
    logscale = seeds[:, None] + orders[:, None] * logsine
    logscale, _ = lax.optimization_barrier((logscale, send))
    table = call(
        legendre_kernel,
        shape((MD // 2, L, 2 * HALF), BF16),
        9,
        grid_spec=pltpu.PrefetchScalarGridSpec(
            num_scalar_prefetch=1,
            grid=(L // LB,),
            in_specs=[
                pl.BlockSpec((1, HALF), lambda b, pos: (0, 0)),
                pl.BlockSpec((MD, HALF), lambda b, pos: (0, 0)),
            ],
            out_specs=pl.BlockSpec((MD // 2, LB, 2 * HALF), lambda b, pos: (0, b, 0)),
            scratch_shapes=[
                pltpu.VMEM((MD, 128), F32),
                pltpu.VMEM((MD, HALF), F32),
                pltpu.VMEM((MD, HALF), F32),
                pltpu.VMEM((MD, HALF), F32),
                pltpu.VMEM((LB * MD, HALF), F32),
            ],
        ),
        name="legendre",
    )(pos, jnp.asarray(cosine), logscale)
    columns, table = lax.optimization_barrier((columns, table))

    spectra = call(dft_kernel, shape((LATS, 2 * MD + FP - FD, CD * TP), BF16), 2, in_specs=[whole, whole], name="dft")(
        near(jnp.asarray(dft_rows())), near(columns.reshape(LONS * FP, CD * TP))
    )
    spec = lax.all_to_all(spectra, "lat", 0, 0, tiled=True)
    mix_copies = call(copies_kernel, shape((LONS, LATS, 8, 256), BF16), 2, name="mix_copies")(spec)
    mix_all = lax.all_to_all(mix_copies, "lon", 0, 0, tiled=True)

    grad_spectra = call(
        synthesis_kernel,
        shape((2, CD, MD, L), F32),
        6,
        grid_spec=pltpu.PrefetchScalarGridSpec(
            num_scalar_prefetch=0,
            grid=(MD // MSTEP,),
            in_specs=[
                pl.BlockSpec((LATS, 2 * MD + FP - FD, CD * TP), lambda b: (0, 0, 0)),
                pl.BlockSpec((MSTEP // 2, L, 2 * HALF), lambda b: (b, 0, 0)),
            ],
            out_specs=pl.BlockSpec((2, CD, MSTEP, L), lambda b: (0, 0, b, 0)),
            scratch_shapes=[
                pltpu.VMEM((4 * CD * MD, HALF), F32),
                pltpu.VMEM((L // 128, 2 * CD * MSTEP, 128), F32),
            ],
        ),
        name="synthesis",
    )(spec, table)
    grad_mix = call(
        mix_kernel,
        shape((K, C, C), F32),
        2,
        in_specs=[whole],
        out_specs=anywhere,
        scratch_shapes=[pltpu.VMEM((K, C, C), F32), pltpu.SemaphoreType.DMA((LATS,))],
        name="mix_out",
    )(near(mix_all))
    return (grad_field.reshape(TD, FD, C), jnp.transpose(grad_spectra, (0, 2, 1, 3)), grad_mix)


def solution(mesh):
    placed = (P("lat", "lon", None), P("lat", "lon", None), P(), P(), P(), P())
    return jax.shard_map(
        on_device,
        mesh=mesh,
        in_specs=placed,
        out_specs=(P("lat", "lon", None), P(None, "lat", "lon", None), P()),
        check_vma=False,
    )
```

```python
import functools
import math

import jax
import jax.numpy as jnp
import ml_dtypes
import numpy as np
from jax import lax
from jax.experimental import pallas as pl
from jax.experimental.pallas import tpu as pltpu
from jax.sharding import Mesh, PartitionSpec as P

C = 384
M = 384
L = 384
K = 3
R = 8
S = 8
LB = 32
NLAT = 192
NLON = 768
LATS = 8
LONS = 32
TD = NLAT // LATS
FD = NLON // LONS
CD = C // LONS
MD = M // LATS
XW = FD + 2 * R
TP = 32
FP = FD + 8
QUAD = 4
CHIPS = LONS // 2
LAT = "lat"
CHIP = "chip"
CORE = "core"
LON = (CHIP, CORE)
F32 = jnp.float32
BF16 = jnp.bfloat16
VMEM_BYTES = 56 * 1024 * 1024


def call(kernel, out_shape, us, **kw):
    return pl.pallas_call(
        kernel,
        out_shape=out_shape,
        cost_estimate=pl.CostEstimate(flops=int(us * 1.1e9), bytes_accessed=int(us * 3.0e6), transcendentals=0),
        compiler_params=pltpu.CompilerParams(vmem_limit_bytes=VMEM_BYTES),
        **kw,
    )


def near(array):
    return pltpu.with_memory_space_constraint(array, pltpu.VMEM)


def shape(dims, dtype):
    return jax.ShapeDtypeStruct(dims, dtype)


def swap_blocks(parts):
    lane = lax.broadcasted_iota(jnp.int32, parts[0].shape, 1)
    low = lane < 64
    even = (lane & 32) == 0
    a0, a1, a2, a3 = parts
    b0 = jnp.where(low, a0, pltpu.roll(a2, 64, 1))
    b2 = jnp.where(low, pltpu.roll(a0, 64, 1), a2)
    b1 = jnp.where(low, a1, pltpu.roll(a3, 64, 1))
    b3 = jnp.where(low, pltpu.roll(a1, 64, 1), a3)
    c0 = jnp.where(even, b0, pltpu.roll(b1, 32, 1))
    c1 = jnp.where(even, pltpu.roll(b0, 96, 1), b1)
    c2 = jnp.where(even, b2, pltpu.roll(b3, 32, 1))
    c3 = jnp.where(even, pltpu.roll(b2, 96, 1), b3)
    return c0, c1, c2, c3


def stencil_kernel(tab, cot, left, right, top, bottom, field, g_out, mix_out, ext, band):
    ext[1:TD + 1, 0:R, :] = left[...].astype(F32)
    ext[1:TD + 1, R:R + FD, :] = cot[...].astype(F32)
    ext[1:TD + 1, R + FD:XW, :] = right[...].astype(F32)
    ext[0:1] = top[...].astype(F32)
    ext[TD + 1:TD + 2] = bottom[...].astype(F32)
    lane = lax.broadcasted_iota(jnp.int32, (FD, 256), 1)
    column = lane
    for edge in range(1, QUAD + 2):
        column = column - jnp.where(lane >= edge * XW, XW, 0)
    apart = (column - lax.broadcasted_iota(jnp.int32, (FD, 256), 0)).astype(F32)
    zero = jnp.zeros((FD, 256), F32)
    for quad in range(TD // QUAD):
        for r in range(QUAD):
            t = quad * QUAD + r
            sums = [zero] * K
            for s in range(S):
                hit = apart == tab[t, K * S + s:K * S + s + 1, :]
                for k in range(K):
                    sums[k] = sums[k] + jnp.where(hit, tab[t, k * S + s:k * S + s + 1, :], 0.0)
            for k in range(K):
                row = (k * QUAD + r) * FD
                band[row:row + FD, :] = sums[k]
        slab = ext[quad * QUAD:quad * QUAD + QUAD + 2].reshape((QUAD + 2) * XW, C).astype(BF16)
        weights = band[:, :(QUAD + 2) * XW].astype(BF16)
        got = jnp.dot(weights, slab, preferred_element_type=F32).astype(BF16)
        rows = QUAD * FD
        for k in range(K):
            g_out[quad * rows:(quad + 1) * rows, k * C:(k + 1) * C] = got[k * rows:(k + 1) * rows]
    mix = lax.dot_general(
        field[...], g_out[...], (((0,), (0,)), ((), ())), preferred_element_type=F32
    )
    mix_out[...] = (mix * (1.0 / math.sqrt(NLAT * NLON))).astype(BF16)


def field_kernel(pos, g, cot, mix, gf_out, send_out, flat, turned, send):
    total = cot[...].astype(F32)
    for k in range(K):
        total = total + lax.dot_general(
            g[:, k * C:(k + 1) * C], mix[k], (((1,), (1,)), ((), ())), preferred_element_type=F32
        )
    rounded = total.astype(BF16)
    gf_out[...] = rounded
    rounded = rounded.astype(F32)
    southern = pos[0] >= LATS // 2
    for t in range(TD):
        row = pl.multiple_of(jnp.where(southern, TD - 1 - t, t) * FD, FD)
        for h in range(C // 128):
            flat[h, pl.ds(row, FD), :] = rounded[t * FD:(t + 1) * FD, h * 128:(h + 1) * 128]
    pad = jnp.zeros((TP - TD, 128), F32)
    for fq in range(FD // 4):
        for h in range(C // 128):
            pieces = []
            for fr in range(4):
                pieces.append(flat[h, pl.ds(fq * 4 + fr, TD, stride=FD), :])
                pieces.append(pad)
            turned[fq, h * 128:(h + 1) * 128, :] = jnp.concatenate(pieces, axis=0).T
    for fq in range(FD // 4):
        for q in range(CD // 4):
            parts = [
                turned[fq, pl.ds(q * 4 + cr, LONS, stride=CD), :] for cr in range(4)
            ]
            for fr, part in enumerate(swap_blocks(parts)):
                send[q, pl.ds(fq * 4 + fr, LONS, stride=FD), :] = part
    send_out[:, FD:, :] = jnp.zeros((LONS, FP - FD, CD * TP), BF16)
    for q in range(CD // 4):
        send_out[:, :FD, q * 128:(q + 1) * 128] = send[q].reshape(LONS, FD, 128).astype(BF16)


def dft_kernel(rows, columns, out):
    got = jnp.dot(rows[...], columns[...], preferred_element_type=F32)
    got = (got * (1.0 / math.sqrt(NLON))).astype(BF16)
    total = jnp.zeros((FP - FD, 2 * 128), F32)
    for j in range(LONS):
        total = total + columns[j * FP + 16:(j + 1) * FP, :256].astype(F32)[8:]
    total = jnp.concatenate([total, jnp.zeros((FP - FD, CD * TP - 256), F32)], axis=1).astype(BF16)
    for i in range(LATS):
        out[i, :2 * MD, :] = got[i * 2 * MD:(i + 1) * 2 * MD]
        out[i, 2 * MD:, :] = total


HALF = LATS // 2 * TP


def legendre_kernel(pos, cosines, logscale, out, coef, prev_s, early_s, scale_s, rows):
    block = pl.program_id(0)
    order = pos[0] * MD + lax.broadcasted_iota(jnp.int32, (MD, 128), 0)
    order_f = order.astype(F32)

    @pl.when(block == 0)
    def _():
        prev_s[...] = jnp.zeros_like(prev_s)
        early_s[...] = jnp.zeros_like(early_s)
        scale_s[...] = logscale[...]

    lane = lax.broadcasted_iota(jnp.int32, (MD, 128), 1)
    degree = block * LB + (lane & (LB - 1))
    deg_f = degree.astype(F32)
    higher = degree > order
    lower_a = jnp.where(higher, deg_f * deg_f - order_f * order_f, 1.0)
    factor_a = jnp.where(higher, jnp.sqrt((4.0 * deg_f * deg_f - 1.0) / lower_a), 0.0)
    before = deg_f - 1.0
    upper_b = jnp.maximum(before * before - order_f * order_f, 0.0)
    lower_b = jnp.maximum(4.0 * before * before - 1.0, 1.0)
    factor_b = jnp.sqrt(upper_b / lower_b)
    coef[...] = jnp.where(lane < LB, factor_a, factor_b)

    x = jnp.broadcast_to(cosines[...], (MD, 128))
    prev = prev_s[...]
    early = early_s[...]
    factor = jnp.exp(scale_s[...])
    for step in range(LB):
        a = jnp.broadcast_to(coef[:, step:step + 1], (MD, 128))
        b = jnp.broadcast_to(coef[:, LB + step:LB + step + 1], (MD, 128))
        seed = jnp.where(order == block * LB + step, 1.0, 0.0)
        fresh = a * (x * prev - b * early) + seed
        rows[step * MD:(step + 1) * MD, :] = fresh * factor
        early, prev = prev, fresh
    biggest = jnp.maximum(jnp.abs(prev), jnp.abs(early))
    divisor = jnp.where(biggest > 0.0, biggest, 1.0)
    prev_s[...] = prev / divisor
    early_s[...] = early / divisor
    scale_s[...] = scale_s[...] + jnp.log(divisor)
    for m in range(MD):
        side = (m % 2) * 128
        out[m // 2, :, side:side + 128] = rows[pl.ds(m, LB, stride=MD), :].astype(BF16)


MSTEP = 8


def synthesis_kernel(spec, leg, out, lined, rows):
    step = pl.program_id(0)

    @pl.when(step == 0)
    def _():
        for q in range(CD // 4):
            span = slice(q * 128, (q + 1) * 128)
            north = [spec[i, :2 * MD, span].astype(F32) for i in range(LATS // 2)]
            south = [spec[LATS - 1 - i, :2 * MD, span].astype(F32) for i in range(LATS // 2)]
            for odd in range(2):
                parts = [n - s if odd else n + s for n, s in zip(north, south)]
                for cr, part in enumerate(swap_blocks(parts)):
                    for p in range(2):
                        base = ((odd * 2 + p) * CD + q * 4 + cr) * MD
                        lined[base:base + MD, :] = part[p * MD:(p + 1) * MD]

    wide = 2 * CD
    odd_lane = (lax.broadcasted_iota(jnp.int32, (wide, L), 1) & 1) == 1
    zero = jnp.zeros((2 * wide, HALF), F32)
    for pair in range(MSTEP // 2):
        first = step * MSTEP + 2 * pair
        mine = [lined[pl.ds(first + side, 2 * wide, stride=MD), :] for side in range(2)]
        lhs = jnp.concatenate(
            [jnp.concatenate([mine[0], zero], axis=1), jnp.concatenate([zero, mine[1]], axis=1)], axis=0
        ).astype(BF16)
        got = lax.dot_general(
            lhs, leg[pair], (((1,), (1,)), ((), ())), preferred_element_type=F32
        ) * math.sqrt(4.0 * math.pi / NLAT)
        done = [
            jnp.where(odd_lane, got[wide:2 * wide], got[:wide]),
            jnp.where(odd_lane, got[2 * wide:3 * wide], got[3 * wide:]),
        ]
        for side in range(2):
            for h in range(L // 128):
                rows[h, pl.ds(2 * pair + side, wide, stride=MSTEP), :] = done[side][:, h * 128:(h + 1) * 128]
    for p in range(2):
        for c in range(CD):
            base = (p * CD + c) * MSTEP
            for h in range(L // 128):
                out[p, c, :, h * 128:(h + 1) * 128] = rows[h, base:base + MSTEP, :]


HALF_TILES = MD // 16 * (K * C // 128)


def tiles_of(chip):
    return [(side, *divmod(2 * chip + side, K * C // 128)) for side in range(2) if 2 * chip + side < HALF_TILES]


def sum_lat_kernel(parts, send, out, rows, sem):
    total = parts[0].astype(F32)
    for i in range(1, LATS):
        total = total + parts[i].astype(F32)
    total = total.astype(BF16)
    rows[...] = jnp.zeros_like(rows)
    for chip in range(CHIPS):
        for side, row, col in tiles_of(chip):
            for core in range(2):
                first = core * (MD // 2) + row * 8
                rows[2 * chip + core, :, side * 128:(side + 1) * 128] = total[first:first + 8, col * 128:(col + 1) * 128]
    copy = pltpu.make_async_copy(rows, out.at[:, FD:, :], sem)
    copy.start()
    copy.wait()


def copies_kernel(spec, out):
    part = spec[:, 2 * MD:, :256]
    for chip in range(CHIPS):
        out[chip] = part


def mix_kernel(core, mine, other, out, rows, sems):
    copies = []
    for i in range(LATS):
        for parts, half in ((mine, core[0]), (other, 1 - core[0])):
            base = pl.multiple_of(i * MD + half * (MD // 2), 8)
            for chip in range(CHIPS):
                for side, row, col in tiles_of(chip):
                    k, d = divmod(col, C // 128)
                    rows[k, pl.ds(base + row * 8, 8), d * 128:(d + 1) * 128] = parts[
                        chip, i, :, side * 128:(side + 1) * 128
                    ].astype(F32)
        span = pl.ds(i * MD, MD)
        copies.append(pltpu.make_async_copy(rows.at[:, span], out.at[:, span], sems.at[i]))
        copies[-1].start()
    for copy in copies:
        copy.wait()


def dft_rows():
    order = np.arange(M).reshape(LATS, 1, MD)
    order = np.broadcast_to(order, (LATS, 2, MD)).reshape(-1)
    part = np.broadcast_to(np.arange(2).reshape(1, 2, 1), (LATS, 2, MD)).reshape(-1)
    angle = 2.0 * np.pi / NLON * ((order[:, None] * np.arange(NLON)[None, :]) % NLON)
    angle = angle.astype(np.float32)
    rows = np.where(part[:, None] == 0, np.cos(angle), -np.sin(angle))
    padded = np.zeros((2 * M, LONS, FP), np.float32)
    padded[:, :, :FD] = rows.reshape(2 * M, LONS, FD)
    return padded.reshape(2 * M, LONS * FP).astype(ml_dtypes.bfloat16)


def latitudes():
    angle = ((np.arange(NLAT) + 0.5) * (np.pi / NLAT)).reshape(LATS, TD)
    cosine = np.zeros((LATS, TP), np.float32)
    logsine = np.zeros((LATS, TP), np.float32)
    cosine[:, :TD] = np.cos(angle)
    logsine[:, :TD] = np.log(np.sin(angle))
    half = LATS // 2
    return cosine[:half].reshape(1, -1), logsine[:half].reshape(1, -1)


def seed_logs():
    degree = np.arange(M, dtype=np.float64)
    steps = np.log((2.0 * degree + 1.0) / (2.0 * degree + 2.0))
    prefix = np.concatenate([np.zeros(1), np.cumsum(steps)[:-1]])
    return (0.5 * np.log((2.0 * degree + 1.0) / (4.0 * np.pi)) + 0.5 * prefix).astype(np.float32)


def band_lanes():
    mark = np.zeros((TD, 3, 256), np.float32)
    for t in range(TD):
        for rr in range(3):
            start = (t % QUAD + rr) * XW
            mark[t, rr, start:start + XW] = 1.0
    return mark


def tap_table(taps, offsets, counts, first_row):
    slot_ids = lax.broadcasted_iota(jnp.int32, taps.shape, 3)
    live = jnp.where(slot_ids < counts[:, None, None, None], taps, 0.0).astype(BF16).astype(F32)
    shift = (R - offsets).astype(F32)[:, None]
    both = jnp.concatenate([live, shift], axis=1)
    both = jnp.pad(both, ((1, 1), (0, 0), (0, 0), (0, 0)))
    both = lax.dynamic_slice_in_dim(both, first_row, TD + 2, 0)
    marks = band_lanes()
    table = 0.0
    for rr in range(3):
        mine = both[rr:rr + TD, :, 2 - rr, :].reshape(TD, (K + 1) * S)
        table = table + mine[:, :, None] * marks[:, rr][:, None, :]
    return table


def on_device(field, cotangent, mix_weight, taps, offsets, counts):
    lat_pos = lax.axis_index(LAT)
    up = [(i, (i + 1) % LONS) for i in range(LONS)]
    down = [(j, i) for i, j in up]
    left = lax.ppermute(cotangent[:, FD - R:], LON, up)
    right = lax.ppermute(cotangent[:, :R], LON, down)
    edge_rows = [
        jnp.concatenate([left[t:t + 1], cotangent[t:t + 1], right[t:t + 1]], axis=1) for t in (0, TD - 1)
    ]
    north = [(i, i + 1) for i in range(LATS - 1)]
    south = [(j, i) for i, j in north]
    top = lax.ppermute(edge_rows[1], LAT, north)
    bottom = lax.ppermute(edge_rows[0], LAT, south)

    whole = pl.BlockSpec(memory_space=pltpu.VMEM)
    tab = tap_table(taps, offsets, counts, lat_pos * TD)
    cells = TD * FD
    grown, mix_part = call(
        stencil_kernel,
        (shape((cells, K * C), BF16), shape((C, K * C), BF16)),
        5,
        in_specs=[whole] * 7,
        scratch_shapes=[pltpu.VMEM((TD + 2, XW, C), F32), pltpu.VMEM((K * QUAD * FD, 256), F32)],
        name="stencil",
    )(near(tab), cotangent, near(left), near(right), near(top), near(bottom), field.reshape(cells, C))
    mix_lat = lax.all_to_all(mix_part.reshape(LATS, MD, K * C), LAT, 0, 0, tiled=True)

    pos = jnp.reshape(lat_pos, (1,)).astype(jnp.int32)
    grad_field, send = call(
        field_kernel,
        (shape((cells, C), BF16), shape((LONS, FP, CD * TP), BF16)),
        5,
        in_specs=[pl.BlockSpec(memory_space=pltpu.SMEM), whole, whole, whole],
        scratch_shapes=[
            pltpu.VMEM((C // 128, cells, 128), F32),
            pltpu.VMEM((FD // 4, C, 128), F32),
            pltpu.VMEM((CD // 4, LONS * FD, 128), F32),
        ],
        name="grad_field",
    )(pos, grown, cotangent.reshape(cells, C), mix_weight)
    anywhere = pl.BlockSpec(memory_space=pl.ANY)
    send = call(
        sum_lat_kernel,
        shape((LONS, FP, CD * TP), BF16),
        2,
        in_specs=[whole, anywhere],
        out_specs=anywhere,
        scratch_shapes=[pltpu.VMEM((LONS, FP - FD, CD * TP), BF16), pltpu.SemaphoreType.DMA],
        input_output_aliases={1: 0},
        name="mix_sum_lat",
    )(near(mix_lat), send)
    columns = lax.all_to_all(send, LON, 0, 0, tiled=True)

    cosine, logsine = latitudes()
    first_order = lat_pos * MD
    seeds = lax.dynamic_slice_in_dim(jnp.asarray(seed_logs()), first_order, MD, 0)
    orders = (first_order + jnp.arange(MD, dtype=jnp.int32)).astype(F32)
    logscale = seeds[:, None] + orders[:, None] * logsine
    logscale, _ = lax.optimization_barrier((logscale, send))
    table = call(
        legendre_kernel,
        shape((MD // 2, L, 2 * HALF), BF16),
        9,
        grid_spec=pltpu.PrefetchScalarGridSpec(
            num_scalar_prefetch=1,
            grid=(L // LB,),
            in_specs=[
                pl.BlockSpec((1, HALF), lambda b, pos: (0, 0)),
                pl.BlockSpec((MD, HALF), lambda b, pos: (0, 0)),
            ],
            out_specs=pl.BlockSpec((MD // 2, LB, 2 * HALF), lambda b, pos: (0, b, 0)),
            scratch_shapes=[
                pltpu.VMEM((MD, 128), F32),
                pltpu.VMEM((MD, HALF), F32),
                pltpu.VMEM((MD, HALF), F32),
                pltpu.VMEM((MD, HALF), F32),
                pltpu.VMEM((LB * MD, HALF), F32),
            ],
        ),
        name="legendre",
    )(pos, jnp.asarray(cosine), logscale)
    columns, table = lax.optimization_barrier((columns, table))

    spectra = call(dft_kernel, shape((LATS, 2 * MD + FP - FD, CD * TP), BF16), 2, in_specs=[whole, whole], name="dft")(
        near(jnp.asarray(dft_rows())), near(columns.reshape(LONS * FP, CD * TP))
    )
    spec = lax.all_to_all(spectra, LAT, 0, 0, tiled=True)
    mix_copies = call(copies_kernel, shape((CHIPS, LATS, 8, 256), BF16), 2, in_specs=[whole], name="mix_copies")(near(spec))
    mix_mine = lax.all_to_all(mix_copies, CHIP, 0, 0, tiled=True)

    grad_spectra = call(
        synthesis_kernel,
        shape((2, CD, MD, L), F32),
        6,
        grid_spec=pltpu.PrefetchScalarGridSpec(
            num_scalar_prefetch=0,
            grid=(MD // MSTEP,),
            in_specs=[
                whole,
                pl.BlockSpec((MSTEP // 2, L, 2 * HALF), lambda b: (b, 0, 0)),
            ],
            out_specs=pl.BlockSpec((2, CD, MSTEP, L), lambda b: (0, 0, b, 0)),
            scratch_shapes=[
                pltpu.VMEM((4 * CD * MD, HALF), F32),
                pltpu.VMEM((L // 128, 2 * CD * MSTEP, 128), F32),
            ],
        ),
        name="synthesis",
    )(near(spec), table)
    mix_mine, grad_spectra = lax.optimization_barrier((mix_mine, grad_spectra))
    mix_other = lax.ppermute(mix_mine, CORE, [(0, 1), (1, 0)])
    grad_mix = call(
        mix_kernel,
        shape((K, C, C), F32),
        2,
        in_specs=[pl.BlockSpec(memory_space=pltpu.SMEM), whole, whole],
        out_specs=anywhere,
        scratch_shapes=[pltpu.VMEM((K, C, C), F32), pltpu.SemaphoreType.DMA((LATS,))],
        name="mix_out",
    )(jnp.reshape(lax.axis_index(CORE), (1,)).astype(jnp.int32), near(mix_mine), near(mix_other))
    return (grad_field.reshape(TD, FD, C), jnp.transpose(grad_spectra, (0, 2, 1, 3)), grad_mix)


def solution(mesh):
    chips = Mesh(mesh.devices.reshape(LATS, CHIPS, 2), (LAT, CHIP, CORE))
    placed = (P(LAT, LON, None), P(LAT, LON, None), P(), P(), P(), P())
    return jax.shard_map(
        on_device,
        mesh=chips,
        in_specs=placed,
        out_specs=(P(LAT, LON, None), P(None, LAT, LON, None), P()),
        check_vma=False,
    )
```

```python
import functools
import math

import jax
import jax.numpy as jnp
import ml_dtypes
import numpy as np
from jax import lax
from jax.experimental import pallas as pl
from jax.experimental.pallas import tpu as pltpu
from jax.sharding import Mesh, PartitionSpec as P

C = 384
M = 384
L = 384
K = 3
R = 8
S = 8
LB = 32
NLAT = 192
NLON = 768
LATS = 8
LONS = 32
TD = NLAT // LATS
FD = NLON // LONS
CD = C // LONS
MD = M // LATS
XW = FD + 2 * R
TP = 32
FP = FD + 8
GROUPS = CD * TP // 128
SLOTS = 7
SENT = GROUPS * FP + (SLOTS - GROUPS) * 8
SPREAD = 40
QUAD = 4
CHIPS = LONS // 2
LAT = "lat"
CHIP = "chip"
CORE = "core"
LON = (CHIP, CORE)
F32 = jnp.float32
BF16 = jnp.bfloat16
VMEM_BYTES = 56 * 1024 * 1024


def call(kernel, out_shape, us, **kw):
    return pl.pallas_call(
        kernel,
        out_shape=out_shape,
        cost_estimate=pl.CostEstimate(flops=int(us * 1.1e9), bytes_accessed=int(us * 3.0e6), transcendentals=0),
        compiler_params=pltpu.CompilerParams(vmem_limit_bytes=VMEM_BYTES),
        **kw,
    )


def near(array):
    return pltpu.with_memory_space_constraint(array, pltpu.VMEM)


def shape(dims, dtype):
    return jax.ShapeDtypeStruct(dims, dtype)


def swap_blocks(parts):
    lane = lax.broadcasted_iota(jnp.int32, parts[0].shape, 1)
    low = lane < 64
    even = (lane & 32) == 0
    a0, a1, a2, a3 = parts
    b0 = jnp.where(low, a0, pltpu.roll(a2, 64, 1))
    b2 = jnp.where(low, pltpu.roll(a0, 64, 1), a2)
    b1 = jnp.where(low, a1, pltpu.roll(a3, 64, 1))
    b3 = jnp.where(low, pltpu.roll(a1, 64, 1), a3)
    c0 = jnp.where(even, b0, pltpu.roll(b1, 32, 1))
    c1 = jnp.where(even, pltpu.roll(b0, 96, 1), b1)
    c2 = jnp.where(even, b2, pltpu.roll(b3, 32, 1))
    c3 = jnp.where(even, pltpu.roll(b2, 96, 1), b3)
    return c0, c1, c2, c3


def stencil_kernel(core, tab, cot, left, right, top, bottom, field, g_out, mine_out, other_out, ext, band):
    ext[1:TD + 1, 0:R, :] = left[...].astype(F32)
    ext[1:TD + 1, R:R + FD, :] = cot[...].astype(F32)
    ext[1:TD + 1, R + FD:XW, :] = right[...].astype(F32)
    ext[0:1] = top[...].astype(F32)
    ext[TD + 1:TD + 2] = bottom[...].astype(F32)
    lane = lax.broadcasted_iota(jnp.int32, (FD, 256), 1)
    column = lane
    for edge in range(1, QUAD + 2):
        column = column - jnp.where(lane >= edge * XW, XW, 0)
    apart = (column - lax.broadcasted_iota(jnp.int32, (FD, 256), 0)).astype(F32)
    zero = jnp.zeros((FD, 256), F32)
    for quad in range(TD // QUAD):
        for r in range(QUAD):
            t = quad * QUAD + r
            sums = [zero] * K
            for s in range(S):
                hit = apart == tab[t, K * S + s:K * S + s + 1, :]
                for k in range(K):
                    sums[k] = sums[k] + jnp.where(hit, tab[t, k * S + s:k * S + s + 1, :], 0.0)
            for k in range(K):
                row = (k * QUAD + r) * FD
                band[row:row + FD, :] = sums[k]
        slab = ext[quad * QUAD:quad * QUAD + QUAD + 2].reshape((QUAD + 2) * XW, C).astype(BF16)
        weights = band[:, :(QUAD + 2) * XW].astype(BF16)
        got = jnp.dot(weights, slab, preferred_element_type=F32).astype(BF16)
        rows = QUAD * FD
        for k in range(K):
            g_out[quad * rows:(quad + 1) * rows, k * C:(k + 1) * C] = got[k * rows:(k + 1) * rows]
    mix = lax.dot_general(
        field[...], g_out[...], (((0,), (0,)), ((), ())), preferred_element_type=F32
    )
    mix = mix * (1.0 / math.sqrt(NLAT * NLON))
    first = core[0] == 0
    low, high = mix[:C // 2], mix[C // 2:]
    mine_out[...] = jnp.where(first, low, high)
    other_out[...] = jnp.where(first, high, low).astype(BF16)


def field_kernel(pos, g, cot, mix, gf_out, send_out, flat, turned, send):
    total = cot[...].astype(F32)
    for k in range(K):
        total = total + lax.dot_general(
            g[:, k * C:(k + 1) * C], mix[k], (((1,), (1,)), ((), ())), preferred_element_type=F32
        )
    rounded = total.astype(BF16)
    gf_out[...] = rounded
    rounded = rounded.astype(F32)
    southern = pos[0] >= LATS // 2
    for t in range(TD):
        row = pl.multiple_of(jnp.where(southern, TD - 1 - t, t) * FD, FD)
        for h in range(C // 128):
            flat[h, pl.ds(row, FD), :] = rounded[t * FD:(t + 1) * FD, h * 128:(h + 1) * 128]
    pad = jnp.zeros((TP - TD, 128), F32)
    for fq in range(FD // 4):
        for h in range(C // 128):
            pieces = []
            for fr in range(4):
                pieces.append(flat[h, pl.ds(fq * 4 + fr, TD, stride=FD), :])
                pieces.append(pad)
            turned[fq, h * 128:(h + 1) * 128, :] = jnp.concatenate(pieces, axis=0).T
    for fq in range(FD // 4):
        for q in range(CD // 4):
            parts = [
                turned[fq, pl.ds(q * 4 + cr, LONS, stride=CD), :] for cr in range(4)
            ]
            for fr, part in enumerate(swap_blocks(parts)):
                send[q, pl.ds(fq * 4 + fr, LONS, stride=FD), :] = part
    for q in range(GROUPS):
        send_out[:, q * FP:q * FP + FD, :] = send[q].reshape(LONS, FD, 128).astype(BF16)


def slot_row(slot):
    return slot * FP + FD if slot < GROUPS else GROUPS * FP + (slot - GROUPS) * 8


def piece_place(piece):
    return 2 * MD + piece // GROUPS * 8, piece % GROUPS * 128


def dft_kernel(rows, columns, out):
    wide = jnp.concatenate(
        [columns[:, q * FP:(q + 1) * FP, :].reshape(LONS * FP, 128) for q in range(GROUPS)], axis=1
    )
    got = jnp.dot(rows[...], wide, preferred_element_type=F32)
    got = (got * (1.0 / math.sqrt(NLON))).astype(BF16)
    for i in range(LATS):
        out[i, :2 * MD, :] = got[i * 2 * MD:(i + 1) * 2 * MD]
    for half in range(2):
        for slot in range(SLOTS):
            first = slot_row(slot) // 16 * 16
            start = slot_row(slot) - first
            total = columns[half, first:first + 16, :].astype(F32)
            for chip in range(1, CHIPS):
                total = total + columns[2 * chip + half, first:first + 16, :].astype(F32)
            total = total[start:start + 8].astype(BF16)
            row, lane = piece_place(half * SLOTS + slot)
            for i in range(LATS):
                out[i, row:row + 8, lane:lane + 128] = total


HALF = LATS // 2 * TP


def legendre_kernel(pos, cosines, logscale, out, coef, prev_s, early_s, scale_s, rows):
    block = pl.program_id(0)
    order = pos[0] * MD + lax.broadcasted_iota(jnp.int32, (MD, 128), 0)
    order_f = order.astype(F32)

    @pl.when(block == 0)
    def _():
        prev_s[...] = jnp.zeros_like(prev_s)
        early_s[...] = jnp.zeros_like(early_s)
        scale_s[...] = logscale[...]

    lane = lax.broadcasted_iota(jnp.int32, (MD, 128), 1)
    degree = block * LB + (lane & (LB - 1))
    deg_f = degree.astype(F32)
    higher = degree > order
    lower_a = jnp.where(higher, deg_f * deg_f - order_f * order_f, 1.0)
    factor_a = jnp.where(higher, jnp.sqrt((4.0 * deg_f * deg_f - 1.0) / lower_a), 0.0)
    before = deg_f - 1.0
    upper_b = jnp.maximum(before * before - order_f * order_f, 0.0)
    lower_b = jnp.maximum(4.0 * before * before - 1.0, 1.0)
    factor_b = jnp.sqrt(upper_b / lower_b)
    coef[...] = jnp.where(lane < LB, factor_a, factor_b)

    x = jnp.broadcast_to(cosines[...], (MD, 128))
    prev = prev_s[...]
    early = early_s[...]
    factor = jnp.exp(scale_s[...])
    for step in range(LB):
        a = jnp.broadcast_to(coef[:, step:step + 1], (MD, 128))
        b = jnp.broadcast_to(coef[:, LB + step:LB + step + 1], (MD, 128))
        seed = jnp.where(order == block * LB + step, 1.0, 0.0)
        fresh = a * (x * prev - b * early) + seed
        rows[step * MD:(step + 1) * MD, :] = fresh * factor
        early, prev = prev, fresh
    biggest = jnp.maximum(jnp.abs(prev), jnp.abs(early))
    divisor = jnp.where(biggest > 0.0, biggest, 1.0)
    prev_s[...] = prev / divisor
    early_s[...] = early / divisor
    scale_s[...] = scale_s[...] + jnp.log(divisor)
    for m in range(MD):
        side = (m % 2) * 128
        out[m // 2, :, side:side + 128] = rows[pl.ds(m, LB, stride=MD), :].astype(BF16)


MSTEP = 8


def synthesis_kernel(spec, leg, out, lined, rows):
    step = pl.program_id(0)

    @pl.when(step == 0)
    def _():
        for q in range(CD // 4):
            span = slice(q * 128, (q + 1) * 128)
            north = [spec[i, :2 * MD, span].astype(F32) for i in range(LATS // 2)]
            south = [spec[LATS - 1 - i, :2 * MD, span].astype(F32) for i in range(LATS // 2)]
            for odd in range(2):
                parts = [n - s if odd else n + s for n, s in zip(north, south)]
                for cr, part in enumerate(swap_blocks(parts)):
                    for p in range(2):
                        base = ((odd * 2 + p) * CD + q * 4 + cr) * MD
                        lined[base:base + MD, :] = part[p * MD:(p + 1) * MD]

    wide = 2 * CD
    odd_lane = (lax.broadcasted_iota(jnp.int32, (wide, L), 1) & 1) == 1
    zero = jnp.zeros((2 * wide, HALF), F32)
    for pair in range(MSTEP // 2):
        first = step * MSTEP + 2 * pair
        mine = [lined[pl.ds(first + side, 2 * wide, stride=MD), :] for side in range(2)]
        lhs = jnp.concatenate(
            [jnp.concatenate([mine[0], zero], axis=1), jnp.concatenate([zero, mine[1]], axis=1)], axis=0
        ).astype(BF16)
        got = lax.dot_general(
            lhs, leg[pair], (((1,), (1,)), ((), ())), preferred_element_type=F32
        ) * math.sqrt(4.0 * math.pi / NLAT)
        done = [
            jnp.where(odd_lane, got[wide:2 * wide], got[:wide]),
            jnp.where(odd_lane, got[2 * wide:3 * wide], got[3 * wide:]),
        ]
        for side in range(2):
            for h in range(L // 128):
                rows[h, pl.ds(2 * pair + side, wide, stride=MSTEP), :] = done[side][:, h * 128:(h + 1) * 128]
    for p in range(2):
        for c in range(CD):
            base = (p * CD + c) * MSTEP
            for h in range(L // 128):
                out[p, c, :, h * 128:(h + 1) * 128] = rows[h, base:base + MSTEP, :]


HALF_TILES = C // 32 * (K * C // 128)


def tiles_of(chip):
    return [(slot, *divmod(SLOTS * chip + slot, K * C // 128)) for slot in range(SLOTS) if SLOTS * chip + slot < HALF_TILES]


def chip_sum_kernel(mine, other, send, out, near_rows, far_rows, sems):
    total = (mine[...] + other[...].astype(F32)).astype(BF16)
    near_rows[...] = jnp.zeros_like(near_rows)
    far_rows[...] = jnp.zeros_like(far_rows)
    for chip in range(CHIPS):
        for slot, row, col in tiles_of(chip):
            for core in range(2):
                first = core * (C // 4) + row * 8
                tile = total[first:first + 8, col * 128:(col + 1) * 128]
                if slot < GROUPS:
                    near_rows[slot, 2 * chip + core] = tile
                else:
                    far = (slot - GROUPS) * 8
                    far_rows[2 * chip + core, far:far + 8, :] = tile
    copies = [
        pltpu.make_async_copy(near_rows.at[q], out.at[:, q * FP + FD:(q + 1) * FP, :], sems.at[q]) for q in range(GROUPS)
    ]
    copies.append(pltpu.make_async_copy(far_rows, out.at[:, GROUPS * FP:, :], sems.at[GROUPS]))
    for copy in copies:
        copy.start()
    for copy in copies:
        copy.wait()


def copies_kernel(spec, out):
    for piece in range(2 * SLOTS):
        row, lane = piece_place(piece)
        first = row // 16 * 16
        total = spec[0, first:first + 16, lane:lane + 128].astype(F32)
        for i in range(1, LATS):
            total = total + spec[i, first:first + 16, lane:lane + 128].astype(F32)
        total = total[row - first:row - first + 8].astype(BF16)
        for chip in range(CHIPS):
            out[chip, piece * 8:(piece + 1) * 8, :] = total


def mix_kernel(core, mine, other, out, rows, sems):
    copies = []
    for half in range(2):
        for parts, held in ((mine, core[0]), (other, 1 - core[0])):
            base = pl.multiple_of(half * (C // 2) + held * (C // 4), 8)
            for chip in range(CHIPS):
                for slot, row, col in tiles_of(chip):
                    k, d = divmod(col, C // 128)
                    piece = (half * SLOTS + slot) * 8
                    rows[k, pl.ds(base + row * 8, 8), d * 128:(d + 1) * 128] = parts[
                        chip, piece:piece + 8, :
                    ].astype(F32)
        span = pl.ds(half * (C // 2), C // 2)
        copies.append(pltpu.make_async_copy(rows.at[:, span], out.at[:, span], sems.at[half]))
        copies[-1].start()
    for copy in copies:
        copy.wait()


def dft_rows():
    order = np.arange(M).reshape(LATS, 1, MD)
    order = np.broadcast_to(order, (LATS, 2, MD)).reshape(-1)
    part = np.broadcast_to(np.arange(2).reshape(1, 2, 1), (LATS, 2, MD)).reshape(-1)
    angle = 2.0 * np.pi / NLON * ((order[:, None] * np.arange(NLON)[None, :]) % NLON)
    angle = angle.astype(np.float32)
    rows = np.where(part[:, None] == 0, np.cos(angle), -np.sin(angle))
    padded = np.zeros((2 * M, LONS, FP), np.float32)
    padded[:, :, :FD] = rows.reshape(2 * M, LONS, FD)
    return padded.reshape(2 * M, LONS * FP).astype(ml_dtypes.bfloat16)


def latitudes():
    angle = ((np.arange(NLAT) + 0.5) * (np.pi / NLAT)).reshape(LATS, TD)
    cosine = np.zeros((LATS, TP), np.float32)
    logsine = np.zeros((LATS, TP), np.float32)
    cosine[:, :TD] = np.cos(angle)
    logsine[:, :TD] = np.log(np.sin(angle))
    half = LATS // 2
    return cosine[:half].reshape(1, -1), logsine[:half].reshape(1, -1)


def seed_logs():
    degree = np.arange(M, dtype=np.float64)
    steps = np.log((2.0 * degree + 1.0) / (2.0 * degree + 2.0))
    prefix = np.concatenate([np.zeros(1), np.cumsum(steps)[:-1]])
    return (0.5 * np.log((2.0 * degree + 1.0) / (4.0 * np.pi)) + 0.5 * prefix).astype(np.float32)


def band_lanes():
    mark = np.zeros((TD, 3, 256), np.float32)
    for t in range(TD):
        for rr in range(3):
            start = (t % QUAD + rr) * XW
            mark[t, rr, start:start + XW] = 1.0
    return mark


def tap_table(taps, offsets, counts, first_row):
    slot_ids = lax.broadcasted_iota(jnp.int32, taps.shape, 3)
    live = jnp.where(slot_ids < counts[:, None, None, None], taps, 0.0).astype(BF16).astype(F32)
    shift = (R - offsets).astype(F32)[:, None]
    both = jnp.concatenate([live, shift], axis=1)
    both = jnp.pad(both, ((1, 1), (0, 0), (0, 0), (0, 0)))
    both = lax.dynamic_slice_in_dim(both, first_row, TD + 2, 0)
    marks = band_lanes()
    table = 0.0
    for rr in range(3):
        mine = both[rr:rr + TD, :, 2 - rr, :].reshape(TD, (K + 1) * S)
        table = table + mine[:, :, None] * marks[:, rr][:, None, :]
    return table


def on_device(field, cotangent, mix_weight, taps, offsets, counts):
    lat_pos = lax.axis_index(LAT)
    up = [(i, (i + 1) % LONS) for i in range(LONS)]
    down = [(j, i) for i, j in up]
    left = lax.ppermute(cotangent[:, FD - R:], LON, up)
    right = lax.ppermute(cotangent[:, :R], LON, down)
    edge_rows = [
        jnp.concatenate([left[t:t + 1], cotangent[t:t + 1], right[t:t + 1]], axis=1) for t in (0, TD - 1)
    ]
    north = [(i, i + 1) for i in range(LATS - 1)]
    south = [(j, i) for i, j in north]
    top = lax.ppermute(edge_rows[1], LAT, north)
    bottom = lax.ppermute(edge_rows[0], LAT, south)

    whole = pl.BlockSpec(memory_space=pltpu.VMEM)
    tab = tap_table(taps, offsets, counts, lat_pos * TD)
    cells = TD * FD
    core = jnp.reshape(lax.axis_index(CORE), (1,)).astype(jnp.int32)
    scalar = pl.BlockSpec(memory_space=pltpu.SMEM)
    anywhere = pl.BlockSpec(memory_space=pl.ANY)
    half = (C // 2, K * C)
    grown, mix_mine, mix_other = call(
        stencil_kernel,
        (shape((cells, K * C), BF16), shape(half, F32), shape(half, BF16)),
        5,
        in_specs=[scalar] + [whole] * 7,
        scratch_shapes=[pltpu.VMEM((TD + 2, XW, C), F32), pltpu.VMEM((K * QUAD * FD, 256), F32)],
        name="stencil",
    )(core, near(tab), cotangent, near(left), near(right), near(top), near(bottom), field.reshape(cells, C))
    swap = [(0, 1), (1, 0)]
    mix_other = lax.ppermute(mix_other, CORE, swap)

    pos = jnp.reshape(lat_pos, (1,)).astype(jnp.int32)
    grad_field, send = call(
        field_kernel,
        (shape((cells, C), BF16), shape((LONS, SENT, 128), BF16)),
        5,
        in_specs=[scalar, whole, whole, whole],
        scratch_shapes=[
            pltpu.VMEM((C // 128, cells, 128), F32),
            pltpu.VMEM((FD // 4, C, 128), F32),
            pltpu.VMEM((CD // 4, LONS * FD, 128), F32),
        ],
        name="grad_field",
    )(pos, grown, cotangent.reshape(cells, C), mix_weight)
    send = call(
        chip_sum_kernel,
        shape((LONS, SENT, 128), BF16),
        2,
        in_specs=[whole, whole, anywhere],
        out_specs=anywhere,
        scratch_shapes=[
            pltpu.VMEM((GROUPS, LONS, FP - FD, 128), BF16),
            pltpu.VMEM((LONS, SENT - GROUPS * FP, 128), BF16),
            pltpu.SemaphoreType.DMA((GROUPS + 1,)),
        ],
        input_output_aliases={2: 0},
        name="mix_chip_sum",
    )(near(mix_mine), near(mix_other), send)
    columns = lax.all_to_all(send, LON, 0, 0, tiled=True)

    cosine, logsine = latitudes()
    first_order = lat_pos * MD
    seeds = lax.dynamic_slice_in_dim(jnp.asarray(seed_logs()), first_order, MD, 0)
    orders = (first_order + jnp.arange(MD, dtype=jnp.int32)).astype(F32)
    logscale = seeds[:, None] + orders[:, None] * logsine
    logscale, _ = lax.optimization_barrier((logscale, send))
    table = call(
        legendre_kernel,
        shape((MD // 2, L, 2 * HALF), BF16),
        9,
        grid_spec=pltpu.PrefetchScalarGridSpec(
            num_scalar_prefetch=1,
            grid=(L // LB,),
            in_specs=[
                pl.BlockSpec((1, HALF), lambda b, pos: (0, 0)),
                pl.BlockSpec((MD, HALF), lambda b, pos: (0, 0)),
            ],
            out_specs=pl.BlockSpec((MD // 2, LB, 2 * HALF), lambda b, pos: (0, b, 0)),
            scratch_shapes=[
                pltpu.VMEM((MD, 128), F32),
                pltpu.VMEM((MD, HALF), F32),
                pltpu.VMEM((MD, HALF), F32),
                pltpu.VMEM((MD, HALF), F32),
                pltpu.VMEM((LB * MD, HALF), F32),
            ],
        ),
        name="legendre",
    )(pos, jnp.asarray(cosine), logscale)
    columns, table = lax.optimization_barrier((columns, table))

    spectra = call(dft_kernel, shape((LATS, 2 * MD + SPREAD, CD * TP), BF16), 2, in_specs=[whole, whole], name="dft")(
        near(jnp.asarray(dft_rows())), near(columns)
    )
    spec = lax.all_to_all(spectra, LAT, 0, 0, tiled=True)
    mix_copies = call(copies_kernel, shape((CHIPS, 2 * SLOTS * 8, 128), BF16), 2, in_specs=[whole], name="mix_copies")(near(spec))
    mix_mine = lax.all_to_all(mix_copies, CHIP, 0, 0, tiled=True)

    grad_spectra = call(
        synthesis_kernel,
        shape((2, CD, MD, L), F32),
        6,
        grid_spec=pltpu.PrefetchScalarGridSpec(
            num_scalar_prefetch=0,
            grid=(MD // MSTEP,),
            in_specs=[
                whole,
                pl.BlockSpec((MSTEP // 2, L, 2 * HALF), lambda b: (b, 0, 0)),
            ],
            out_specs=pl.BlockSpec((2, CD, MSTEP, L), lambda b: (0, 0, b, 0)),
            scratch_shapes=[
                pltpu.VMEM((4 * CD * MD, HALF), F32),
                pltpu.VMEM((L // 128, 2 * CD * MSTEP, 128), F32),
            ],
        ),
        name="synthesis",
    )(near(spec), table)
    mix_mine, grad_spectra = lax.optimization_barrier((mix_mine, grad_spectra))
    mix_other = lax.ppermute(mix_mine, CORE, swap)
    grad_mix = call(
        mix_kernel,
        shape((K, C, C), F32),
        2,
        in_specs=[scalar, whole, whole],
        out_specs=anywhere,
        scratch_shapes=[pltpu.VMEM((K, C, C), F32), pltpu.SemaphoreType.DMA((2,))],
        name="mix_out",
    )(core, near(mix_mine), near(mix_other))
    return (grad_field.reshape(TD, FD, C), jnp.transpose(grad_spectra, (0, 2, 1, 3)), grad_mix)


def solution(mesh):
    chips = Mesh(mesh.devices.reshape(LATS, CHIPS, 2), (LAT, CHIP, CORE))
    placed = (P(LAT, LON, None), P(LAT, LON, None), P(), P(), P(), P())
    return jax.shard_map(
        on_device,
        mesh=chips,
        in_specs=placed,
        out_specs=(P(LAT, LON, None), P(None, LAT, LON, None), P()),
        check_vma=False,
    )
```

```python
import functools
import math

import jax
import jax.numpy as jnp
import ml_dtypes
import numpy as np
from jax import lax
from jax.experimental import pallas as pl
from jax.experimental.pallas import tpu as pltpu
from jax.sharding import Mesh, PartitionSpec as P

C = 384
M = 384
L = 384
K = 3
R = 8
S = 8
LB = 32
NLAT = 192
NLON = 768
LATS = 8
LONS = 32
TD = NLAT // LATS
FD = NLON // LONS
CD = C // LONS
MD = M // LATS
XW = FD + 2 * R
TP = 32
FP = FD + 8
GROUPS = CD * TP // 128
SLOTS = 7
SENT = GROUPS * FP + (SLOTS - GROUPS) * 8
SPREAD = 40
QUAD = 4
CHIPS = LONS // 2
LAT = "lat"
CHIP = "chip"
CORE = "core"
LON = (CHIP, CORE)
F32 = jnp.float32
BF16 = jnp.bfloat16
VMEM_BYTES = 56 * 1024 * 1024


def call(kernel, out_shape, us, **kw):
    return pl.pallas_call(
        kernel,
        out_shape=out_shape,
        cost_estimate=pl.CostEstimate(flops=int(us * 1.1e9), bytes_accessed=int(us * 3.0e6), transcendentals=0),
        compiler_params=pltpu.CompilerParams(vmem_limit_bytes=VMEM_BYTES),
        **kw,
    )


def near(array):
    return pltpu.with_memory_space_constraint(array, pltpu.VMEM)


def shape(dims, dtype):
    return jax.ShapeDtypeStruct(dims, dtype)


def near_shape(dims, dtype):
    return pltpu.VMEM(dims, dtype)


def swap_blocks(parts):
    lane = lax.broadcasted_iota(jnp.int32, parts[0].shape, 1)
    low = lane < 64
    even = (lane & 32) == 0
    a0, a1, a2, a3 = parts
    b0 = jnp.where(low, a0, pltpu.roll(a2, 64, 1))
    b2 = jnp.where(low, pltpu.roll(a0, 64, 1), a2)
    b1 = jnp.where(low, a1, pltpu.roll(a3, 64, 1))
    b3 = jnp.where(low, pltpu.roll(a1, 64, 1), a3)
    c0 = jnp.where(even, b0, pltpu.roll(b1, 32, 1))
    c1 = jnp.where(even, pltpu.roll(b0, 96, 1), b1)
    c2 = jnp.where(even, b2, pltpu.roll(b3, 32, 1))
    c3 = jnp.where(even, pltpu.roll(b2, 96, 1), b3)
    return c0, c1, c2, c3


def stencil_kernel(core, tab, cot, left, right, top, bottom, field, g_out, mine_out, other_out, ext, band):
    ext[1:TD + 1, 0:R, :] = left[...].astype(F32)
    ext[1:TD + 1, R:R + FD, :] = cot[...].astype(F32)
    ext[1:TD + 1, R + FD:XW, :] = right[...].astype(F32)
    ext[0:1] = top[...].astype(F32)
    ext[TD + 1:TD + 2] = bottom[...].astype(F32)
    lane = lax.broadcasted_iota(jnp.int32, (FD, 256), 1)
    column = lane
    for edge in range(1, QUAD + 2):
        column = column - jnp.where(lane >= edge * XW, XW, 0)
    apart = (column - lax.broadcasted_iota(jnp.int32, (FD, 256), 0)).astype(F32)
    zero = jnp.zeros((FD, 256), F32)
    for quad in range(TD // QUAD):
        for r in range(QUAD):
            t = quad * QUAD + r
            sums = [zero] * K
            for s in range(S):
                hit = apart == tab[t, K * S + s:K * S + s + 1, :]
                for k in range(K):
                    sums[k] = sums[k] + jnp.where(hit, tab[t, k * S + s:k * S + s + 1, :], 0.0)
            for k in range(K):
                row = (k * QUAD + r) * FD
                band[row:row + FD, :] = sums[k]
        slab = ext[quad * QUAD:quad * QUAD + QUAD + 2].reshape((QUAD + 2) * XW, C).astype(BF16)
        weights = band[:, :(QUAD + 2) * XW].astype(BF16)
        got = jnp.dot(weights, slab, preferred_element_type=F32).astype(BF16)
        rows = QUAD * FD
        for k in range(K):
            g_out[quad * rows:(quad + 1) * rows, k * C:(k + 1) * C] = got[k * rows:(k + 1) * rows]
    mix = lax.dot_general(
        field[...], g_out[...], (((0,), (0,)), ((), ())), preferred_element_type=F32
    )
    mix = mix * (1.0 / math.sqrt(NLAT * NLON))
    first = core[0] == 0
    low, high = mix[:C // 2], mix[C // 2:]
    mine_out[...] = jnp.where(first, low, high)
    other_out[...] = jnp.where(first, high, low).astype(BF16)


def field_kernel(pos, g, cot, mix, gf_out, send_out, flat, turned, send):
    total = cot[...].astype(F32)
    for k in range(K):
        total = total + lax.dot_general(
            g[:, k * C:(k + 1) * C], mix[k], (((1,), (1,)), ((), ())), preferred_element_type=F32
        )
    rounded = total.astype(BF16)
    gf_out[...] = rounded
    rounded = rounded.astype(F32)
    southern = pos[0] >= LATS // 2
    for t in range(TD):
        row = pl.multiple_of(jnp.where(southern, TD - 1 - t, t) * FD, FD)
        for h in range(C // 128):
            flat[h, pl.ds(row, FD), :] = rounded[t * FD:(t + 1) * FD, h * 128:(h + 1) * 128]
    pad = jnp.zeros((TP - TD, 128), F32)
    for fq in range(FD // 4):
        for h in range(C // 128):
            pieces = []
            for fr in range(4):
                pieces.append(flat[h, pl.ds(fq * 4 + fr, TD, stride=FD), :])
                pieces.append(pad)
            turned[fq, h * 128:(h + 1) * 128, :] = jnp.concatenate(pieces, axis=0).T
    for fq in range(FD // 4):
        for q in range(CD // 4):
            parts = [
                turned[fq, pl.ds(q * 4 + cr, LONS, stride=CD), :] for cr in range(4)
            ]
            for fr, part in enumerate(swap_blocks(parts)):
                send[q, pl.ds(fq * 4 + fr, LONS, stride=FD), :] = part
    for q in range(GROUPS):
        send_out[:, q * FP:q * FP + FD, :] = send[q].reshape(LONS, FD, 128).astype(BF16)


def slot_row(slot):
    return slot * FP + FD if slot < GROUPS else GROUPS * FP + (slot - GROUPS) * 8


def piece_place(piece):
    return 2 * MD + piece // GROUPS * 8, piece % GROUPS * 128


def dft_kernel(rows, columns, out):
    wide = jnp.concatenate(
        [columns[:, q * FP:(q + 1) * FP, :].reshape(LONS * FP, 128) for q in range(GROUPS)], axis=1
    )
    got = jnp.dot(rows[...], wide, preferred_element_type=F32)
    got = (got * (1.0 / math.sqrt(NLON))).astype(BF16)
    for i in range(LATS):
        out[i, :2 * MD, :] = got[i * 2 * MD:(i + 1) * 2 * MD]
    for half in range(2):
        for slot in range(SLOTS):
            first = slot_row(slot) // 16 * 16
            start = slot_row(slot) - first
            total = columns[half, first:first + 16, :].astype(F32)
            for chip in range(1, CHIPS):
                total = total + columns[2 * chip + half, first:first + 16, :].astype(F32)
            total = total[start:start + 8].astype(BF16)
            row, lane = piece_place(half * SLOTS + slot)
            for i in range(LATS):
                out[i, row:row + 8, lane:lane + 128] = total


HALF = LATS // 2 * TP


def legendre_kernel(pos, cosines, logscale, out, coef, prev_s, early_s, scale_s, rows):
    block = pl.program_id(0)
    order = pos[0] * MD + lax.broadcasted_iota(jnp.int32, (MD, 128), 0)
    order_f = order.astype(F32)

    @pl.when(block == 0)
    def _():
        prev_s[...] = jnp.zeros_like(prev_s)
        early_s[...] = jnp.zeros_like(early_s)
        scale_s[...] = logscale[...]

    lane = lax.broadcasted_iota(jnp.int32, (MD, 128), 1)
    degree = block * LB + (lane & (LB - 1))
    deg_f = degree.astype(F32)
    higher = degree > order
    lower_a = jnp.where(higher, deg_f * deg_f - order_f * order_f, 1.0)
    factor_a = jnp.where(higher, jnp.sqrt((4.0 * deg_f * deg_f - 1.0) / lower_a), 0.0)
    before = deg_f - 1.0
    upper_b = jnp.maximum(before * before - order_f * order_f, 0.0)
    lower_b = jnp.maximum(4.0 * before * before - 1.0, 1.0)
    factor_b = jnp.sqrt(upper_b / lower_b)
    coef[...] = jnp.where(lane < LB, factor_a, factor_b)

    x = jnp.broadcast_to(cosines[...], (MD, 128))
    prev = prev_s[...]
    early = early_s[...]
    factor = jnp.exp(scale_s[...])
    for step in range(LB):
        a = jnp.broadcast_to(coef[:, step:step + 1], (MD, 128))
        b = jnp.broadcast_to(coef[:, LB + step:LB + step + 1], (MD, 128))
        seed = jnp.where(order == block * LB + step, 1.0, 0.0)
        fresh = a * (x * prev - b * early) + seed
        rows[step * MD:(step + 1) * MD, :] = fresh * factor
        early, prev = prev, fresh
    biggest = jnp.maximum(jnp.abs(prev), jnp.abs(early))
    divisor = jnp.where(biggest > 0.0, biggest, 1.0)
    prev_s[...] = prev / divisor
    early_s[...] = early / divisor
    scale_s[...] = scale_s[...] + jnp.log(divisor)
    for m in range(MD):
        side = (m % 2) * 128
        out[m // 2, :, side:side + 128] = rows[pl.ds(m, LB, stride=MD), :].astype(BF16)


MSTEP = 8


def synthesis_kernel(spec, leg, out, lined, rows):
    step = pl.program_id(0)

    @pl.when(step == 0)
    def _():
        for q in range(CD // 4):
            span = slice(q * 128, (q + 1) * 128)
            north = [spec[i, :2 * MD, span].astype(F32) for i in range(LATS // 2)]
            south = [spec[LATS - 1 - i, :2 * MD, span].astype(F32) for i in range(LATS // 2)]
            for odd in range(2):
                parts = [n - s if odd else n + s for n, s in zip(north, south)]
                for cr, part in enumerate(swap_blocks(parts)):
                    for p in range(2):
                        base = ((odd * 2 + p) * CD + q * 4 + cr) * MD
                        lined[base:base + MD, :] = part[p * MD:(p + 1) * MD]

    wide = 2 * CD
    odd_lane = (lax.broadcasted_iota(jnp.int32, (wide, L), 1) & 1) == 1
    zero = jnp.zeros((2 * wide, HALF), F32)
    for pair in range(MSTEP // 2):
        first = step * MSTEP + 2 * pair
        mine = [lined[pl.ds(first + side, 2 * wide, stride=MD), :] for side in range(2)]
        lhs = jnp.concatenate(
            [jnp.concatenate([mine[0], zero], axis=1), jnp.concatenate([zero, mine[1]], axis=1)], axis=0
        ).astype(BF16)
        got = lax.dot_general(
            lhs, leg[pair], (((1,), (1,)), ((), ())), preferred_element_type=F32
        ) * math.sqrt(4.0 * math.pi / NLAT)
        done = [
            jnp.where(odd_lane, got[wide:2 * wide], got[:wide]),
            jnp.where(odd_lane, got[2 * wide:3 * wide], got[3 * wide:]),
        ]
        for side in range(2):
            for h in range(L // 128):
                rows[h, pl.ds(2 * pair + side, wide, stride=MSTEP), :] = done[side][:, h * 128:(h + 1) * 128]
    for p in range(2):
        for c in range(CD):
            base = (p * CD + c) * MSTEP
            for h in range(L // 128):
                out[p, c, :, h * 128:(h + 1) * 128] = rows[h, base:base + MSTEP, :]


HALF_TILES = C // 32 * (K * C // 128)


def tiles_of(chip):
    return [(slot, *divmod(SLOTS * chip + slot, K * C // 128)) for slot in range(SLOTS) if SLOTS * chip + slot < HALF_TILES]


def chip_sum_kernel(mine, other, send, out, near_rows, far_rows, sems):
    total = (mine[...] + other[...].astype(F32)).astype(BF16)
    near_rows[...] = jnp.zeros_like(near_rows)
    far_rows[...] = jnp.zeros_like(far_rows)
    for chip in range(CHIPS):
        for slot, row, col in tiles_of(chip):
            for core in range(2):
                first = core * (C // 4) + row * 8
                tile = total[first:first + 8, col * 128:(col + 1) * 128]
                if slot < GROUPS:
                    near_rows[slot, 2 * chip + core] = tile
                else:
                    far = (slot - GROUPS) * 8
                    far_rows[2 * chip + core, far:far + 8, :] = tile
    copies = [
        pltpu.make_async_copy(near_rows.at[q], out.at[:, q * FP + FD:(q + 1) * FP, :], sems.at[q]) for q in range(GROUPS)
    ]
    copies.append(pltpu.make_async_copy(far_rows, out.at[:, GROUPS * FP:, :], sems.at[GROUPS]))
    for copy in copies:
        copy.start()
    for copy in copies:
        copy.wait()


def copies_kernel(spec, out):
    for piece in range(2 * SLOTS):
        row, lane = piece_place(piece)
        first = row // 16 * 16
        total = spec[0, first:first + 16, lane:lane + 128].astype(F32)
        for i in range(1, LATS):
            total = total + spec[i, first:first + 16, lane:lane + 128].astype(F32)
        total = total[row - first:row - first + 8].astype(BF16)
        for chip in range(CHIPS):
            out[chip, piece * 8:(piece + 1) * 8, :] = total


def mix_kernel(core, mine, other, out, rows, sems):
    copies = []
    for half in range(2):
        for parts, held in ((mine, core[0]), (other, 1 - core[0])):
            base = pl.multiple_of(half * (C // 2) + held * (C // 4), 8)
            for chip in range(CHIPS):
                for slot, row, col in tiles_of(chip):
                    k, d = divmod(col, C // 128)
                    piece = (half * SLOTS + slot) * 8
                    rows[k, pl.ds(base + row * 8, 8), d * 128:(d + 1) * 128] = parts[
                        chip, piece:piece + 8, :
                    ].astype(F32)
        span = pl.ds(half * (C // 2), C // 2)
        copies.append(pltpu.make_async_copy(rows.at[:, span], out.at[:, span], sems.at[half]))
        copies[-1].start()
    for copy in copies:
        copy.wait()


def dft_rows():
    order = np.arange(M).reshape(LATS, 1, MD)
    order = np.broadcast_to(order, (LATS, 2, MD)).reshape(-1)
    part = np.broadcast_to(np.arange(2).reshape(1, 2, 1), (LATS, 2, MD)).reshape(-1)
    angle = 2.0 * np.pi / NLON * ((order[:, None] * np.arange(NLON)[None, :]) % NLON)
    angle = angle.astype(np.float32)
    rows = np.where(part[:, None] == 0, np.cos(angle), -np.sin(angle))
    padded = np.zeros((2 * M, LONS, FP), np.float32)
    padded[:, :, :FD] = rows.reshape(2 * M, LONS, FD)
    return padded.reshape(2 * M, LONS * FP).astype(ml_dtypes.bfloat16)


def latitudes():
    angle = ((np.arange(NLAT) + 0.5) * (np.pi / NLAT)).reshape(LATS, TD)
    cosine = np.zeros((LATS, TP), np.float32)
    logsine = np.zeros((LATS, TP), np.float32)
    cosine[:, :TD] = np.cos(angle)
    logsine[:, :TD] = np.log(np.sin(angle))
    half = LATS // 2
    return cosine[:half].reshape(1, -1), logsine[:half].reshape(1, -1)


def seed_logs():
    degree = np.arange(M, dtype=np.float64)
    steps = np.log((2.0 * degree + 1.0) / (2.0 * degree + 2.0))
    prefix = np.concatenate([np.zeros(1), np.cumsum(steps)[:-1]])
    return (0.5 * np.log((2.0 * degree + 1.0) / (4.0 * np.pi)) + 0.5 * prefix).astype(np.float32)


def band_lanes():
    mark = np.zeros((TD, 3, 256), np.float32)
    for t in range(TD):
        for rr in range(3):
            start = (t % QUAD + rr) * XW
            mark[t, rr, start:start + XW] = 1.0
    return mark


def tap_table(taps, offsets, counts, first_row):
    slot_ids = lax.broadcasted_iota(jnp.int32, taps.shape, 3)
    live = jnp.where(slot_ids < counts[:, None, None, None], taps, 0.0).astype(BF16).astype(F32)
    shift = (R - offsets).astype(F32)[:, None]
    both = jnp.concatenate([live, shift], axis=1)
    both = jnp.pad(both, ((1, 1), (0, 0), (0, 0), (0, 0)))
    both = lax.dynamic_slice_in_dim(both, first_row, TD + 2, 0)
    marks = band_lanes()
    table = 0.0
    for rr in range(3):
        mine = both[rr:rr + TD, :, 2 - rr, :].reshape(TD, (K + 1) * S)
        table = table + mine[:, :, None] * marks[:, rr][:, None, :]
    return table


def on_device(field, cotangent, mix_weight, taps, offsets, counts):
    lat_pos = lax.axis_index(LAT)
    up = [(i, (i + 1) % LONS) for i in range(LONS)]
    down = [(j, i) for i, j in up]
    left = lax.ppermute(cotangent[:, FD - R:], LON, up)
    right = lax.ppermute(cotangent[:, :R], LON, down)
    edge_rows = [
        jnp.concatenate([left[t:t + 1], cotangent[t:t + 1], right[t:t + 1]], axis=1) for t in (0, TD - 1)
    ]
    north = [(i, i + 1) for i in range(LATS - 1)]
    south = [(j, i) for i, j in north]
    top = lax.ppermute(edge_rows[1], LAT, north)
    bottom = lax.ppermute(edge_rows[0], LAT, south)

    whole = pl.BlockSpec(memory_space=pltpu.VMEM)
    taps, offsets, counts, _ = lax.optimization_barrier((taps, offsets, counts, edge_rows))
    tab = tap_table(taps, offsets, counts, lat_pos * TD)
    cells = TD * FD
    core = jnp.reshape(lax.axis_index(CORE), (1,)).astype(jnp.int32)
    scalar = pl.BlockSpec(memory_space=pltpu.SMEM)
    anywhere = pl.BlockSpec(memory_space=pl.ANY)
    half = (C // 2, K * C)
    grown, mix_mine, mix_other = call(
        stencil_kernel,
        (near_shape((cells, K * C), BF16), near_shape(half, F32), near_shape(half, BF16)),
        5,
        in_specs=[scalar] + [whole] * 7,
        scratch_shapes=[pltpu.VMEM((TD + 2, XW, C), F32), pltpu.VMEM((K * QUAD * FD, 256), F32)],
        name="stencil",
    )(core, near(tab), near(cotangent), near(left), near(right), near(top), near(bottom), near(field.reshape(cells, C)))
    swap = [(0, 1), (1, 0)]
    mix_other = lax.ppermute(mix_other, CORE, swap)

    pos = jnp.reshape(lat_pos, (1,)).astype(jnp.int32)
    grad_field, send = call(
        field_kernel,
        (shape((cells, C), BF16), shape((LONS, SENT, 128), BF16)),
        5,
        in_specs=[scalar, whole, whole, whole],
        scratch_shapes=[
            pltpu.VMEM((C // 128, cells, 128), F32),
            pltpu.VMEM((FD // 4, C, 128), F32),
            pltpu.VMEM((CD // 4, LONS * FD, 128), F32),
        ],
        name="grad_field",
    )(pos, near(grown), near(cotangent.reshape(cells, C)), near(mix_weight))
    send = call(
        chip_sum_kernel,
        shape((LONS, SENT, 128), BF16),
        2,
        in_specs=[whole, whole, anywhere],
        out_specs=anywhere,
        scratch_shapes=[
            pltpu.VMEM((GROUPS, LONS, FP - FD, 128), BF16),
            pltpu.VMEM((LONS, SENT - GROUPS * FP, 128), BF16),
            pltpu.SemaphoreType.DMA((GROUPS + 1,)),
        ],
        input_output_aliases={2: 0},
        name="mix_chip_sum",
    )(near(mix_mine), near(mix_other), send)
    columns = lax.all_to_all(send, LON, 0, 0, tiled=True)

    cosine, logsine = latitudes()
    first_order = lat_pos * MD
    seeds = lax.dynamic_slice_in_dim(jnp.asarray(seed_logs()), first_order, MD, 0)
    orders = (first_order + jnp.arange(MD, dtype=jnp.int32)).astype(F32)
    logscale = seeds[:, None] + orders[:, None] * logsine
    logscale, _ = lax.optimization_barrier((logscale, send))
    table = call(
        legendre_kernel,
        shape((MD // 2, L, 2 * HALF), BF16),
        9,
        grid_spec=pltpu.PrefetchScalarGridSpec(
            num_scalar_prefetch=1,
            grid=(L // LB,),
            in_specs=[
                pl.BlockSpec((1, HALF), lambda b, pos: (0, 0)),
                pl.BlockSpec((MD, HALF), lambda b, pos: (0, 0)),
            ],
            out_specs=pl.BlockSpec((MD // 2, LB, 2 * HALF), lambda b, pos: (0, b, 0)),
            scratch_shapes=[
                pltpu.VMEM((MD, 128), F32),
                pltpu.VMEM((MD, HALF), F32),
                pltpu.VMEM((MD, HALF), F32),
                pltpu.VMEM((MD, HALF), F32),
                pltpu.VMEM((LB * MD, HALF), F32),
            ],
        ),
        name="legendre",
    )(pos, jnp.asarray(cosine), logscale)
    columns, table = lax.optimization_barrier((columns, table))

    spectra = call(dft_kernel, near_shape((LATS, 2 * MD + SPREAD, CD * TP), BF16), 2, in_specs=[whole, whole], name="dft")(
        near(jnp.asarray(dft_rows())), near(columns)
    )
    spec = lax.all_to_all(spectra, LAT, 0, 0, tiled=True)
    mix_copies = call(copies_kernel, near_shape((CHIPS, 2 * SLOTS * 8, 128), BF16), 2, in_specs=[whole], name="mix_copies")(near(spec))
    mix_mine = lax.all_to_all(mix_copies, CHIP, 0, 0, tiled=True)

    grad_spectra = call(
        synthesis_kernel,
        shape((2, CD, MD, L), F32),
        6,
        grid_spec=pltpu.PrefetchScalarGridSpec(
            num_scalar_prefetch=0,
            grid=(MD // MSTEP,),
            in_specs=[
                whole,
                pl.BlockSpec((MSTEP // 2, L, 2 * HALF), lambda b: (b, 0, 0)),
            ],
            out_specs=pl.BlockSpec((2, CD, MSTEP, L), lambda b: (0, 0, b, 0)),
            scratch_shapes=[
                pltpu.VMEM((4 * CD * MD, HALF), F32),
                pltpu.VMEM((L // 128, 2 * CD * MSTEP, 128), F32),
            ],
        ),
        name="synthesis",
    )(near(spec), table)
    mix_mine, grad_spectra = lax.optimization_barrier((mix_mine, grad_spectra))
    mix_other = lax.ppermute(mix_mine, CORE, swap)
    grad_mix = call(
        mix_kernel,
        shape((K, C, C), F32),
        2,
        in_specs=[scalar, whole, whole],
        out_specs=anywhere,
        scratch_shapes=[pltpu.VMEM((K, C, C), F32), pltpu.SemaphoreType.DMA((2,))],
        name="mix_out",
    )(core, near(mix_mine), near(mix_other))
    return (grad_field.reshape(TD, FD, C), jnp.transpose(grad_spectra, (0, 2, 1, 3)), grad_mix)


def solution(mesh):
    chips = Mesh(mesh.devices.reshape(LATS, CHIPS, 2), (LAT, CHIP, CORE))
    placed = (P(LAT, LON, None), P(LAT, LON, None), P(), P(), P(), P())
    return jax.shard_map(
        on_device,
        mesh=chips,
        in_specs=placed,
        out_specs=(P(LAT, LON, None), P(None, LAT, LON, None), P()),
        check_vma=False,
    )
```

```python
import functools
import math

import jax
import jax.numpy as jnp
import ml_dtypes
import numpy as np
from jax import lax
from jax.experimental import pallas as pl
from jax.experimental.pallas import tpu as pltpu
from jax.sharding import Mesh, PartitionSpec as P

C = 384
M = 384
L = 384
K = 3
R = 8
S = 8
LB = 32
NLAT = 192
NLON = 768
LATS = 8
LONS = 32
TD = NLAT // LATS
FD = NLON // LONS
CD = C // LONS
MD = M // LATS
XW = FD + 2 * R
TP = 32
FP = FD + 8
COLS = CD * TD
GROUPS = COLS // 128
REST = COLS - GROUPS * 128
SLOTS = 7
REST_ROW = GROUPS * FP + (SLOTS - GROUPS) * 8
SENT = REST_ROW + 8
TAIL_ROW = GROUPS * 2 * MD + 2 * MD * REST // 128
SPREAD = TAIL_ROW + 2 * SLOTS * 8
QUAD = 4
CHIPS = LONS // 2
LAT = "lat"
CHIP = "chip"
CORE = "core"
LON = (CHIP, CORE)
F32 = jnp.float32
BF16 = jnp.bfloat16
VMEM_BYTES = 56 * 1024 * 1024


def call(kernel, out_shape, us, **kw):
    return pl.pallas_call(
        kernel,
        out_shape=out_shape,
        cost_estimate=pl.CostEstimate(flops=int(us * 1.1e9), bytes_accessed=int(us * 3.0e6), transcendentals=0),
        compiler_params=pltpu.CompilerParams(vmem_limit_bytes=VMEM_BYTES),
        **kw,
    )


def near(array):
    return pltpu.with_memory_space_constraint(array, pltpu.VMEM)


def shape(dims, dtype):
    return jax.ShapeDtypeStruct(dims, dtype)


def near_shape(dims, dtype):
    return pltpu.VMEM(dims, dtype)


def swap_blocks(parts):
    lane = lax.broadcasted_iota(jnp.int32, parts[0].shape, 1)
    low = lane < 64
    even = (lane & 32) == 0
    a0, a1, a2, a3 = parts
    b0 = jnp.where(low, a0, pltpu.roll(a2, 64, 1))
    b2 = jnp.where(low, pltpu.roll(a0, 64, 1), a2)
    b1 = jnp.where(low, a1, pltpu.roll(a3, 64, 1))
    b3 = jnp.where(low, pltpu.roll(a1, 64, 1), a3)
    c0 = jnp.where(even, b0, pltpu.roll(b1, 32, 1))
    c1 = jnp.where(even, pltpu.roll(b0, 96, 1), b1)
    c2 = jnp.where(even, b2, pltpu.roll(b3, 32, 1))
    c3 = jnp.where(even, pltpu.roll(b2, 96, 1), b3)
    return c0, c1, c2, c3


def stencil_kernel(core, tab, cot, left, right, top, bottom, field, g_out, mine_out, other_out, ext, band):
    ext[1:TD + 1, 0:R, :] = left[...].astype(F32)
    ext[1:TD + 1, R:R + FD, :] = cot[...].astype(F32)
    ext[1:TD + 1, R + FD:XW, :] = right[...].astype(F32)
    ext[0:1] = top[...].astype(F32)
    ext[TD + 1:TD + 2] = bottom[...].astype(F32)
    lane = lax.broadcasted_iota(jnp.int32, (FD, 256), 1)
    column = lane
    for edge in range(1, QUAD + 2):
        column = column - jnp.where(lane >= edge * XW, XW, 0)
    apart = (column - lax.broadcasted_iota(jnp.int32, (FD, 256), 0)).astype(F32)
    zero = jnp.zeros((FD, 256), F32)
    for quad in range(TD // QUAD):
        for r in range(QUAD):
            t = quad * QUAD + r
            sums = [zero] * K
            for s in range(S):
                hit = apart == tab[t, K * S + s:K * S + s + 1, :]
                for k in range(K):
                    sums[k] = sums[k] + jnp.where(hit, tab[t, k * S + s:k * S + s + 1, :], 0.0)
            for k in range(K):
                row = (k * QUAD + r) * FD
                band[row:row + FD, :] = sums[k]
        slab = ext[quad * QUAD:quad * QUAD + QUAD + 2].reshape((QUAD + 2) * XW, C).astype(BF16)
        weights = band[:, :(QUAD + 2) * XW].astype(BF16)
        got = jnp.dot(weights, slab, preferred_element_type=F32).astype(BF16)
        rows = QUAD * FD
        for k in range(K):
            g_out[quad * rows:(quad + 1) * rows, k * C:(k + 1) * C] = got[k * rows:(k + 1) * rows]
    mix = lax.dot_general(
        field[...], g_out[...], (((0,), (0,)), ((), ())), preferred_element_type=F32
    )
    mix = mix * (1.0 / math.sqrt(NLAT * NLON))
    first = core[0] == 0
    low, high = mix[:C // 2], mix[C // 2:]
    mine_out[...] = jnp.where(first, low, high)
    other_out[...] = jnp.where(first, high, low).astype(BF16)


def field_kernel(pos, g, cot, mix, pack, gf_out, send_out, flat, turned, send):
    total = cot[...].astype(F32)
    for k in range(K):
        total = total + lax.dot_general(
            g[:, k * C:(k + 1) * C], mix[k], (((1,), (1,)), ((), ())), preferred_element_type=F32
        )
    rounded = total.astype(BF16)
    gf_out[...] = rounded
    rounded = rounded.astype(F32)
    southern = pos[0] >= LATS // 2
    for t in range(TD):
        row = pl.multiple_of(jnp.where(southern, TD - 1 - t, t) * FD, FD)
        for h in range(C // 128):
            flat[h, pl.ds(row, FD), :] = rounded[t * FD:(t + 1) * FD, h * 128:(h + 1) * 128]
    pad = jnp.zeros((TP - TD, 128), F32)
    for fq in range(FD // 4):
        for h in range(C // 128):
            pieces = []
            for fr in range(4):
                pieces.append(flat[h, pl.ds(fq * 4 + fr, TD, stride=FD), :])
                pieces.append(pad)
            turned[fq, h * 128:(h + 1) * 128, :] = jnp.concatenate(pieces, axis=0).T
    for fq in range(FD // 4):
        for q in range(CD // 4):
            parts = [
                turned[fq, pl.ds(q * 4 + cr, LONS, stride=CD), :] for cr in range(4)
            ]
            for fr, part in enumerate(swap_blocks(parts)):
                send[q, pl.ds(fq * 4 + fr, LONS, stride=FD), :] = part
    padded = jnp.concatenate([send[q] for q in range(CD // 4)], axis=1).astype(BF16)
    packed = jnp.dot(padded, pack[...], preferred_element_type=F32)
    for q in range(GROUPS):
        send_out[:, q * FP:q * FP + FD, :] = packed[:, q * 128:(q + 1) * 128].reshape(LONS, FD, 128).astype(BF16)
    last = packed[:, GROUPS * 128:].reshape(LONS, FD // 8, 8, 128)
    rest = last[:, 0]
    for b in range(1, FD // 8):
        rest = rest + pltpu.roll(last[:, b], b * REST, 2)
    send_out[:, REST_ROW - 8:, :] = jnp.concatenate([jnp.zeros_like(rest), rest], axis=1).astype(BF16)


def slot_row(slot):
    return slot * FP + FD if slot < GROUPS else GROUPS * FP + (slot - GROUPS) * 8


def piece_row(piece):
    return TAIL_ROW + piece * 8


def dft_kernel(rows, columns, out):
    parts = [columns[:, q * FP:(q + 1) * FP, :].reshape(LONS * FP, 128) for q in range(GROUPS)]
    rest = columns[:, REST_ROW - 8:, :].astype(F32)[:, 8:]
    blocks = [rest if b == 0 else pltpu.roll(rest, 128 - b * REST, 2) for b in range(FD // 8)]
    blocks.append(jnp.zeros_like(rest))
    parts.append(jnp.concatenate(blocks, axis=1).reshape(LONS * FP, 128).astype(BF16))
    got = jnp.dot(rows[...], jnp.concatenate(parts, axis=1), preferred_element_type=F32)
    got = got * (1.0 / math.sqrt(NLON))
    pieces = []
    for half in range(2):
        for slot in range(SLOTS):
            first = slot_row(slot) // 16 * 16
            start = slot_row(slot) - first
            total = columns[half, first:first + 16, :].astype(F32)
            for chip in range(1, CHIPS):
                total = total + columns[2 * chip + half, first:first + 16, :].astype(F32)
            pieces.append(total[start:start + 8])
    step = 2 * MD * REST // 128
    inside = lax.broadcasted_iota(jnp.int32, (step, 128), 1) < REST
    for i in range(LATS):
        mine = got[i * 2 * MD:(i + 1) * 2 * MD]
        for q in range(GROUPS):
            out[i, q * 2 * MD:(q + 1) * 2 * MD, :] = mine[:, q * 128:(q + 1) * 128].astype(BF16)
        quarters = [
            jnp.where(inside, mine[b * step:(b + 1) * step, GROUPS * 128:], 0.0) for b in range(128 // REST)
        ]
        rest = quarters[0]
        for b in range(1, 128 // REST):
            rest = rest + pltpu.roll(quarters[b], b * REST, 1)
        out[i, GROUPS * 2 * MD:, :] = jnp.concatenate([rest] + pieces, axis=0).astype(BF16)


HALF = LATS // 2 * TP


def legendre_kernel(pos, cosines, logscale, out, coef, prev_s, early_s, scale_s, rows):
    block = pl.program_id(0)
    order = pos[0] * MD + lax.broadcasted_iota(jnp.int32, (MD, 128), 0)
    order_f = order.astype(F32)

    @pl.when(block == 0)
    def _():
        prev_s[...] = jnp.zeros_like(prev_s)
        early_s[...] = jnp.zeros_like(early_s)
        scale_s[...] = logscale[...]

    lane = lax.broadcasted_iota(jnp.int32, (MD, 128), 1)
    degree = block * LB + (lane & (LB - 1))
    deg_f = degree.astype(F32)
    higher = degree > order
    lower_a = jnp.where(higher, deg_f * deg_f - order_f * order_f, 1.0)
    factor_a = jnp.where(higher, jnp.sqrt((4.0 * deg_f * deg_f - 1.0) / lower_a), 0.0)
    before = deg_f - 1.0
    upper_b = jnp.maximum(before * before - order_f * order_f, 0.0)
    lower_b = jnp.maximum(4.0 * before * before - 1.0, 1.0)
    factor_b = jnp.sqrt(upper_b / lower_b)
    coef[...] = jnp.where(lane < LB, factor_a, factor_b)

    x = jnp.broadcast_to(cosines[...], (MD, 128))
    prev = prev_s[...]
    early = early_s[...]
    factor = jnp.exp(scale_s[...])
    for step in range(LB):
        a = jnp.broadcast_to(coef[:, step:step + 1], (MD, 128))
        b = jnp.broadcast_to(coef[:, LB + step:LB + step + 1], (MD, 128))
        seed = jnp.where(order == block * LB + step, 1.0, 0.0)
        fresh = a * (x * prev - b * early) + seed
        rows[step * MD:(step + 1) * MD, :] = fresh * factor
        early, prev = prev, fresh
    biggest = jnp.maximum(jnp.abs(prev), jnp.abs(early))
    divisor = jnp.where(biggest > 0.0, biggest, 1.0)
    prev_s[...] = prev / divisor
    early_s[...] = early / divisor
    scale_s[...] = scale_s[...] + jnp.log(divisor)
    for m in range(MD):
        side = (m % 2) * 128
        out[m // 2, :, side:side + 128] = rows[pl.ds(m, LB, stride=MD), :].astype(BF16)


MSTEP = 8


def synthesis_kernel(spec, pack, leg, out, lined, rows):
    step = pl.program_id(0)

    @pl.when(step == 0)
    def _():
        packed = []
        for i in range(LATS):
            groups = [spec[i, q * 2 * MD:(q + 1) * 2 * MD, :] for q in range(GROUPS)]
            rest = spec[i, GROUPS * 2 * MD:GROUPS * 2 * MD + 32, :].astype(F32)[:2 * MD * REST // 128]
            blocks = [rest if b == 0 else pltpu.roll(rest, 128 - b * REST, 1) for b in range(128 // REST)]
            groups.append(jnp.concatenate(blocks, axis=0).astype(BF16))
            packed.append(jnp.concatenate(groups, axis=1))
        padded = lax.dot_general(
            jnp.concatenate(packed, axis=0), pack[...], (((1,), (1,)), ((), ())), preferred_element_type=F32
        )
        padded = [padded[i * 2 * MD:(i + 1) * 2 * MD] for i in range(LATS)]
        for q in range(CD // 4):
            span = slice(q * 128, (q + 1) * 128)
            north = [padded[i][:, span] for i in range(LATS // 2)]
            south = [padded[LATS - 1 - i][:, span] for i in range(LATS // 2)]
            for odd in range(2):
                parts = [n - s if odd else n + s for n, s in zip(north, south)]
                for cr, part in enumerate(swap_blocks(parts)):
                    for p in range(2):
                        base = ((odd * 2 + p) * CD + q * 4 + cr) * MD
                        lined[base:base + MD, :] = part[p * MD:(p + 1) * MD]

    wide = 2 * CD
    odd_lane = (lax.broadcasted_iota(jnp.int32, (wide, L), 1) & 1) == 1
    zero = jnp.zeros((2 * wide, HALF), F32)
    for pair in range(MSTEP // 2):
        first = step * MSTEP + 2 * pair
        mine = [lined[pl.ds(first + side, 2 * wide, stride=MD), :] for side in range(2)]
        lhs = jnp.concatenate(
            [jnp.concatenate([mine[0], zero], axis=1), jnp.concatenate([zero, mine[1]], axis=1)], axis=0
        ).astype(BF16)
        got = lax.dot_general(
            lhs, leg[pair], (((1,), (1,)), ((), ())), preferred_element_type=F32
        ) * math.sqrt(4.0 * math.pi / NLAT)
        done = [
            jnp.where(odd_lane, got[wide:2 * wide], got[:wide]),
            jnp.where(odd_lane, got[2 * wide:3 * wide], got[3 * wide:]),
        ]
        for side in range(2):
            for h in range(L // 128):
                rows[h, pl.ds(2 * pair + side, wide, stride=MSTEP), :] = done[side][:, h * 128:(h + 1) * 128]
    for p in range(2):
        for c in range(CD):
            base = (p * CD + c) * MSTEP
            for h in range(L // 128):
                out[p, c, :, h * 128:(h + 1) * 128] = rows[h, base:base + MSTEP, :]


HALF_TILES = C // 32 * (K * C // 128)


def tiles_of(chip):
    return [(slot, *divmod(SLOTS * chip + slot, K * C // 128)) for slot in range(SLOTS) if SLOTS * chip + slot < HALF_TILES]


def chip_sum_kernel(mine, other, send, out, near_rows, far_rows, sems):
    total = (mine[...] + other[...].astype(F32)).astype(BF16)
    near_rows[...] = jnp.zeros_like(near_rows)
    far_rows[...] = jnp.zeros_like(far_rows)
    for chip in range(CHIPS):
        for slot, row, col in tiles_of(chip):
            for core in range(2):
                first = core * (C // 4) + row * 8
                tile = total[first:first + 8, col * 128:(col + 1) * 128]
                if slot < GROUPS:
                    near_rows[slot, 2 * chip + core] = tile
                else:
                    far = (slot - GROUPS) * 8
                    far_rows[2 * chip + core, far:far + 8, :] = tile
    copies = [
        pltpu.make_async_copy(near_rows.at[q], out.at[:, q * FP + FD:(q + 1) * FP, :], sems.at[q]) for q in range(GROUPS)
    ]
    copies.append(pltpu.make_async_copy(far_rows, out.at[:, GROUPS * FP:REST_ROW, :], sems.at[GROUPS]))
    for copy in copies:
        copy.start()
    for copy in copies:
        copy.wait()


def copies_kernel(spec, out):
    for piece in range(2 * SLOTS):
        row = piece_row(piece)
        first = row // 16 * 16
        total = spec[0, first:first + 16, :].astype(F32)
        for i in range(1, LATS):
            total = total + spec[i, first:first + 16, :].astype(F32)
        total = total[row - first:row - first + 8].astype(BF16)
        for chip in range(CHIPS):
            out[chip, piece * 8:(piece + 1) * 8, :] = total


def mix_kernel(core, mine, other, out, rows, sems):
    copies = []
    for half in range(2):
        for parts, held in ((mine, core[0]), (other, 1 - core[0])):
            base = pl.multiple_of(half * (C // 2) + held * (C // 4), 8)
            for chip in range(CHIPS):
                for slot, row, col in tiles_of(chip):
                    k, d = divmod(col, C // 128)
                    piece = (half * SLOTS + slot) * 8
                    rows[k, pl.ds(base + row * 8, 8), d * 128:(d + 1) * 128] = parts[
                        chip, piece:piece + 8, :
                    ].astype(F32)
        span = pl.ds(half * (C // 2), C // 2)
        copies.append(pltpu.make_async_copy(rows.at[:, span], out.at[:, span], sems.at[half]))
        copies[-1].start()
    for copy in copies:
        copy.wait()


def dft_rows():
    order = np.arange(M).reshape(LATS, 1, MD)
    order = np.broadcast_to(order, (LATS, 2, MD)).reshape(-1)
    part = np.broadcast_to(np.arange(2).reshape(1, 2, 1), (LATS, 2, MD)).reshape(-1)
    angle = 2.0 * np.pi / NLON * ((order[:, None] * np.arange(NLON)[None, :]) % NLON)
    angle = angle.astype(np.float32)
    rows = np.where(part[:, None] == 0, np.cos(angle), -np.sin(angle))
    padded = np.zeros((2 * M, LONS, FP), np.float32)
    padded[:, :, :FD] = rows.reshape(2 * M, LONS, FD)
    return padded.reshape(2 * M, LONS * FP).astype(ml_dtypes.bfloat16)


def packing():
    pack = np.zeros((CD * TP, CD * TP), np.float32)
    for c in range(CD):
        for t in range(TD):
            pack[c * TP + t, c * TD + t] = 1.0
    return pack.astype(ml_dtypes.bfloat16)


def latitudes():
    angle = ((np.arange(NLAT) + 0.5) * (np.pi / NLAT)).reshape(LATS, TD)
    cosine = np.zeros((LATS, TP), np.float32)
    logsine = np.zeros((LATS, TP), np.float32)
    cosine[:, :TD] = np.cos(angle)
    logsine[:, :TD] = np.log(np.sin(angle))
    half = LATS // 2
    return cosine[:half].reshape(1, -1), logsine[:half].reshape(1, -1)


def seed_logs():
    degree = np.arange(M, dtype=np.float64)
    steps = np.log((2.0 * degree + 1.0) / (2.0 * degree + 2.0))
    prefix = np.concatenate([np.zeros(1), np.cumsum(steps)[:-1]])
    return (0.5 * np.log((2.0 * degree + 1.0) / (4.0 * np.pi)) + 0.5 * prefix).astype(np.float32)


def band_lanes():
    mark = np.zeros((TD, 3, 256), np.float32)
    for t in range(TD):
        for rr in range(3):
            start = (t % QUAD + rr) * XW
            mark[t, rr, start:start + XW] = 1.0
    return mark


def tap_table(taps, offsets, counts, first_row):
    slot_ids = lax.broadcasted_iota(jnp.int32, taps.shape, 3)
    live = jnp.where(slot_ids < counts[:, None, None, None], taps, 0.0).astype(BF16).astype(F32)
    shift = (R - offsets).astype(F32)[:, None]
    both = jnp.concatenate([live, shift], axis=1)
    both = jnp.pad(both, ((1, 1), (0, 0), (0, 0), (0, 0)))
    both = lax.dynamic_slice_in_dim(both, first_row, TD + 2, 0)
    marks = band_lanes()
    table = 0.0
    for rr in range(3):
        mine = both[rr:rr + TD, :, 2 - rr, :].reshape(TD, (K + 1) * S)
        table = table + mine[:, :, None] * marks[:, rr][:, None, :]
    return table


def on_device(field, cotangent, mix_weight, taps, offsets, counts):
    lat_pos = lax.axis_index(LAT)
    up = [(i, (i + 1) % LONS) for i in range(LONS)]
    down = [(j, i) for i, j in up]
    left = lax.ppermute(cotangent[:, FD - R:], LON, up)
    right = lax.ppermute(cotangent[:, :R], LON, down)
    edge_rows = [
        jnp.concatenate([left[t:t + 1], cotangent[t:t + 1], right[t:t + 1]], axis=1) for t in (0, TD - 1)
    ]
    north = [(i, i + 1) for i in range(LATS - 1)]
    south = [(j, i) for i, j in north]
    top = lax.ppermute(edge_rows[1], LAT, north)
    bottom = lax.ppermute(edge_rows[0], LAT, south)

    whole = pl.BlockSpec(memory_space=pltpu.VMEM)
    taps, offsets, counts, _ = lax.optimization_barrier((taps, offsets, counts, edge_rows))
    tab = tap_table(taps, offsets, counts, lat_pos * TD)
    cells = TD * FD
    core = jnp.reshape(lax.axis_index(CORE), (1,)).astype(jnp.int32)
    scalar = pl.BlockSpec(memory_space=pltpu.SMEM)
    anywhere = pl.BlockSpec(memory_space=pl.ANY)
    half = (C // 2, K * C)
    grown, mix_mine, mix_other = call(
        stencil_kernel,
        (near_shape((cells, K * C), BF16), near_shape(half, F32), near_shape(half, BF16)),
        5,
        in_specs=[scalar] + [whole] * 7,
        scratch_shapes=[pltpu.VMEM((TD + 2, XW, C), F32), pltpu.VMEM((K * QUAD * FD, 256), F32)],
        name="stencil",
    )(core, near(tab), near(cotangent), near(left), near(right), near(top), near(bottom), near(field.reshape(cells, C)))
    swap = [(0, 1), (1, 0)]
    mix_other = lax.ppermute(mix_other, CORE, swap)

    pos = jnp.reshape(lat_pos, (1,)).astype(jnp.int32)
    pack = jnp.asarray(packing())
    grad_field, send = call(
        field_kernel,
        (shape((cells, C), BF16), shape((LONS, SENT, 128), BF16)),
        5,
        in_specs=[scalar, whole, whole, whole, whole],
        scratch_shapes=[
            pltpu.VMEM((C // 128, cells, 128), F32),
            pltpu.VMEM((FD // 4, C, 128), F32),
            pltpu.VMEM((CD // 4, LONS * FD, 128), F32),
        ],
        name="grad_field",
    )(pos, near(grown), near(cotangent.reshape(cells, C)), near(mix_weight), near(pack))
    send = call(
        chip_sum_kernel,
        shape((LONS, SENT, 128), BF16),
        2,
        in_specs=[whole, whole, anywhere],
        out_specs=anywhere,
        scratch_shapes=[
            pltpu.VMEM((GROUPS, LONS, FP - FD, 128), BF16),
            pltpu.VMEM((LONS, REST_ROW - GROUPS * FP, 128), BF16),
            pltpu.SemaphoreType.DMA((GROUPS + 1,)),
        ],
        input_output_aliases={2: 0},
        name="mix_chip_sum",
    )(near(mix_mine), near(mix_other), send)
    columns = lax.all_to_all(send, LON, 0, 0, tiled=True)

    cosine, logsine = latitudes()
    first_order = lat_pos * MD
    seeds = lax.dynamic_slice_in_dim(jnp.asarray(seed_logs()), first_order, MD, 0)
    orders = (first_order + jnp.arange(MD, dtype=jnp.int32)).astype(F32)
    logscale = seeds[:, None] + orders[:, None] * logsine
    logscale, _ = lax.optimization_barrier((logscale, send))
    table = call(
        legendre_kernel,
        shape((MD // 2, L, 2 * HALF), BF16),
        9,
        grid_spec=pltpu.PrefetchScalarGridSpec(
            num_scalar_prefetch=1,
            grid=(L // LB,),
            in_specs=[
                pl.BlockSpec((1, HALF), lambda b, pos: (0, 0)),
                pl.BlockSpec((MD, HALF), lambda b, pos: (0, 0)),
            ],
            out_specs=pl.BlockSpec((MD // 2, LB, 2 * HALF), lambda b, pos: (0, b, 0)),
            scratch_shapes=[
                pltpu.VMEM((MD, 128), F32),
                pltpu.VMEM((MD, HALF), F32),
                pltpu.VMEM((MD, HALF), F32),
                pltpu.VMEM((MD, HALF), F32),
                pltpu.VMEM((LB * MD, HALF), F32),
            ],
        ),
        name="legendre",
    )(pos, jnp.asarray(cosine), logscale)
    columns, table = lax.optimization_barrier((columns, table))

    spectra = call(dft_kernel, near_shape((LATS, SPREAD, 128), BF16), 2, in_specs=[whole, whole], name="dft")(
        near(jnp.asarray(dft_rows())), near(columns)
    )
    spec = lax.all_to_all(spectra, LAT, 0, 0, tiled=True)
    mix_copies = call(copies_kernel, near_shape((CHIPS, 2 * SLOTS * 8, 128), BF16), 2, in_specs=[whole], name="mix_copies")(near(spec))
    mix_mine = lax.all_to_all(mix_copies, CHIP, 0, 0, tiled=True)

    grad_spectra = call(
        synthesis_kernel,
        shape((2, CD, MD, L), F32),
        6,
        grid_spec=pltpu.PrefetchScalarGridSpec(
            num_scalar_prefetch=0,
            grid=(MD // MSTEP,),
            in_specs=[
                whole,
                whole,
                pl.BlockSpec((MSTEP // 2, L, 2 * HALF), lambda b: (b, 0, 0)),
            ],
            out_specs=pl.BlockSpec((2, CD, MSTEP, L), lambda b: (0, 0, b, 0)),
            scratch_shapes=[
                pltpu.VMEM((4 * CD * MD, HALF), F32),
                pltpu.VMEM((L // 128, 2 * CD * MSTEP, 128), F32),
            ],
        ),
        name="synthesis",
    )(near(spec), near(pack), table)
    mix_mine, grad_spectra = lax.optimization_barrier((mix_mine, grad_spectra))
    mix_other = lax.ppermute(mix_mine, CORE, swap)
    grad_mix = call(
        mix_kernel,
        shape((K, C, C), F32),
        2,
        in_specs=[scalar, whole, whole],
        out_specs=anywhere,
        scratch_shapes=[pltpu.VMEM((K, C, C), F32), pltpu.SemaphoreType.DMA((2,))],
        name="mix_out",
    )(core, near(mix_mine), near(mix_other))
    return (grad_field.reshape(TD, FD, C), jnp.transpose(grad_spectra, (0, 2, 1, 3)), grad_mix)


def solution(mesh):
    chips = Mesh(mesh.devices.reshape(LATS, CHIPS, 2), (LAT, CHIP, CORE))
    placed = (P(LAT, LON, None), P(LAT, LON, None), P(), P(), P(), P())
    return jax.shard_map(
        on_device,
        mesh=chips,
        in_specs=placed,
        out_specs=(P(LAT, LON, None), P(None, LAT, LON, None), P()),
        check_vma=False,
    )
```

```python
import functools
import math

import jax
import jax.numpy as jnp
import ml_dtypes
import numpy as np
from jax import lax
from jax.experimental import pallas as pl
from jax.experimental.pallas import tpu as pltpu
from jax.sharding import Mesh, PartitionSpec as P

C = 384
M = 384
L = 384
K = 3
R = 8
S = 8
LB = 32
NLAT = 192
NLON = 768
LATS = 8
LONS = 32
TD = NLAT // LATS
FD = NLON // LONS
CD = C // LONS
MD = M // LATS
XW = FD + 2 * R
TP = 32
FP = FD + 8
COLS = CD * TD
GROUPS = COLS // 128
REST = COLS - GROUPS * 128
SLOTS = 7
REST_ROW = GROUPS * FP + (SLOTS - GROUPS) * 8
SENT = REST_ROW + 8
TAIL_ROW = GROUPS * 2 * MD + 2 * MD * REST // 128
SPREAD = TAIL_ROW + 2 * SLOTS * 8
QUAD = 4
CHIPS = LONS // 2
LAT = "lat"
CHIP = "chip"
CORE = "core"
LON = (CHIP, CORE)
F32 = jnp.float32
BF16 = jnp.bfloat16
VMEM_BYTES = 18 * 1024 * 1024


def call(kernel, out_shape, us, **kw):
    return pl.pallas_call(
        kernel,
        out_shape=out_shape,
        cost_estimate=pl.CostEstimate(flops=int(us * 1.1e9), bytes_accessed=int(us * 3.0e6), transcendentals=0),
        compiler_params=pltpu.CompilerParams(vmem_limit_bytes=VMEM_BYTES),
        **kw,
    )


def near(array):
    return pltpu.with_memory_space_constraint(array, pltpu.VMEM)


def shape(dims, dtype):
    return jax.ShapeDtypeStruct(dims, dtype)


def near_shape(dims, dtype):
    return pltpu.VMEM(dims, dtype)


def swap_blocks(parts):
    lane = lax.broadcasted_iota(jnp.int32, parts[0].shape, 1)
    low = lane < 64
    even = (lane & 32) == 0
    a0, a1, a2, a3 = parts
    b0 = jnp.where(low, a0, pltpu.roll(a2, 64, 1))
    b2 = jnp.where(low, pltpu.roll(a0, 64, 1), a2)
    b1 = jnp.where(low, a1, pltpu.roll(a3, 64, 1))
    b3 = jnp.where(low, pltpu.roll(a1, 64, 1), a3)
    c0 = jnp.where(even, b0, pltpu.roll(b1, 32, 1))
    c1 = jnp.where(even, pltpu.roll(b0, 96, 1), b1)
    c2 = jnp.where(even, b2, pltpu.roll(b3, 32, 1))
    c3 = jnp.where(even, pltpu.roll(b2, 96, 1), b3)
    return c0, c1, c2, c3


ROWS = QUAD * FD
INNER = TD // QUAD - 2


def widen(ext, rows, cot, left, right):
    there = slice(rows.start + 1, rows.stop + 1)
    ext[there, 0:R, :] = left[rows].astype(F32)
    ext[there, R:R + FD, :] = cot[rows].astype(F32)
    ext[there, R + FD:XW, :] = right[rows].astype(F32)


def offsets_in_band():
    lane = lax.broadcasted_iota(jnp.int32, (FD, 256), 1)
    column = lane
    for edge in range(1, QUAD + 2):
        column = column - jnp.where(lane >= edge * XW, XW, 0)
    return (column - lax.broadcasted_iota(jnp.int32, (FD, 256), 0)).astype(F32)


def stencil_quad(quad, apart, tab, ext, band):
    zero = jnp.zeros((FD, 256), F32)
    for r in range(QUAD):
        t = quad * QUAD + r
        sums = [zero] * K
        for s in range(S):
            hit = apart == tab[t, K * S + s:K * S + s + 1, :]
            for k in range(K):
                sums[k] = sums[k] + jnp.where(hit, tab[t, k * S + s:k * S + s + 1, :], 0.0)
        for k in range(K):
            row = (k * QUAD + r) * FD
            band[row:row + FD, :] = sums[k]
    slab = ext[quad * QUAD:quad * QUAD + QUAD + 2].reshape((QUAD + 2) * XW, C).astype(BF16)
    weights = band[:, :(QUAD + 2) * XW].astype(BF16)
    return jnp.dot(weights, slab, preferred_element_type=F32).astype(BF16)


def cells_dot(field, g):
    return lax.dot_general(field, g, (((0,), (0,)), ((), ())), preferred_element_type=F32)


def inner_kernel(tab, cot, left, right, field, g_out, mix_out, ext, band):
    widen(ext, slice(QUAD - 1, TD - QUAD + 1), cot, left, right)
    apart = offsets_in_band()
    for n in range(INNER):
        got = stencil_quad(n + 1, apart, tab, ext, band)
        for k in range(K):
            g_out[n * ROWS:(n + 1) * ROWS, k * C:(k + 1) * C] = got[k * ROWS:(k + 1) * ROWS]
    mix_out[...] = cells_dot(field[ROWS:(INNER + 1) * ROWS, :], g_out[...])


def outer_kernel(core, tab, cot, left, right, top, bottom, field, mix_inner, g_out, mine_out, other_out, ext, band):
    widen(ext, slice(0, QUAD + 1), cot, left, right)
    widen(ext, slice(TD - QUAD - 1, TD), cot, left, right)
    ext[0:1] = top[...].astype(F32)
    ext[TD + 1:TD + 2] = bottom[...].astype(F32)
    apart = offsets_in_band()
    for n in range(2):
        got = stencil_quad(n * (INNER + 1), apart, tab, ext, band)
        for k in range(K):
            g_out[n * ROWS:(n + 1) * ROWS, k * C:(k + 1) * C] = got[k * ROWS:(k + 1) * ROWS]
    mine = jnp.concatenate([field[:ROWS, :], field[(INNER + 1) * ROWS:, :]], axis=0)
    mix = (mix_inner[...] + cells_dot(mine, g_out[...])) * (1.0 / math.sqrt(NLAT * NLON))
    first = core[0] == 0
    low, high = mix[:C // 2], mix[C // 2:]
    mine_out[...] = jnp.where(first, low, high)
    other_out[...] = jnp.where(first, high, low).astype(BF16)


def field_kernel(pos, g_inner, g_outer, cot, mix, pack, gf_out, send_out, flat, turned, send):
    inner = jnp.zeros((INNER * ROWS, C), F32)
    outer = jnp.zeros((2 * ROWS, C), F32)
    for k in range(K):
        span = slice(k * C, (k + 1) * C)
        inner = inner + lax.dot_general(
            g_inner[:, span], mix[k], (((1,), (1,)), ((), ())), preferred_element_type=F32
        )
        outer = outer + lax.dot_general(
            g_outer[:, span], mix[k], (((1,), (1,)), ((), ())), preferred_element_type=F32
        )
    total = cot[...].astype(F32) + jnp.concatenate([outer[:ROWS], inner, outer[ROWS:]], axis=0)
    rounded = total.astype(BF16)
    gf_out[...] = rounded
    rounded = rounded.astype(F32)
    southern = pos[0] >= LATS // 2
    for t in range(TD):
        row = pl.multiple_of(jnp.where(southern, TD - 1 - t, t) * FD, FD)
        for h in range(C // 128):
            flat[h, pl.ds(row, FD), :] = rounded[t * FD:(t + 1) * FD, h * 128:(h + 1) * 128]
    pad = jnp.zeros((TP - TD, 128), F32)
    for fq in range(FD // 4):
        for h in range(C // 128):
            pieces = []
            for fr in range(4):
                pieces.append(flat[h, pl.ds(fq * 4 + fr, TD, stride=FD), :])
                pieces.append(pad)
            turned[fq, h * 128:(h + 1) * 128, :] = jnp.concatenate(pieces, axis=0).T
    for fq in range(FD // 4):
        for q in range(CD // 4):
            parts = [
                turned[fq, pl.ds(q * 4 + cr, LONS, stride=CD), :] for cr in range(4)
            ]
            for fr, part in enumerate(swap_blocks(parts)):
                send[q, pl.ds(fq * 4 + fr, LONS, stride=FD), :] = part
    padded = jnp.concatenate([send[q] for q in range(CD // 4)], axis=1).astype(BF16)
    packed = jnp.dot(padded, pack[...], preferred_element_type=F32)
    for q in range(GROUPS):
        send_out[:, q * FP:q * FP + FD, :] = packed[:, q * 128:(q + 1) * 128].reshape(LONS, FD, 128).astype(BF16)
    last = packed[:, GROUPS * 128:].reshape(LONS, FD // 8, 8, 128)
    rest = last[:, 0]
    for b in range(1, FD // 8):
        rest = rest + pltpu.roll(last[:, b], b * REST, 2)
    send_out[:, REST_ROW - 8:, :] = jnp.concatenate([jnp.zeros_like(rest), rest], axis=1).astype(BF16)


def slot_row(slot):
    return slot * FP + FD if slot < GROUPS else GROUPS * FP + (slot - GROUPS) * 8


def piece_row(piece):
    return TAIL_ROW + piece * 8


def dft_kernel(rows, columns, out):
    parts = [columns[:, q * FP:(q + 1) * FP, :].reshape(LONS * FP, 128) for q in range(GROUPS)]
    rest = columns[:, REST_ROW - 8:, :].astype(F32)[:, 8:]
    blocks = [rest if b == 0 else pltpu.roll(rest, 128 - b * REST, 2) for b in range(FD // 8)]
    blocks.append(jnp.zeros_like(rest))
    parts.append(jnp.concatenate(blocks, axis=1).reshape(LONS * FP, 128).astype(BF16))
    got = jnp.dot(rows[...], jnp.concatenate(parts, axis=1), preferred_element_type=F32)
    got = got * (1.0 / math.sqrt(NLON))
    pieces = []
    for half in range(2):
        for slot in range(SLOTS):
            first = slot_row(slot) // 16 * 16
            start = slot_row(slot) - first
            total = columns[half, first:first + 16, :].astype(F32)
            for chip in range(1, CHIPS):
                total = total + columns[2 * chip + half, first:first + 16, :].astype(F32)
            pieces.append(total[start:start + 8])
    step = 2 * MD * REST // 128
    inside = lax.broadcasted_iota(jnp.int32, (step, 128), 1) < REST
    for i in range(LATS):
        mine = got[i * 2 * MD:(i + 1) * 2 * MD]
        for q in range(GROUPS):
            out[i, q * 2 * MD:(q + 1) * 2 * MD, :] = mine[:, q * 128:(q + 1) * 128].astype(BF16)
        quarters = [
            jnp.where(inside, mine[b * step:(b + 1) * step, GROUPS * 128:], 0.0) for b in range(128 // REST)
        ]
        rest = quarters[0]
        for b in range(1, 128 // REST):
            rest = rest + pltpu.roll(quarters[b], b * REST, 1)
        out[i, GROUPS * 2 * MD:, :] = jnp.concatenate([rest] + pieces, axis=0).astype(BF16)


HALF = LATS // 2 * TP


def legendre_kernel(pos, cosines, logscale, out, coef, prev_s, early_s, scale_s, rows):
    block = pl.program_id(0)
    order = pos[0] * MD + lax.broadcasted_iota(jnp.int32, (MD, 128), 0)
    order_f = order.astype(F32)

    @pl.when(block == 0)
    def _():
        prev_s[...] = jnp.zeros_like(prev_s)
        early_s[...] = jnp.zeros_like(early_s)
        scale_s[...] = logscale[...]

    lane = lax.broadcasted_iota(jnp.int32, (MD, 128), 1)
    degree = block * LB + (lane & (LB - 1))
    deg_f = degree.astype(F32)
    higher = degree > order
    lower_a = jnp.where(higher, deg_f * deg_f - order_f * order_f, 1.0)
    factor_a = jnp.where(higher, jnp.sqrt((4.0 * deg_f * deg_f - 1.0) / lower_a), 0.0)
    before = deg_f - 1.0
    upper_b = jnp.maximum(before * before - order_f * order_f, 0.0)
    lower_b = jnp.maximum(4.0 * before * before - 1.0, 1.0)
    factor_b = jnp.sqrt(upper_b / lower_b)
    coef[...] = jnp.where(lane < LB, factor_a, factor_b)

    x = jnp.broadcast_to(cosines[...], (MD, 128))
    prev = prev_s[...]
    early = early_s[...]
    factor = jnp.exp(scale_s[...])
    for step in range(LB):
        a = jnp.broadcast_to(coef[:, step:step + 1], (MD, 128))
        b = jnp.broadcast_to(coef[:, LB + step:LB + step + 1], (MD, 128))
        seed = jnp.where(order == block * LB + step, 1.0, 0.0)
        fresh = a * (x * prev - b * early) + seed
        rows[step * MD:(step + 1) * MD, :] = fresh * factor
        early, prev = prev, fresh
    biggest = jnp.maximum(jnp.abs(prev), jnp.abs(early))
    divisor = jnp.where(biggest > 0.0, biggest, 1.0)
    prev_s[...] = prev / divisor
    early_s[...] = early / divisor
    scale_s[...] = scale_s[...] + jnp.log(divisor)
    for m in range(MD):
        side = (m % 2) * 128
        out[m // 2, :, side:side + 128] = rows[pl.ds(m, LB, stride=MD), :].astype(BF16)


MSTEP = 8


def synthesis_kernel(spec, pack, leg, out, lined, rows):
    step = pl.program_id(0)

    @pl.when(step == 0)
    def _():
        packed = []
        for i in range(LATS):
            groups = [spec[i, q * 2 * MD:(q + 1) * 2 * MD, :] for q in range(GROUPS)]
            rest = spec[i, GROUPS * 2 * MD:GROUPS * 2 * MD + 32, :].astype(F32)[:2 * MD * REST // 128]
            blocks = [rest if b == 0 else pltpu.roll(rest, 128 - b * REST, 1) for b in range(128 // REST)]
            groups.append(jnp.concatenate(blocks, axis=0).astype(BF16))
            packed.append(jnp.concatenate(groups, axis=1))
        padded = lax.dot_general(
            jnp.concatenate(packed, axis=0), pack[...], (((1,), (1,)), ((), ())), preferred_element_type=F32
        )
        padded = [padded[i * 2 * MD:(i + 1) * 2 * MD] for i in range(LATS)]
        for q in range(CD // 4):
            span = slice(q * 128, (q + 1) * 128)
            north = [padded[i][:, span] for i in range(LATS // 2)]
            south = [padded[LATS - 1 - i][:, span] for i in range(LATS // 2)]
            for odd in range(2):
                parts = [n - s if odd else n + s for n, s in zip(north, south)]
                for cr, part in enumerate(swap_blocks(parts)):
                    for p in range(2):
                        base = ((odd * 2 + p) * CD + q * 4 + cr) * MD
                        lined[base:base + MD, :] = part[p * MD:(p + 1) * MD]

    wide = 2 * CD
    odd_lane = (lax.broadcasted_iota(jnp.int32, (wide, L), 1) & 1) == 1
    zero = jnp.zeros((2 * wide, HALF), F32)
    for pair in range(MSTEP // 2):
        first = step * MSTEP + 2 * pair
        mine = [lined[pl.ds(first + side, 2 * wide, stride=MD), :] for side in range(2)]
        lhs = jnp.concatenate(
            [jnp.concatenate([mine[0], zero], axis=1), jnp.concatenate([zero, mine[1]], axis=1)], axis=0
        ).astype(BF16)
        got = lax.dot_general(
            lhs, leg[pair], (((1,), (1,)), ((), ())), preferred_element_type=F32
        ) * math.sqrt(4.0 * math.pi / NLAT)
        done = [
            jnp.where(odd_lane, got[wide:2 * wide], got[:wide]),
            jnp.where(odd_lane, got[2 * wide:3 * wide], got[3 * wide:]),
        ]
        for side in range(2):
            for h in range(L // 128):
                rows[h, pl.ds(2 * pair + side, wide, stride=MSTEP), :] = done[side][:, h * 128:(h + 1) * 128]
    for p in range(2):
        for c in range(CD):
            base = (p * CD + c) * MSTEP
            for h in range(L // 128):
                out[p, c, :, h * 128:(h + 1) * 128] = rows[h, base:base + MSTEP, :]


HALF_TILES = C // 32 * (K * C // 128)


def tiles_of(chip):
    return [(slot, *divmod(SLOTS * chip + slot, K * C // 128)) for slot in range(SLOTS) if SLOTS * chip + slot < HALF_TILES]


def chip_sum_kernel(mine, other, send, out, near_rows, far_rows, sems):
    total = (mine[...] + other[...].astype(F32)).astype(BF16)
    near_rows[...] = jnp.zeros_like(near_rows)
    far_rows[...] = jnp.zeros_like(far_rows)
    for chip in range(CHIPS):
        for slot, row, col in tiles_of(chip):
            for core in range(2):
                first = core * (C // 4) + row * 8
                tile = total[first:first + 8, col * 128:(col + 1) * 128]
                if slot < GROUPS:
                    near_rows[slot, 2 * chip + core] = tile
                else:
                    far = (slot - GROUPS) * 8
                    far_rows[2 * chip + core, far:far + 8, :] = tile
    copies = [
        pltpu.make_async_copy(near_rows.at[q], out.at[:, q * FP + FD:(q + 1) * FP, :], sems.at[q]) for q in range(GROUPS)
    ]
    copies.append(pltpu.make_async_copy(far_rows, out.at[:, GROUPS * FP:REST_ROW, :], sems.at[GROUPS]))
    for copy in copies:
        copy.start()
    for copy in copies:
        copy.wait()


def copies_kernel(spec, out):
    for piece in range(2 * SLOTS):
        row = piece_row(piece)
        first = row // 16 * 16
        total = spec[0, first:first + 16, :].astype(F32)
        for i in range(1, LATS):
            total = total + spec[i, first:first + 16, :].astype(F32)
        total = total[row - first:row - first + 8].astype(BF16)
        for chip in range(CHIPS):
            out[chip, piece * 8:(piece + 1) * 8, :] = total


def mix_kernel(core, mine, other, out, rows, sems):
    copies = []
    for half in range(2):
        for parts, held in ((mine, core[0]), (other, 1 - core[0])):
            base = pl.multiple_of(half * (C // 2) + held * (C // 4), 8)
            for chip in range(CHIPS):
                for slot, row, col in tiles_of(chip):
                    k, d = divmod(col, C // 128)
                    piece = (half * SLOTS + slot) * 8
                    rows[k, pl.ds(base + row * 8, 8), d * 128:(d + 1) * 128] = parts[
                        chip, piece:piece + 8, :
                    ].astype(F32)
        span = pl.ds(half * (C // 2), C // 2)
        copies.append(pltpu.make_async_copy(rows.at[:, span], out.at[:, span], sems.at[half]))
        copies[-1].start()
    for copy in copies:
        copy.wait()


def dft_rows():
    order = np.arange(M).reshape(LATS, 1, MD)
    order = np.broadcast_to(order, (LATS, 2, MD)).reshape(-1)
    part = np.broadcast_to(np.arange(2).reshape(1, 2, 1), (LATS, 2, MD)).reshape(-1)
    angle = 2.0 * np.pi / NLON * ((order[:, None] * np.arange(NLON)[None, :]) % NLON)
    angle = angle.astype(np.float32)
    rows = np.where(part[:, None] == 0, np.cos(angle), -np.sin(angle))
    padded = np.zeros((2 * M, LONS, FP), np.float32)
    padded[:, :, :FD] = rows.reshape(2 * M, LONS, FD)
    return padded.reshape(2 * M, LONS * FP).astype(ml_dtypes.bfloat16)


def packing():
    pack = np.zeros((CD * TP, CD * TP), np.float32)
    for c in range(CD):
        for t in range(TD):
            pack[c * TP + t, c * TD + t] = 1.0
    return pack.astype(ml_dtypes.bfloat16)


def latitudes():
    angle = ((np.arange(NLAT) + 0.5) * (np.pi / NLAT)).reshape(LATS, TD)
    cosine = np.zeros((LATS, TP), np.float32)
    logsine = np.zeros((LATS, TP), np.float32)
    cosine[:, :TD] = np.cos(angle)
    logsine[:, :TD] = np.log(np.sin(angle))
    half = LATS // 2
    return cosine[:half].reshape(1, -1), logsine[:half].reshape(1, -1)


def seed_logs():
    degree = np.arange(M, dtype=np.float64)
    steps = np.log((2.0 * degree + 1.0) / (2.0 * degree + 2.0))
    prefix = np.concatenate([np.zeros(1), np.cumsum(steps)[:-1]])
    return (0.5 * np.log((2.0 * degree + 1.0) / (4.0 * np.pi)) + 0.5 * prefix).astype(np.float32)


def band_lanes():
    mark = np.zeros((TD, 3, 256), np.float32)
    for t in range(TD):
        for rr in range(3):
            start = (t % QUAD + rr) * XW
            mark[t, rr, start:start + XW] = 1.0
    return mark


def tap_table(taps, offsets, counts, first_row):
    slot_ids = lax.broadcasted_iota(jnp.int32, taps.shape, 3)
    live = jnp.where(slot_ids < counts[:, None, None, None], taps, 0.0).astype(BF16).astype(F32)
    shift = (R - offsets).astype(F32)[:, None]
    both = jnp.concatenate([live, shift], axis=1)
    both = jnp.pad(both, ((1, 1), (0, 0), (0, 0), (0, 0)))
    both = lax.dynamic_slice_in_dim(both, first_row, TD + 2, 0)
    marks = band_lanes()
    table = 0.0
    for rr in range(3):
        mine = both[rr:rr + TD, :, 2 - rr, :].reshape(TD, (K + 1) * S)
        table = table + mine[:, :, None] * marks[:, rr][:, None, :]
    return table


def on_device(field, cotangent, mix_weight, taps, offsets, counts):
    lat_pos = lax.axis_index(LAT)
    up = [(i, (i + 1) % LONS) for i in range(LONS)]
    down = [(j, i) for i, j in up]
    left = lax.ppermute(cotangent[:, FD - R:], LON, up)
    right = lax.ppermute(cotangent[:, :R], LON, down)
    edge_rows = [
        jnp.concatenate([left[t:t + 1], cotangent[t:t + 1], right[t:t + 1]], axis=1) for t in (0, TD - 1)
    ]
    north = [(i, i + 1) for i in range(LATS - 1)]
    south = [(j, i) for i, j in north]
    top = lax.ppermute(edge_rows[1], LAT, north)
    bottom = lax.ppermute(edge_rows[0], LAT, south)

    whole = pl.BlockSpec(memory_space=pltpu.VMEM)
    taps, offsets, counts, _ = lax.optimization_barrier((taps, offsets, counts, edge_rows))
    tab = tap_table(taps, offsets, counts, lat_pos * TD)
    cells = TD * FD
    core = jnp.reshape(lax.axis_index(CORE), (1,)).astype(jnp.int32)
    scalar = pl.BlockSpec(memory_space=pltpu.SMEM)
    anywhere = pl.BlockSpec(memory_space=pl.ANY)
    half = (C // 2, K * C)
    rims = (near(left), near(right))
    near_cot, near_field = near(cotangent), near(field.reshape(cells, C))
    scratch = [pltpu.VMEM((TD + 2, XW, C), F32), pltpu.VMEM((K * ROWS, 256), F32)]
    g_inner, mix_inner = call(
        inner_kernel,
        (near_shape((INNER * ROWS, K * C), BF16), near_shape((C, K * C), F32)),
        2,
        in_specs=[whole] * 5,
        scratch_shapes=scratch,
        name="stencil_inner",
    )(near(tab), near_cot, *rims, near_field)
    pack = near(jnp.asarray(packing()))
    mix_near = near(mix_weight)
    top, bottom, pack, mix_near = lax.optimization_barrier((top, bottom, pack, mix_near))
    g_outer, mix_mine, mix_other = call(
        outer_kernel,
        (near_shape((2 * ROWS, K * C), BF16), near_shape(half, F32), near_shape(half, BF16)),
        2,
        in_specs=[scalar] + [whole] * 8,
        scratch_shapes=scratch,
        name="stencil_outer",
    )(core, near(tab), near_cot, *rims, near(top), near(bottom), near_field, near(mix_inner))
    swap = [(0, 1), (1, 0)]
    mix_other = lax.ppermute(mix_other, CORE, swap)

    pos = jnp.reshape(lat_pos, (1,)).astype(jnp.int32)
    grad_field, send = call(
        field_kernel,
        (shape((cells, C), BF16), shape((LONS, SENT, 128), BF16)),
        5,
        in_specs=[scalar] + [whole] * 5,
        scratch_shapes=[
            pltpu.VMEM((C // 128, cells, 128), F32),
            pltpu.VMEM((FD // 4, C, 128), F32),
            pltpu.VMEM((CD // 4, LONS * FD, 128), F32),
        ],
        name="grad_field",
    )(pos, near(g_inner), near(g_outer), near(cotangent.reshape(cells, C)), near(mix_near), near(pack))
    send = call(
        chip_sum_kernel,
        shape((LONS, SENT, 128), BF16),
        2,
        in_specs=[whole, whole, anywhere],
        out_specs=anywhere,
        scratch_shapes=[
            pltpu.VMEM((GROUPS, LONS, FP - FD, 128), BF16),
            pltpu.VMEM((LONS, REST_ROW - GROUPS * FP, 128), BF16),
            pltpu.SemaphoreType.DMA((GROUPS + 1,)),
        ],
        input_output_aliases={2: 0},
        name="mix_chip_sum",
    )(near(mix_mine), near(mix_other), send)
    columns = lax.all_to_all(send, LON, 0, 0, tiled=True)

    cosine, logsine = latitudes()
    first_order = lat_pos * MD
    seeds = lax.dynamic_slice_in_dim(jnp.asarray(seed_logs()), first_order, MD, 0)
    orders = (first_order + jnp.arange(MD, dtype=jnp.int32)).astype(F32)
    logscale = seeds[:, None] + orders[:, None] * logsine
    logscale, _ = lax.optimization_barrier((logscale, send))
    table = call(
        legendre_kernel,
        shape((MD // 2, L, 2 * HALF), BF16),
        9,
        grid_spec=pltpu.PrefetchScalarGridSpec(
            num_scalar_prefetch=1,
            grid=(L // LB,),
            in_specs=[
                pl.BlockSpec((1, HALF), lambda b, pos: (0, 0)),
                pl.BlockSpec((MD, HALF), lambda b, pos: (0, 0)),
            ],
            out_specs=pl.BlockSpec((MD // 2, LB, 2 * HALF), lambda b, pos: (0, b, 0)),
            scratch_shapes=[
                pltpu.VMEM((MD, 128), F32),
                pltpu.VMEM((MD, HALF), F32),
                pltpu.VMEM((MD, HALF), F32),
                pltpu.VMEM((MD, HALF), F32),
                pltpu.VMEM((LB * MD, HALF), F32),
            ],
        ),
        name="legendre",
    )(pos, jnp.asarray(cosine), logscale)
    columns, table = lax.optimization_barrier((columns, table))

    spectra = call(dft_kernel, near_shape((LATS, SPREAD, 128), BF16), 2, in_specs=[whole, whole], name="dft")(
        near(jnp.asarray(dft_rows())), near(columns)
    )
    spec = lax.all_to_all(spectra, LAT, 0, 0, tiled=True)
    mix_copies = call(copies_kernel, near_shape((CHIPS, 2 * SLOTS * 8, 128), BF16), 2, in_specs=[whole], name="mix_copies")(near(spec))
    mix_mine = lax.all_to_all(mix_copies, CHIP, 0, 0, tiled=True)

    grad_spectra = call(
        synthesis_kernel,
        shape((2, CD, MD, L), F32),
        6,
        grid_spec=pltpu.PrefetchScalarGridSpec(
            num_scalar_prefetch=0,
            grid=(MD // MSTEP,),
            in_specs=[
                whole,
                whole,
                pl.BlockSpec((MSTEP // 2, L, 2 * HALF), lambda b: (b, 0, 0)),
            ],
            out_specs=pl.BlockSpec((2, CD, MSTEP, L), lambda b: (0, 0, b, 0)),
            scratch_shapes=[
                pltpu.VMEM((4 * CD * MD, HALF), F32),
                pltpu.VMEM((L // 128, 2 * CD * MSTEP, 128), F32),
            ],
        ),
        name="synthesis",
    )(near(spec), near(pack), table)
    mix_mine, grad_spectra = lax.optimization_barrier((mix_mine, grad_spectra))
    mix_other = lax.ppermute(mix_mine, CORE, swap)
    grad_mix = call(
        mix_kernel,
        shape((K, C, C), F32),
        2,
        in_specs=[scalar, whole, whole],
        out_specs=anywhere,
        scratch_shapes=[pltpu.VMEM((K, C, C), F32), pltpu.SemaphoreType.DMA((2,))],
        name="mix_out",
    )(core, near(mix_mine), near(mix_other))
    return (grad_field.reshape(TD, FD, C), jnp.transpose(grad_spectra, (0, 2, 1, 3)), grad_mix)


def solution(mesh):
    chips = Mesh(mesh.devices.reshape(LATS, CHIPS, 2), (LAT, CHIP, CORE))
    placed = (P(LAT, LON, None), P(LAT, LON, None), P(), P(), P(), P())
    return jax.shard_map(
        on_device,
        mesh=chips,
        in_specs=placed,
        out_specs=(P(LAT, LON, None), P(None, LAT, LON, None), P()),
        check_vma=False,
    )
```

```python
import functools
import math

import jax
import jax.numpy as jnp
import ml_dtypes
import numpy as np
from jax import lax
from jax.experimental import pallas as pl
from jax.experimental.pallas import tpu as pltpu
from jax.sharding import Mesh, PartitionSpec as P

C = 384
M = 384
L = 384
K = 3
R = 8
S = 8
LB = 32
NLAT = 192
NLON = 768
LATS = 8
LONS = 32
TD = NLAT // LATS
FD = NLON // LONS
CD = C // LONS
MD = M // LATS
XW = FD + 2 * R
TP = 32
FP = FD + 8
COLS = CD * TD
GROUPS = COLS // 128
REST = COLS - GROUPS * 128
SLOTS = 7
REST_ROW = GROUPS * FP + (SLOTS - GROUPS) * 8
SENT = REST_ROW + 8
TAIL_ROW = GROUPS * 2 * MD + 2 * MD * REST // 128
SPREAD = TAIL_ROW + 2 * SLOTS * 8
QUAD = 4
CHIPS = LONS // 2
LAT = "lat"
CHIP = "chip"
CORE = "core"
LON = (CHIP, CORE)
F32 = jnp.float32
BF16 = jnp.bfloat16
VMEM_BYTES = 18 * 1024 * 1024


def call(kernel, out_shape, us, **kw):
    return pl.pallas_call(
        kernel,
        out_shape=out_shape,
        cost_estimate=pl.CostEstimate(flops=int(us * 1.1e9), bytes_accessed=int(us * 3.0e6), transcendentals=0),
        compiler_params=pltpu.CompilerParams(vmem_limit_bytes=VMEM_BYTES),
        **kw,
    )


def near(array):
    return pltpu.with_memory_space_constraint(array, pltpu.VMEM)


def shape(dims, dtype):
    return jax.ShapeDtypeStruct(dims, dtype)


def near_shape(dims, dtype):
    return pltpu.VMEM(dims, dtype)


def swap_blocks(parts):
    lane = lax.broadcasted_iota(jnp.int32, parts[0].shape, 1)
    low = lane < 64
    even = (lane & 32) == 0
    a0, a1, a2, a3 = parts
    b0 = jnp.where(low, a0, pltpu.roll(a2, 64, 1))
    b2 = jnp.where(low, pltpu.roll(a0, 64, 1), a2)
    b1 = jnp.where(low, a1, pltpu.roll(a3, 64, 1))
    b3 = jnp.where(low, pltpu.roll(a1, 64, 1), a3)
    c0 = jnp.where(even, b0, pltpu.roll(b1, 32, 1))
    c1 = jnp.where(even, pltpu.roll(b0, 96, 1), b1)
    c2 = jnp.where(even, b2, pltpu.roll(b3, 32, 1))
    c3 = jnp.where(even, pltpu.roll(b2, 96, 1), b3)
    return c0, c1, c2, c3


ROWS = QUAD * FD
INNER = TD // QUAD - 2


def widen(ext, rows, cot, left, right):
    there = slice(rows.start + 1, rows.stop + 1)
    ext[there, 0:R, :] = left[rows].astype(F32)
    ext[there, R:R + FD, :] = cot[rows].astype(F32)
    ext[there, R + FD:XW, :] = right[rows].astype(F32)


def offsets_in_band():
    lane = lax.broadcasted_iota(jnp.int32, (FD, 256), 1)
    column = lane
    for edge in range(1, QUAD + 2):
        column = column - jnp.where(lane >= edge * XW, XW, 0)
    return (column - lax.broadcasted_iota(jnp.int32, (FD, 256), 0)).astype(F32)


def stencil_quad(quad, apart, tab, ext, band):
    zero = jnp.zeros((FD, 256), F32)
    for r in range(QUAD):
        t = quad * QUAD + r
        sums = [zero] * K
        for s in range(S):
            hit = apart == tab[t, K * S + s:K * S + s + 1, :]
            for k in range(K):
                sums[k] = sums[k] + jnp.where(hit, tab[t, k * S + s:k * S + s + 1, :], 0.0)
        for k in range(K):
            row = (k * QUAD + r) * FD
            band[row:row + FD, :] = sums[k]
    slab = ext[quad * QUAD:quad * QUAD + QUAD + 2].reshape((QUAD + 2) * XW, C).astype(BF16)
    weights = band[:, :(QUAD + 2) * XW].astype(BF16)
    return jnp.dot(weights, slab, preferred_element_type=F32).astype(BF16)


def cells_dot(field, g):
    return lax.dot_general(field, g, (((0,), (0,)), ((), ())), preferred_element_type=F32)


def inner_kernel(tab, cot, left, right, field, g_out, mix_out, ext, band):
    widen(ext, slice(QUAD - 1, TD - QUAD + 1), cot, left, right)
    apart = offsets_in_band()
    for n in range(INNER):
        got = stencil_quad(n + 1, apart, tab, ext, band)
        for k in range(K):
            g_out[n * ROWS:(n + 1) * ROWS, k * C:(k + 1) * C] = got[k * ROWS:(k + 1) * ROWS]
    mix_out[...] = cells_dot(field[ROWS:(INNER + 1) * ROWS, :], g_out[...])


def outer_kernel(core, tab, cot, left, right, top, bottom, field, mix_inner, g_out, mine_out, other_out, ext, band):
    widen(ext, slice(0, QUAD + 1), cot, left, right)
    widen(ext, slice(TD - QUAD - 1, TD), cot, left, right)
    ext[0:1] = top[...].astype(F32)
    ext[TD + 1:TD + 2] = bottom[...].astype(F32)
    apart = offsets_in_band()
    for n in range(2):
        got = stencil_quad(n * (INNER + 1), apart, tab, ext, band)
        for k in range(K):
            g_out[n * ROWS:(n + 1) * ROWS, k * C:(k + 1) * C] = got[k * ROWS:(k + 1) * ROWS]
    mine = jnp.concatenate([field[:ROWS, :], field[(INNER + 1) * ROWS:, :]], axis=0)
    mix = (mix_inner[...] + cells_dot(mine, g_out[...])) * (1.0 / math.sqrt(NLAT * NLON))
    first = core[0] == 0
    low, high = mix[:C // 2], mix[C // 2:]
    mine_out[...] = jnp.where(first, low, high)
    other_out[...] = jnp.where(first, high, low).astype(BF16)


def field_kernel(pos, g_inner, g_outer, cot, mix, pack, gf_out, send_out, flat, turned, send):
    inner = jnp.zeros((INNER * ROWS, C), F32)
    outer = jnp.zeros((2 * ROWS, C), F32)
    for k in range(K):
        span = slice(k * C, (k + 1) * C)
        inner = inner + lax.dot_general(
            g_inner[:, span], mix[k], (((1,), (1,)), ((), ())), preferred_element_type=F32
        )
        outer = outer + lax.dot_general(
            g_outer[:, span], mix[k], (((1,), (1,)), ((), ())), preferred_element_type=F32
        )
    total = cot[...].astype(F32) + jnp.concatenate([outer[:ROWS], inner, outer[ROWS:]], axis=0)
    rounded = total.astype(BF16)
    gf_out[...] = rounded
    rounded = rounded.astype(F32)
    southern = pos[0] >= LATS // 2
    for t in range(TD):
        row = pl.multiple_of(jnp.where(southern, TD - 1 - t, t) * FD, FD)
        for h in range(C // 128):
            flat[h, pl.ds(row, FD), :] = rounded[t * FD:(t + 1) * FD, h * 128:(h + 1) * 128]
    pad = jnp.zeros((TP - TD, 128), F32)
    for fq in range(FD // 4):
        for h in range(C // 128):
            pieces = []
            for fr in range(4):
                pieces.append(flat[h, pl.ds(fq * 4 + fr, TD, stride=FD), :])
                pieces.append(pad)
            turned[fq, h * 128:(h + 1) * 128, :] = jnp.concatenate(pieces, axis=0).T
    for fq in range(FD // 4):
        for q in range(CD // 4):
            parts = [
                turned[fq, pl.ds(q * 4 + cr, LONS, stride=CD), :] for cr in range(4)
            ]
            for fr, part in enumerate(swap_blocks(parts)):
                send[q, pl.ds(fq * 4 + fr, LONS, stride=FD), :] = part
    padded = jnp.concatenate([send[q] for q in range(CD // 4)], axis=1).astype(BF16)
    packed = jnp.dot(padded, pack[...], preferred_element_type=F32)
    for q in range(GROUPS):
        send_out[:, q * FP:q * FP + FD, :] = packed[:, q * 128:(q + 1) * 128].reshape(LONS, FD, 128).astype(BF16)
    last = packed[:, GROUPS * 128:].reshape(LONS, FD // 8, 8, 128)
    rest = last[:, 0]
    for b in range(1, FD // 8):
        rest = rest + pltpu.roll(last[:, b], b * REST, 2)
    send_out[:, REST_ROW - 8:, :] = jnp.concatenate([jnp.zeros_like(rest), rest], axis=1).astype(BF16)


def slot_row(slot):
    return slot * FP + FD if slot < GROUPS else GROUPS * FP + (slot - GROUPS) * 8


def piece_row(piece):
    return TAIL_ROW + piece * 8


def dft_kernel(rows, columns, out):
    parts = [columns[:, q * FP:(q + 1) * FP, :].reshape(LONS * FP, 128) for q in range(GROUPS)]
    rest = columns[:, REST_ROW - 8:, :].astype(F32)[:, 8:]
    blocks = [rest if b == 0 else pltpu.roll(rest, 128 - b * REST, 2) for b in range(FD // 8)]
    blocks.append(jnp.zeros_like(rest))
    parts.append(jnp.concatenate(blocks, axis=1).reshape(LONS * FP, 128).astype(BF16))
    got = jnp.dot(rows[...], jnp.concatenate(parts, axis=1), preferred_element_type=F32)
    got = got * (1.0 / math.sqrt(NLON))
    pieces = []
    for half in range(2):
        for slot in range(SLOTS):
            first = slot_row(slot) // 16 * 16
            start = slot_row(slot) - first
            total = columns[half, first:first + 16, :].astype(F32)
            for chip in range(1, CHIPS):
                total = total + columns[2 * chip + half, first:first + 16, :].astype(F32)
            pieces.append(total[start:start + 8])
    step = 2 * MD * REST // 128
    inside = lax.broadcasted_iota(jnp.int32, (step, 128), 1) < REST
    for i in range(LATS):
        mine = got[i * 2 * MD:(i + 1) * 2 * MD]
        for q in range(GROUPS):
            out[i, q * 2 * MD:(q + 1) * 2 * MD, :] = mine[:, q * 128:(q + 1) * 128].astype(BF16)
        quarters = [
            jnp.where(inside, mine[b * step:(b + 1) * step, GROUPS * 128:], 0.0) for b in range(128 // REST)
        ]
        rest = quarters[0]
        for b in range(1, 128 // REST):
            rest = rest + pltpu.roll(quarters[b], b * REST, 1)
        out[i, GROUPS * 2 * MD:, :] = jnp.concatenate([rest] + pieces, axis=0).astype(BF16)


HALF = LATS // 2 * TP


def legendre_kernel(pos, cosines, logscale, out, coef, prev_s, early_s, scale_s, rows):
    block = pl.program_id(0)
    order = pos[0] * MD + lax.broadcasted_iota(jnp.int32, (MD, 128), 0)
    order_f = order.astype(F32)

    @pl.when(block == 0)
    def _():
        prev_s[...] = jnp.zeros_like(prev_s)
        early_s[...] = jnp.zeros_like(early_s)
        scale_s[...] = logscale[...]

    lane = lax.broadcasted_iota(jnp.int32, (MD, 128), 1)
    degree = block * LB + (lane & (LB - 1))
    deg_f = degree.astype(F32)
    higher = degree > order
    lower_a = jnp.where(higher, deg_f * deg_f - order_f * order_f, 1.0)
    factor_a = jnp.where(higher, jnp.sqrt((4.0 * deg_f * deg_f - 1.0) / lower_a), 0.0)
    before = deg_f - 1.0
    upper_b = jnp.maximum(before * before - order_f * order_f, 0.0)
    lower_b = jnp.maximum(4.0 * before * before - 1.0, 1.0)
    factor_b = jnp.sqrt(upper_b / lower_b)
    coef[...] = jnp.where(lane < LB, factor_a, factor_b)

    x = jnp.broadcast_to(cosines[...], (MD, 128))
    prev = prev_s[...]
    early = early_s[...]
    factor = jnp.exp(scale_s[...])
    for step in range(LB):
        a = jnp.broadcast_to(coef[:, step:step + 1], (MD, 128))
        b = jnp.broadcast_to(coef[:, LB + step:LB + step + 1], (MD, 128))
        seed = jnp.where(order == block * LB + step, 1.0, 0.0)
        fresh = a * (x * prev - b * early) + seed
        rows[step * MD:(step + 1) * MD, :] = fresh * factor
        early, prev = prev, fresh
    biggest = jnp.maximum(jnp.abs(prev), jnp.abs(early))
    divisor = jnp.where(biggest > 0.0, biggest, 1.0)
    prev_s[...] = prev / divisor
    early_s[...] = early / divisor
    scale_s[...] = scale_s[...] + jnp.log(divisor)
    for m in range(MD):
        side = (m % 2) * 128
        out[m // 2, :, side:side + 128] = rows[pl.ds(m, LB, stride=MD), :].astype(BF16)


MSTEP = 8


def synthesis_kernel(spec, pack, leg, out, lined, rows):
    step = pl.program_id(0)

    @pl.when(step == 0)
    def _():
        packed = []
        for i in range(LATS):
            groups = [spec[i, q * 2 * MD:(q + 1) * 2 * MD, :] for q in range(GROUPS)]
            rest = spec[i, GROUPS * 2 * MD:GROUPS * 2 * MD + 32, :].astype(F32)[:2 * MD * REST // 128]
            blocks = [rest if b == 0 else pltpu.roll(rest, 128 - b * REST, 1) for b in range(128 // REST)]
            groups.append(jnp.concatenate(blocks, axis=0).astype(BF16))
            packed.append(jnp.concatenate(groups, axis=1))
        padded = lax.dot_general(
            jnp.concatenate(packed, axis=0), pack[...], (((1,), (1,)), ((), ())), preferred_element_type=F32
        )
        padded = [padded[i * 2 * MD:(i + 1) * 2 * MD] for i in range(LATS)]
        for q in range(CD // 4):
            span = slice(q * 128, (q + 1) * 128)
            north = [padded[i][:, span] for i in range(LATS // 2)]
            south = [padded[LATS - 1 - i][:, span] for i in range(LATS // 2)]
            for odd in range(2):
                parts = [n - s if odd else n + s for n, s in zip(north, south)]
                for cr, part in enumerate(swap_blocks(parts)):
                    for p in range(2):
                        base = ((odd * 2 + p) * CD + q * 4 + cr) * MD
                        lined[base:base + MD, :] = part[p * MD:(p + 1) * MD]

    wide = 2 * CD
    odd_lane = (lax.broadcasted_iota(jnp.int32, (wide, L), 1) & 1) == 1
    zero = jnp.zeros((2 * wide, HALF), F32)
    for pair in range(MSTEP // 2):
        first = step * MSTEP + 2 * pair
        mine = [lined[pl.ds(first + side, 2 * wide, stride=MD), :] for side in range(2)]
        lhs = jnp.concatenate(
            [jnp.concatenate([mine[0], zero], axis=1), jnp.concatenate([zero, mine[1]], axis=1)], axis=0
        ).astype(BF16)
        got = lax.dot_general(
            lhs, leg[pair], (((1,), (1,)), ((), ())), preferred_element_type=F32
        ) * math.sqrt(4.0 * math.pi / NLAT)
        done = [
            jnp.where(odd_lane, got[wide:2 * wide], got[:wide]),
            jnp.where(odd_lane, got[2 * wide:3 * wide], got[3 * wide:]),
        ]
        for side in range(2):
            for h in range(L // 128):
                rows[h, pl.ds(2 * pair + side, wide, stride=MSTEP), :] = done[side][:, h * 128:(h + 1) * 128]
    for p in range(2):
        for c in range(CD):
            base = (p * CD + c) * MSTEP
            for h in range(L // 128):
                out[p, c, :, h * 128:(h + 1) * 128] = rows[h, base:base + MSTEP, :]


HALF_TILES = C // 32 * (K * C // 128)


def tiles_of(chip):
    return [(slot, *divmod(SLOTS * chip + slot, K * C // 128)) for slot in range(SLOTS) if SLOTS * chip + slot < HALF_TILES]


def chip_sum_kernel(mine, other, send, out, near_rows, far_rows, sems):
    total = (mine[...] + other[...].astype(F32)).astype(BF16)
    near_rows[...] = jnp.zeros_like(near_rows)
    far_rows[...] = jnp.zeros_like(far_rows)
    for chip in range(CHIPS):
        for slot, row, col in tiles_of(chip):
            for core in range(2):
                first = core * (C // 4) + row * 8
                tile = total[first:first + 8, col * 128:(col + 1) * 128]
                if slot < GROUPS:
                    near_rows[slot, 2 * chip + core] = tile
                else:
                    far = (slot - GROUPS) * 8
                    far_rows[2 * chip + core, far:far + 8, :] = tile
    copies = [
        pltpu.make_async_copy(near_rows.at[q], out.at[:, q * FP + FD:(q + 1) * FP, :], sems.at[q]) for q in range(GROUPS)
    ]
    copies.append(pltpu.make_async_copy(far_rows, out.at[:, GROUPS * FP:REST_ROW, :], sems.at[GROUPS]))
    for copy in copies:
        copy.start()
    for copy in copies:
        copy.wait()


def copies_kernel(spec, out):
    for piece in range(2 * SLOTS):
        row = piece_row(piece)
        first = row // 16 * 16
        total = spec[0, first:first + 16, :].astype(F32)
        for i in range(1, LATS):
            total = total + spec[i, first:first + 16, :].astype(F32)
        total = total[row - first:row - first + 8].astype(BF16)
        for chip in range(CHIPS):
            out[chip, piece * 8:(piece + 1) * 8, :] = total


def mix_kernel(held, parts, *rest):
    out, rows, sems = rest[-3:]
    copies = []
    for half in range(2):
        for chip in range(CHIPS):
            for slot, row, col in tiles_of(chip):
                k, d = divmod(col, C // 128)
                piece = (half * SLOTS + slot) * 8
                rows[half, k, row * 8:row * 8 + 8, d * 128:(d + 1) * 128] = parts[chip, piece:piece + 8, :].astype(F32)
        base = pl.multiple_of(half * (C // 2) + held[0] * (C // 4), 8)
        copies.append(pltpu.make_async_copy(rows.at[half], out.at[:, pl.ds(base, C // 4)], sems.at[half]))
        copies[-1].start()
    for copy in copies:
        copy.wait()


def dft_rows():
    order = np.arange(M).reshape(LATS, 1, MD)
    order = np.broadcast_to(order, (LATS, 2, MD)).reshape(-1)
    part = np.broadcast_to(np.arange(2).reshape(1, 2, 1), (LATS, 2, MD)).reshape(-1)
    angle = 2.0 * np.pi / NLON * ((order[:, None] * np.arange(NLON)[None, :]) % NLON)
    angle = angle.astype(np.float32)
    rows = np.where(part[:, None] == 0, np.cos(angle), -np.sin(angle))
    padded = np.zeros((2 * M, LONS, FP), np.float32)
    padded[:, :, :FD] = rows.reshape(2 * M, LONS, FD)
    return padded.reshape(2 * M, LONS * FP).astype(ml_dtypes.bfloat16)


def packing():
    pack = np.zeros((CD * TP, CD * TP), np.float32)
    for c in range(CD):
        for t in range(TD):
            pack[c * TP + t, c * TD + t] = 1.0
    return pack.astype(ml_dtypes.bfloat16)


def latitudes():
    angle = ((np.arange(NLAT) + 0.5) * (np.pi / NLAT)).reshape(LATS, TD)
    cosine = np.zeros((LATS, TP), np.float32)
    logsine = np.zeros((LATS, TP), np.float32)
    cosine[:, :TD] = np.cos(angle)
    logsine[:, :TD] = np.log(np.sin(angle))
    half = LATS // 2
    return cosine[:half].reshape(1, -1), logsine[:half].reshape(1, -1)


def seed_logs():
    degree = np.arange(M, dtype=np.float64)
    steps = np.log((2.0 * degree + 1.0) / (2.0 * degree + 2.0))
    prefix = np.concatenate([np.zeros(1), np.cumsum(steps)[:-1]])
    return (0.5 * np.log((2.0 * degree + 1.0) / (4.0 * np.pi)) + 0.5 * prefix).astype(np.float32)


def band_lanes():
    mark = np.zeros((TD, 3, 256), np.float32)
    for t in range(TD):
        for rr in range(3):
            start = (t % QUAD + rr) * XW
            mark[t, rr, start:start + XW] = 1.0
    return mark


def tap_rows(taps, offsets, counts, first_row):
    slot_ids = lax.broadcasted_iota(jnp.int32, taps.shape, 3)
    live = jnp.where(slot_ids < counts[:, None, None, None], taps, 0.0).astype(BF16).astype(F32)
    shift = (R - offsets).astype(F32)[:, None]
    both = jnp.concatenate([live, shift], axis=1)
    both = jnp.pad(both, ((1, 1), (0, 0), (0, 0), (0, 0)))
    return lax.dynamic_slice_in_dim(both, first_row, TD + 2, 0)


def tap_table(both):
    marks = band_lanes()
    table = 0.0
    for rr in range(3):
        mine = both[rr:rr + TD, :, 2 - rr, :].reshape(TD, (K + 1) * S)
        table = table + mine[:, :, None] * marks[:, rr][:, None, :]
    return table


def on_device(field, cotangent, mix_weight, taps, offsets, counts):
    lat_pos = lax.axis_index(LAT)
    up = [(i, (i + 1) % LONS) for i in range(LONS)]
    down = [(j, i) for i, j in up]
    left = lax.ppermute(cotangent[:, FD - R:], LON, up)
    right = lax.ppermute(cotangent[:, :R], LON, down)
    edge_rows = [
        jnp.concatenate([left[t:t + 1], cotangent[t:t + 1], right[t:t + 1]], axis=1) for t in (0, TD - 1)
    ]
    north = [(i, i + 1) for i in range(LATS - 1)]
    south = [(j, i) for i, j in north]
    top = lax.ppermute(edge_rows[1], LAT, north)
    bottom = lax.ppermute(edge_rows[0], LAT, south)

    whole = pl.BlockSpec(memory_space=pltpu.VMEM)
    tap_part, _ = lax.optimization_barrier((tap_rows(taps, offsets, counts, lat_pos * TD), edge_rows))
    tab = tap_table(tap_part)
    cells = TD * FD
    core = jnp.reshape(lax.axis_index(CORE), (1,)).astype(jnp.int32)
    scalar = pl.BlockSpec(memory_space=pltpu.SMEM)
    anywhere = pl.BlockSpec(memory_space=pl.ANY)
    half = (C // 2, K * C)
    rims = (near(left), near(right))
    near_cot, near_field = near(cotangent), near(field.reshape(cells, C))
    scratch = [pltpu.VMEM((TD + 2, XW, C), F32), pltpu.VMEM((K * ROWS, 256), F32)]
    g_inner, mix_inner = call(
        inner_kernel,
        (near_shape((INNER * ROWS, K * C), BF16), near_shape((C, K * C), F32)),
        2,
        in_specs=[whole] * 5,
        scratch_shapes=scratch,
        name="stencil_inner",
    )(near(tab), near_cot, *rims, near_field)
    pack = near(jnp.asarray(packing()))
    mix_near = near(mix_weight)
    top, bottom, pack, mix_near = lax.optimization_barrier((top, bottom, pack, mix_near))
    g_outer, mix_mine, mix_other = call(
        outer_kernel,
        (near_shape((2 * ROWS, K * C), BF16), near_shape(half, F32), near_shape(half, BF16)),
        2,
        in_specs=[scalar] + [whole] * 8,
        scratch_shapes=scratch,
        name="stencil_outer",
    )(core, near(tab), near_cot, *rims, near(top), near(bottom), near_field, near(mix_inner))
    swap = [(0, 1), (1, 0)]
    mix_other = lax.ppermute(mix_other, CORE, swap)

    pos = jnp.reshape(lat_pos, (1,)).astype(jnp.int32)
    grad_field, send = call(
        field_kernel,
        (shape((cells, C), BF16), shape((LONS, SENT, 128), BF16)),
        5,
        in_specs=[scalar] + [whole] * 5,
        scratch_shapes=[
            pltpu.VMEM((C // 128, cells, 128), F32),
            pltpu.VMEM((FD // 4, C, 128), F32),
            pltpu.VMEM((CD // 4, LONS * FD, 128), F32),
        ],
        name="grad_field",
    )(pos, near(g_inner), near(g_outer), near(cotangent.reshape(cells, C)), near(mix_near), near(pack))
    send = call(
        chip_sum_kernel,
        shape((LONS, SENT, 128), BF16),
        2,
        in_specs=[whole, whole, anywhere],
        out_specs=anywhere,
        scratch_shapes=[
            pltpu.VMEM((GROUPS, LONS, FP - FD, 128), BF16),
            pltpu.VMEM((LONS, REST_ROW - GROUPS * FP, 128), BF16),
            pltpu.SemaphoreType.DMA((GROUPS + 1,)),
        ],
        input_output_aliases={2: 0},
        name="mix_chip_sum",
    )(near(mix_mine), near(mix_other), send)
    columns = lax.all_to_all(send, LON, 0, 0, tiled=True)

    cosine, logsine = latitudes()
    first_order = lat_pos * MD
    seeds = lax.dynamic_slice_in_dim(jnp.asarray(seed_logs()), first_order, MD, 0)
    orders = (first_order + jnp.arange(MD, dtype=jnp.int32)).astype(F32)
    logscale = seeds[:, None] + orders[:, None] * logsine
    logscale, _ = lax.optimization_barrier((logscale, send))
    table = call(
        legendre_kernel,
        shape((MD // 2, L, 2 * HALF), BF16),
        9,
        grid_spec=pltpu.PrefetchScalarGridSpec(
            num_scalar_prefetch=1,
            grid=(L // LB,),
            in_specs=[
                pl.BlockSpec((1, HALF), lambda b, pos: (0, 0)),
                pl.BlockSpec((MD, HALF), lambda b, pos: (0, 0)),
            ],
            out_specs=pl.BlockSpec((MD // 2, LB, 2 * HALF), lambda b, pos: (0, b, 0)),
            scratch_shapes=[
                pltpu.VMEM((MD, 128), F32),
                pltpu.VMEM((MD, HALF), F32),
                pltpu.VMEM((MD, HALF), F32),
                pltpu.VMEM((MD, HALF), F32),
                pltpu.VMEM((LB * MD, HALF), F32),
            ],
        ),
        name="legendre",
    )(pos, jnp.asarray(cosine), logscale)
    columns, table = lax.optimization_barrier((columns, table))

    spectra = call(dft_kernel, near_shape((LATS, SPREAD, 128), BF16), 2, in_specs=[whole, whole], name="dft")(
        near(jnp.asarray(dft_rows())), near(columns)
    )
    spec = lax.all_to_all(spectra, LAT, 0, 0, tiled=True)
    mix_copies = call(copies_kernel, near_shape((CHIPS, 2 * SLOTS * 8, 128), BF16), 2, in_specs=[whole], name="mix_copies")(near(spec))
    mix_mine = lax.all_to_all(mix_copies, CHIP, 0, 0, tiled=True)

    grad_spectra = call(
        synthesis_kernel,
        shape((2, CD, MD, L), F32),
        6,
        grid_spec=pltpu.PrefetchScalarGridSpec(
            num_scalar_prefetch=0,
            grid=(MD // MSTEP,),
            in_specs=[
                whole,
                whole,
                pl.BlockSpec((MSTEP // 2, L, 2 * HALF), lambda b: (b, 0, 0)),
            ],
            out_specs=pl.BlockSpec((2, CD, MSTEP, L), lambda b: (0, 0, b, 0)),
            scratch_shapes=[
                pltpu.VMEM((4 * CD * MD, HALF), F32),
                pltpu.VMEM((L // 128, 2 * CD * MSTEP, 128), F32),
            ],
        ),
        name="synthesis",
    )(near(spec), near(pack), table)
    mix_mine, grad_spectra = lax.optimization_barrier((mix_mine, grad_spectra))
    mix_other = lax.ppermute(mix_mine, CORE, swap)
    grad_mix = ()
    for held, parts in ((core, mix_mine), (1 - core, mix_other)):
        grad_mix = (
            call(
                mix_kernel,
                shape((K, C, C), F32),
                1,
                in_specs=[scalar, whole] + [anywhere] * len(grad_mix),
                out_specs=anywhere,
                scratch_shapes=[pltpu.VMEM((2, K, C // 4, C), F32), pltpu.SemaphoreType.DMA((2,))],
                input_output_aliases={2: 0} if grad_mix else {},
                name="mix_out",
            )(held, near(parts), *grad_mix),
        )
    return (grad_field.reshape(TD, FD, C), jnp.transpose(grad_spectra, (0, 2, 1, 3)), grad_mix[0])


def solution(mesh):
    chips = Mesh(mesh.devices.reshape(LATS, CHIPS, 2), (LAT, CHIP, CORE))
    placed = (P(LAT, LON, None), P(LAT, LON, None), P(), P(), P(), P())
    return jax.shard_map(
        on_device,
        mesh=chips,
        in_specs=placed,
        out_specs=(P(LAT, LON, None), P(None, LAT, LON, None), P()),
        check_vma=False,
    )
```

```python
import functools
import math

import jax
import jax.numpy as jnp
import ml_dtypes
import numpy as np
from jax import lax
from jax.experimental import pallas as pl
from jax.experimental.pallas import tpu as pltpu
from jax.sharding import Mesh, PartitionSpec as P

C = 384
M = 384
L = 384
K = 3
R = 8
S = 8
LB = 32
NLAT = 192
NLON = 768
LATS = 8
LONS = 32
TD = NLAT // LATS
FD = NLON // LONS
CD = C // LONS
MD = M // LATS
XW = FD + 2 * R
TP = 32
FP = FD + 8
COLS = CD * TD
GROUPS = COLS // 128
REST = COLS - GROUPS * 128
SLOTS = 7
REST_ROW = GROUPS * FP + (SLOTS - GROUPS) * 8
SENT = REST_ROW + 8
TAIL_ROW = GROUPS * 2 * MD + 2 * MD * REST // 128
SPREAD = TAIL_ROW + 2 * SLOTS * 8
QUAD = 4
CHIPS = LONS // 2
LAT = "lat"
CHIP = "chip"
CORE = "core"
LON = (CHIP, CORE)
F32 = jnp.float32
BF16 = jnp.bfloat16
VMEM_BYTES = 18 * 1024 * 1024


def call(kernel, out_shape, us, **kw):
    return pl.pallas_call(
        kernel,
        out_shape=out_shape,
        cost_estimate=pl.CostEstimate(flops=int(us * 1.1e9), bytes_accessed=int(us * 3.0e6), transcendentals=0),
        compiler_params=pltpu.CompilerParams(vmem_limit_bytes=VMEM_BYTES),
        **kw,
    )


def near(array):
    return pltpu.with_memory_space_constraint(array, pltpu.VMEM)


def shape(dims, dtype):
    return jax.ShapeDtypeStruct(dims, dtype)


def near_shape(dims, dtype):
    return pltpu.VMEM(dims, dtype)


def swap_blocks(parts):
    lane = lax.broadcasted_iota(jnp.int32, parts[0].shape, 1)
    low = lane < 64
    even = (lane & 32) == 0
    a0, a1, a2, a3 = parts
    b0 = jnp.where(low, a0, pltpu.roll(a2, 64, 1))
    b2 = jnp.where(low, pltpu.roll(a0, 64, 1), a2)
    b1 = jnp.where(low, a1, pltpu.roll(a3, 64, 1))
    b3 = jnp.where(low, pltpu.roll(a1, 64, 1), a3)
    c0 = jnp.where(even, b0, pltpu.roll(b1, 32, 1))
    c1 = jnp.where(even, pltpu.roll(b0, 96, 1), b1)
    c2 = jnp.where(even, b2, pltpu.roll(b3, 32, 1))
    c3 = jnp.where(even, pltpu.roll(b2, 96, 1), b3)
    return c0, c1, c2, c3


ROWS = QUAD * FD
INNER = TD // QUAD - 2


def widen(ext, rows, cot, left, right):
    there = slice(rows.start + 1, rows.stop + 1)
    ext[there, 0:R, :] = left[rows].astype(F32)
    ext[there, R:R + FD, :] = cot[rows].astype(F32)
    ext[there, R + FD:XW, :] = right[rows].astype(F32)


def offsets_in_band():
    lane = lax.broadcasted_iota(jnp.int32, (FD, 256), 1)
    column = lane
    for edge in range(1, QUAD + 2):
        column = column - jnp.where(lane >= edge * XW, XW, 0)
    return (column - lax.broadcasted_iota(jnp.int32, (FD, 256), 0)).astype(F32)


def stencil_quad(quad, apart, tab, ext, band):
    zero = jnp.zeros((FD, 256), F32)
    for r in range(QUAD):
        t = quad * QUAD + r
        sums = [zero] * K
        for s in range(S):
            hit = apart == tab[t, K * S + s:K * S + s + 1, :]
            for k in range(K):
                sums[k] = sums[k] + jnp.where(hit, tab[t, k * S + s:k * S + s + 1, :], 0.0)
        for k in range(K):
            row = (k * QUAD + r) * FD
            band[row:row + FD, :] = sums[k]
    slab = ext[quad * QUAD:quad * QUAD + QUAD + 2].reshape((QUAD + 2) * XW, C).astype(BF16)
    weights = band[:, :(QUAD + 2) * XW].astype(BF16)
    return jnp.dot(weights, slab, preferred_element_type=F32).astype(BF16)


def cells_dot(field, g):
    return lax.dot_general(field, g, (((0,), (0,)), ((), ())), preferred_element_type=F32)


def weigh(g, mix):
    total = jnp.zeros((g.shape[0], C), F32)
    for k in range(K):
        total = total + lax.dot_general(
            g[:, k * C:(k + 1) * C], mix[k], (((1,), (1,)), ((), ())), preferred_element_type=F32
        )
    return total


def inner_kernel(tab, cot, left, right, field, mix, field_out, mix_out, g_out, ext, band):
    widen(ext, slice(QUAD - 1, TD - QUAD + 1), cot, left, right)
    apart = offsets_in_band()
    for n in range(INNER):
        got = stencil_quad(n + 1, apart, tab, ext, band)
        for k in range(K):
            g_out[n * ROWS:(n + 1) * ROWS, k * C:(k + 1) * C] = got[k * ROWS:(k + 1) * ROWS]
    mix_out[...] = cells_dot(field[ROWS:(INNER + 1) * ROWS, :], g_out[...])
    field_out[...] = weigh(g_out, mix)


def outer_kernel(core, tab, cot, left, right, top, bottom, field, mix_inner, g_out, mine_out, other_out, ext, band):
    widen(ext, slice(0, QUAD + 1), cot, left, right)
    widen(ext, slice(TD - QUAD - 1, TD), cot, left, right)
    ext[0:1] = top[...].astype(F32)
    ext[TD + 1:TD + 2] = bottom[...].astype(F32)
    apart = offsets_in_band()
    for n in range(2):
        got = stencil_quad(n * (INNER + 1), apart, tab, ext, band)
        for k in range(K):
            g_out[n * ROWS:(n + 1) * ROWS, k * C:(k + 1) * C] = got[k * ROWS:(k + 1) * ROWS]
    mine = jnp.concatenate([field[:ROWS, :], field[(INNER + 1) * ROWS:, :]], axis=0)
    mix = (mix_inner[...] + cells_dot(mine, g_out[...])) * (1.0 / math.sqrt(NLAT * NLON))
    first = core[0] == 0
    low, high = mix[:C // 2], mix[C // 2:]
    mine_out[...] = jnp.where(first, low, high)
    other_out[...] = jnp.where(first, high, low).astype(BF16)


def field_kernel(pos, inner, g_outer, cot, mix, pack, gf_out, send_out, flat, turned, send):
    outer = weigh(g_outer, mix)
    total = cot[...].astype(F32) + jnp.concatenate([outer[:ROWS], inner[...], outer[ROWS:]], axis=0)
    rounded = total.astype(BF16)
    gf_out[...] = rounded
    rounded = rounded.astype(F32)
    southern = pos[0] >= LATS // 2
    for t in range(TD):
        row = pl.multiple_of(jnp.where(southern, TD - 1 - t, t) * FD, FD)
        for h in range(C // 128):
            flat[h, pl.ds(row, FD), :] = rounded[t * FD:(t + 1) * FD, h * 128:(h + 1) * 128]
    pad = jnp.zeros((TP - TD, 128), F32)
    for fq in range(FD // 4):
        for h in range(C // 128):
            pieces = []
            for fr in range(4):
                pieces.append(flat[h, pl.ds(fq * 4 + fr, TD, stride=FD), :])
                pieces.append(pad)
            turned[fq, h * 128:(h + 1) * 128, :] = jnp.concatenate(pieces, axis=0).T
    for fq in range(FD // 4):
        for q in range(CD // 4):
            parts = [
                turned[fq, pl.ds(q * 4 + cr, LONS, stride=CD), :] for cr in range(4)
            ]
            for fr, part in enumerate(swap_blocks(parts)):
                send[q, pl.ds(fq * 4 + fr, LONS, stride=FD), :] = part
    padded = jnp.concatenate([send[q] for q in range(CD // 4)], axis=1).astype(BF16)
    packed = jnp.dot(padded, pack[...], preferred_element_type=F32)
    for q in range(GROUPS):
        send_out[:, q * FP:q * FP + FD, :] = packed[:, q * 128:(q + 1) * 128].reshape(LONS, FD, 128).astype(BF16)
    last = packed[:, GROUPS * 128:].reshape(LONS, FD // 8, 8, 128)
    rest = last[:, 0]
    for b in range(1, FD // 8):
        rest = rest + pltpu.roll(last[:, b], b * REST, 2)
    send_out[:, REST_ROW - 8:, :] = jnp.concatenate([jnp.zeros_like(rest), rest], axis=1).astype(BF16)


def slot_row(slot):
    return slot * FP + FD if slot < GROUPS else GROUPS * FP + (slot - GROUPS) * 8


def piece_row(piece):
    return TAIL_ROW + piece * 8


def dft_kernel(rows, columns, out):
    parts = [columns[:, q * FP:(q + 1) * FP, :].reshape(LONS * FP, 128) for q in range(GROUPS)]
    rest = columns[:, REST_ROW - 8:, :].astype(F32)[:, 8:]
    blocks = [rest if b == 0 else pltpu.roll(rest, 128 - b * REST, 2) for b in range(FD // 8)]
    blocks.append(jnp.zeros_like(rest))
    parts.append(jnp.concatenate(blocks, axis=1).reshape(LONS * FP, 128).astype(BF16))
    got = jnp.dot(rows[...], jnp.concatenate(parts, axis=1), preferred_element_type=F32)
    got = got * (1.0 / math.sqrt(NLON))
    pieces = []
    for half in range(2):
        for slot in range(SLOTS):
            first = slot_row(slot) // 16 * 16
            start = slot_row(slot) - first
            total = columns[half, first:first + 16, :].astype(F32)
            for chip in range(1, CHIPS):
                total = total + columns[2 * chip + half, first:first + 16, :].astype(F32)
            pieces.append(total[start:start + 8])
    step = 2 * MD * REST // 128
    inside = lax.broadcasted_iota(jnp.int32, (step, 128), 1) < REST
    for i in range(LATS):
        mine = got[i * 2 * MD:(i + 1) * 2 * MD]
        for q in range(GROUPS):
            out[i, q * 2 * MD:(q + 1) * 2 * MD, :] = mine[:, q * 128:(q + 1) * 128].astype(BF16)
        quarters = [
            jnp.where(inside, mine[b * step:(b + 1) * step, GROUPS * 128:], 0.0) for b in range(128 // REST)
        ]
        rest = quarters[0]
        for b in range(1, 128 // REST):
            rest = rest + pltpu.roll(quarters[b], b * REST, 1)
        out[i, GROUPS * 2 * MD:, :] = jnp.concatenate([rest] + pieces, axis=0).astype(BF16)


HALF = LATS // 2 * TP


def legendre_kernel(pos, cosines, logscale, out, coef, prev_s, early_s, scale_s, rows):
    block = pl.program_id(0)
    order = pos[0] * MD + lax.broadcasted_iota(jnp.int32, (MD, 128), 0)
    order_f = order.astype(F32)

    @pl.when(block == 0)
    def _():
        prev_s[...] = jnp.zeros_like(prev_s)
        early_s[...] = jnp.zeros_like(early_s)
        scale_s[...] = logscale[...]

    lane = lax.broadcasted_iota(jnp.int32, (MD, 128), 1)
    degree = block * LB + (lane & (LB - 1))
    deg_f = degree.astype(F32)
    higher = degree > order
    lower_a = jnp.where(higher, deg_f * deg_f - order_f * order_f, 1.0)
    factor_a = jnp.where(higher, jnp.sqrt((4.0 * deg_f * deg_f - 1.0) / lower_a), 0.0)
    before = deg_f - 1.0
    upper_b = jnp.maximum(before * before - order_f * order_f, 0.0)
    lower_b = jnp.maximum(4.0 * before * before - 1.0, 1.0)
    factor_b = jnp.sqrt(upper_b / lower_b)
    coef[...] = jnp.where(lane < LB, factor_a, factor_b)

    x = jnp.broadcast_to(cosines[...], (MD, 128))
    prev = prev_s[...]
    early = early_s[...]
    factor = jnp.exp(scale_s[...])
    for step in range(LB):
        a = jnp.broadcast_to(coef[:, step:step + 1], (MD, 128))
        b = jnp.broadcast_to(coef[:, LB + step:LB + step + 1], (MD, 128))
        seed = jnp.where(order == block * LB + step, 1.0, 0.0)
        fresh = a * (x * prev - b * early) + seed
        rows[step * MD:(step + 1) * MD, :] = fresh * factor
        early, prev = prev, fresh
    biggest = jnp.maximum(jnp.abs(prev), jnp.abs(early))
    divisor = jnp.where(biggest > 0.0, biggest, 1.0)
    prev_s[...] = prev / divisor
    early_s[...] = early / divisor
    scale_s[...] = scale_s[...] + jnp.log(divisor)
    for m in range(MD):
        side = (m % 2) * 128
        out[m // 2, :, side:side + 128] = rows[pl.ds(m, LB, stride=MD), :].astype(BF16)


MSTEP = 8


def synthesis_kernel(spec, pack, leg, out, lined, rows):
    step = pl.program_id(0)

    @pl.when(step == 0)
    def _():
        packed = []
        for i in range(LATS):
            groups = [spec[i, q * 2 * MD:(q + 1) * 2 * MD, :] for q in range(GROUPS)]
            rest = spec[i, GROUPS * 2 * MD:GROUPS * 2 * MD + 32, :].astype(F32)[:2 * MD * REST // 128]
            blocks = [rest if b == 0 else pltpu.roll(rest, 128 - b * REST, 1) for b in range(128 // REST)]
            groups.append(jnp.concatenate(blocks, axis=0).astype(BF16))
            packed.append(jnp.concatenate(groups, axis=1))
        padded = lax.dot_general(
            jnp.concatenate(packed, axis=0), pack[...], (((1,), (1,)), ((), ())), preferred_element_type=F32
        )
        padded = [padded[i * 2 * MD:(i + 1) * 2 * MD] for i in range(LATS)]
        for q in range(CD // 4):
            span = slice(q * 128, (q + 1) * 128)
            north = [padded[i][:, span] for i in range(LATS // 2)]
            south = [padded[LATS - 1 - i][:, span] for i in range(LATS // 2)]
            for odd in range(2):
                parts = [n - s if odd else n + s for n, s in zip(north, south)]
                for cr, part in enumerate(swap_blocks(parts)):
                    for p in range(2):
                        base = ((odd * 2 + p) * CD + q * 4 + cr) * MD
                        lined[base:base + MD, :] = part[p * MD:(p + 1) * MD]

    wide = 2 * CD
    odd_lane = (lax.broadcasted_iota(jnp.int32, (wide, L), 1) & 1) == 1
    zero = jnp.zeros((2 * wide, HALF), F32)
    for pair in range(MSTEP // 2):
        first = step * MSTEP + 2 * pair
        mine = [lined[pl.ds(first + side, 2 * wide, stride=MD), :] for side in range(2)]
        lhs = jnp.concatenate(
            [jnp.concatenate([mine[0], zero], axis=1), jnp.concatenate([zero, mine[1]], axis=1)], axis=0
        ).astype(BF16)
        got = lax.dot_general(
            lhs, leg[pair], (((1,), (1,)), ((), ())), preferred_element_type=F32
        ) * math.sqrt(4.0 * math.pi / NLAT)
        done = [
            jnp.where(odd_lane, got[wide:2 * wide], got[:wide]),
            jnp.where(odd_lane, got[2 * wide:3 * wide], got[3 * wide:]),
        ]
        for side in range(2):
            for h in range(L // 128):
                rows[h, pl.ds(2 * pair + side, wide, stride=MSTEP), :] = done[side][:, h * 128:(h + 1) * 128]
    for p in range(2):
        for c in range(CD):
            base = (p * CD + c) * MSTEP
            for h in range(L // 128):
                out[p, c, :, h * 128:(h + 1) * 128] = rows[h, base:base + MSTEP, :]


HALF_TILES = C // 32 * (K * C // 128)


def tiles_of(chip):
    return [(slot, *divmod(SLOTS * chip + slot, K * C // 128)) for slot in range(SLOTS) if SLOTS * chip + slot < HALF_TILES]


def chip_sum_kernel(mine, other, send, out, near_rows, far_rows, sems):
    total = (mine[...] + other[...].astype(F32)).astype(BF16)
    near_rows[...] = jnp.zeros_like(near_rows)
    far_rows[...] = jnp.zeros_like(far_rows)
    for chip in range(CHIPS):
        for slot, row, col in tiles_of(chip):
            for core in range(2):
                first = core * (C // 4) + row * 8
                tile = total[first:first + 8, col * 128:(col + 1) * 128]
                if slot < GROUPS:
                    near_rows[slot, 2 * chip + core] = tile
                else:
                    far = (slot - GROUPS) * 8
                    far_rows[2 * chip + core, far:far + 8, :] = tile
    copies = [
        pltpu.make_async_copy(near_rows.at[q], out.at[:, q * FP + FD:(q + 1) * FP, :], sems.at[q]) for q in range(GROUPS)
    ]
    copies.append(pltpu.make_async_copy(far_rows, out.at[:, GROUPS * FP:REST_ROW, :], sems.at[GROUPS]))
    for copy in copies:
        copy.start()
    for copy in copies:
        copy.wait()


def copies_kernel(spec, out):
    for piece in range(2 * SLOTS):
        row = piece_row(piece)
        first = row // 16 * 16
        total = spec[0, first:first + 16, :].astype(F32)
        for i in range(1, LATS):
            total = total + spec[i, first:first + 16, :].astype(F32)
        total = total[row - first:row - first + 8].astype(BF16)
        for chip in range(CHIPS):
            out[chip, piece * 8:(piece + 1) * 8, :] = total


def mix_kernel(held, parts, *rest):
    out, rows, sems = rest[-3:]
    copies = []
    for half in range(2):
        for chip in range(CHIPS):
            for slot, row, col in tiles_of(chip):
                k, d = divmod(col, C // 128)
                piece = (half * SLOTS + slot) * 8
                rows[half, k, row * 8:row * 8 + 8, d * 128:(d + 1) * 128] = parts[chip, piece:piece + 8, :].astype(F32)
        base = pl.multiple_of(half * (C // 2) + held[0] * (C // 4), 8)
        copies.append(pltpu.make_async_copy(rows.at[half], out.at[:, pl.ds(base, C // 4)], sems.at[half]))
        copies[-1].start()
    for copy in copies:
        copy.wait()


def dft_rows():
    order = np.arange(M).reshape(LATS, 1, MD)
    order = np.broadcast_to(order, (LATS, 2, MD)).reshape(-1)
    part = np.broadcast_to(np.arange(2).reshape(1, 2, 1), (LATS, 2, MD)).reshape(-1)
    angle = 2.0 * np.pi / NLON * ((order[:, None] * np.arange(NLON)[None, :]) % NLON)
    angle = angle.astype(np.float32)
    rows = np.where(part[:, None] == 0, np.cos(angle), -np.sin(angle))
    padded = np.zeros((2 * M, LONS, FP), np.float32)
    padded[:, :, :FD] = rows.reshape(2 * M, LONS, FD)
    return padded.reshape(2 * M, LONS * FP).astype(ml_dtypes.bfloat16)


def packing():
    pack = np.zeros((CD * TP, CD * TP), np.float32)
    for c in range(CD):
        for t in range(TD):
            pack[c * TP + t, c * TD + t] = 1.0
    return pack.astype(ml_dtypes.bfloat16)


def latitudes():
    angle = ((np.arange(NLAT) + 0.5) * (np.pi / NLAT)).reshape(LATS, TD)
    cosine = np.zeros((LATS, TP), np.float32)
    logsine = np.zeros((LATS, TP), np.float32)
    cosine[:, :TD] = np.cos(angle)
    logsine[:, :TD] = np.log(np.sin(angle))
    half = LATS // 2
    return cosine[:half].reshape(1, -1), logsine[:half].reshape(1, -1)


def seed_logs():
    degree = np.arange(M, dtype=np.float64)
    steps = np.log((2.0 * degree + 1.0) / (2.0 * degree + 2.0))
    prefix = np.concatenate([np.zeros(1), np.cumsum(steps)[:-1]])
    return (0.5 * np.log((2.0 * degree + 1.0) / (4.0 * np.pi)) + 0.5 * prefix).astype(np.float32)


def band_lanes():
    mark = np.zeros((TD, 3, 256), np.float32)
    for t in range(TD):
        for rr in range(3):
            start = (t % QUAD + rr) * XW
            mark[t, rr, start:start + XW] = 1.0
    return mark


def tap_rows(taps, offsets, counts, first_row):
    slot_ids = lax.broadcasted_iota(jnp.int32, taps.shape, 3)
    live = jnp.where(slot_ids < counts[:, None, None, None], taps, 0.0).astype(BF16).astype(F32)
    shift = (R - offsets).astype(F32)[:, None]
    both = jnp.concatenate([live, shift], axis=1)
    both = jnp.pad(both, ((1, 1), (0, 0), (0, 0), (0, 0)))
    return lax.dynamic_slice_in_dim(both, first_row, TD + 2, 0)


def tap_table(both):
    marks = band_lanes()
    table = 0.0
    for rr in range(3):
        mine = both[rr:rr + TD, :, 2 - rr, :].reshape(TD, (K + 1) * S)
        table = table + mine[:, :, None] * marks[:, rr][:, None, :]
    return table


def on_device(field, cotangent, mix_weight, taps, offsets, counts):
    lat_pos = lax.axis_index(LAT)
    up = [(i, (i + 1) % LONS) for i in range(LONS)]
    down = [(j, i) for i, j in up]
    left = lax.ppermute(cotangent[:, FD - R:], LON, up)
    right = lax.ppermute(cotangent[:, :R], LON, down)
    edge_rows = [
        jnp.concatenate([left[t:t + 1], cotangent[t:t + 1], right[t:t + 1]], axis=1) for t in (0, TD - 1)
    ]
    north = [(i, i + 1) for i in range(LATS - 1)]
    south = [(j, i) for i, j in north]
    top = lax.ppermute(edge_rows[1], LAT, north)
    bottom = lax.ppermute(edge_rows[0], LAT, south)

    whole = pl.BlockSpec(memory_space=pltpu.VMEM)
    tap_part, _ = lax.optimization_barrier((tap_rows(taps, offsets, counts, lat_pos * TD), edge_rows))
    tab = tap_table(tap_part)
    cells = TD * FD
    core = jnp.reshape(lax.axis_index(CORE), (1,)).astype(jnp.int32)
    scalar = pl.BlockSpec(memory_space=pltpu.SMEM)
    anywhere = pl.BlockSpec(memory_space=pl.ANY)
    half = (C // 2, K * C)
    rims = (near(left), near(right))
    near_cot, near_field = near(cotangent), near(field.reshape(cells, C))
    scratch = [pltpu.VMEM((TD + 2, XW, C), F32), pltpu.VMEM((K * ROWS, 256), F32)]
    mix_near = near(mix_weight)
    field_inner, mix_inner = call(
        inner_kernel,
        (near_shape((INNER * ROWS, C), F32), near_shape((C, K * C), F32)),
        2,
        in_specs=[whole] * 6,
        scratch_shapes=[pltpu.VMEM((INNER * ROWS, K * C), BF16)] + scratch,
        name="stencil_inner",
    )(near(tab), near_cot, *rims, near_field, mix_near)
    pack = near(jnp.asarray(packing()))
    top, bottom, pack = lax.optimization_barrier((top, bottom, pack))
    g_outer, mix_mine, mix_other = call(
        outer_kernel,
        (near_shape((2 * ROWS, K * C), BF16), near_shape(half, F32), near_shape(half, BF16)),
        2,
        in_specs=[scalar] + [whole] * 8,
        scratch_shapes=scratch,
        name="stencil_outer",
    )(core, near(tab), near_cot, *rims, near(top), near(bottom), near_field, near(mix_inner))
    swap = [(0, 1), (1, 0)]
    mix_other = lax.ppermute(mix_other, CORE, swap)

    pos = jnp.reshape(lat_pos, (1,)).astype(jnp.int32)
    grad_field, send = call(
        field_kernel,
        (shape((cells, C), BF16), shape((LONS, SENT, 128), BF16)),
        5,
        in_specs=[scalar] + [whole] * 5,
        scratch_shapes=[
            pltpu.VMEM((C // 128, cells, 128), F32),
            pltpu.VMEM((FD // 4, C, 128), F32),
            pltpu.VMEM((CD // 4, LONS * FD, 128), F32),
        ],
        name="grad_field",
    )(pos, near(field_inner), near(g_outer), near(cotangent.reshape(cells, C)), near(mix_near), near(pack))
    send = call(
        chip_sum_kernel,
        shape((LONS, SENT, 128), BF16),
        2,
        in_specs=[whole, whole, anywhere],
        out_specs=anywhere,
        scratch_shapes=[
            pltpu.VMEM((GROUPS, LONS, FP - FD, 128), BF16),
            pltpu.VMEM((LONS, REST_ROW - GROUPS * FP, 128), BF16),
            pltpu.SemaphoreType.DMA((GROUPS + 1,)),
        ],
        input_output_aliases={2: 0},
        name="mix_chip_sum",
    )(near(mix_mine), near(mix_other), send)
    columns = lax.all_to_all(send, LON, 0, 0, tiled=True)

    cosine, logsine = latitudes()
    first_order = lat_pos * MD
    seeds = lax.dynamic_slice_in_dim(jnp.asarray(seed_logs()), first_order, MD, 0)
    orders = (first_order + jnp.arange(MD, dtype=jnp.int32)).astype(F32)
    logscale = seeds[:, None] + orders[:, None] * logsine
    logscale, _ = lax.optimization_barrier((logscale, send))
    table = call(
        legendre_kernel,
        shape((MD // 2, L, 2 * HALF), BF16),
        9,
        grid_spec=pltpu.PrefetchScalarGridSpec(
            num_scalar_prefetch=1,
            grid=(L // LB,),
            in_specs=[
                pl.BlockSpec((1, HALF), lambda b, pos: (0, 0)),
                pl.BlockSpec((MD, HALF), lambda b, pos: (0, 0)),
            ],
            out_specs=pl.BlockSpec((MD // 2, LB, 2 * HALF), lambda b, pos: (0, b, 0)),
            scratch_shapes=[
                pltpu.VMEM((MD, 128), F32),
                pltpu.VMEM((MD, HALF), F32),
                pltpu.VMEM((MD, HALF), F32),
                pltpu.VMEM((MD, HALF), F32),
                pltpu.VMEM((LB * MD, HALF), F32),
            ],
        ),
        name="legendre",
    )(pos, jnp.asarray(cosine), logscale)
    columns, table = lax.optimization_barrier((columns, table))

    spectra = call(dft_kernel, near_shape((LATS, SPREAD, 128), BF16), 2, in_specs=[whole, whole], name="dft")(
        near(jnp.asarray(dft_rows())), near(columns)
    )
    spec = lax.all_to_all(spectra, LAT, 0, 0, tiled=True)
    mix_copies = call(copies_kernel, near_shape((CHIPS, 2 * SLOTS * 8, 128), BF16), 2, in_specs=[whole], name="mix_copies")(near(spec))
    mix_mine = lax.all_to_all(mix_copies, CHIP, 0, 0, tiled=True)

    grad_spectra = call(
        synthesis_kernel,
        shape((2, CD, MD, L), F32),
        6,
        grid_spec=pltpu.PrefetchScalarGridSpec(
            num_scalar_prefetch=0,
            grid=(MD // MSTEP,),
            in_specs=[
                whole,
                whole,
                pl.BlockSpec((MSTEP // 2, L, 2 * HALF), lambda b: (b, 0, 0)),
            ],
            out_specs=pl.BlockSpec((2, CD, MSTEP, L), lambda b: (0, 0, b, 0)),
            scratch_shapes=[
                pltpu.VMEM((4 * CD * MD, HALF), F32),
                pltpu.VMEM((L // 128, 2 * CD * MSTEP, 128), F32),
            ],
        ),
        name="synthesis",
    )(near(spec), near(pack), table)
    mix_mine, grad_spectra = lax.optimization_barrier((mix_mine, grad_spectra))
    mix_other = lax.ppermute(mix_mine, CORE, swap)
    grad_mix = ()
    for held, parts in ((core, mix_mine), (1 - core, mix_other)):
        grad_mix = (
            call(
                mix_kernel,
                shape((K, C, C), F32),
                1,
                in_specs=[scalar, whole] + [anywhere] * len(grad_mix),
                out_specs=anywhere,
                scratch_shapes=[pltpu.VMEM((2, K, C // 4, C), F32), pltpu.SemaphoreType.DMA((2,))],
                input_output_aliases={2: 0} if grad_mix else {},
                name="mix_out",
            )(held, near(parts), *grad_mix),
        )
    return (grad_field.reshape(TD, FD, C), jnp.transpose(grad_spectra, (0, 2, 1, 3)), grad_mix[0])


def solution(mesh):
    chips = Mesh(mesh.devices.reshape(LATS, CHIPS, 2), (LAT, CHIP, CORE))
    placed = (P(LAT, LON, None), P(LAT, LON, None), P(), P(), P(), P())
    return jax.shard_map(
        on_device,
        mesh=chips,
        in_specs=placed,
        out_specs=(P(LAT, LON, None), P(None, LAT, LON, None), P()),
        check_vma=False,
    )
```

```python
import functools
import math

import jax
import jax.numpy as jnp
import ml_dtypes
import numpy as np
from jax import lax
from jax.experimental import pallas as pl
from jax.experimental.pallas import tpu as pltpu
from jax.sharding import Mesh, PartitionSpec as P

C = 384
M = 384
L = 384
K = 3
R = 8
S = 8
LB = 32
NLAT = 192
NLON = 768
LATS = 8
LONS = 32
TD = NLAT // LATS
FD = NLON // LONS
CD = C // LONS
MD = M // LATS
XW = FD + 2 * R
TP = 32
FP = FD + 8
COLS = CD * TD
GROUPS = COLS // 128
REST = COLS - GROUPS * 128
SLOTS = 7
REST_ROW = GROUPS * FP + (SLOTS - GROUPS) * 8
SENT = REST_ROW + 8
TAIL_ROW = GROUPS * 2 * MD + 2 * MD * REST // 128
SPREAD = TAIL_ROW + 2 * SLOTS * 8
QUAD = 4
CHIPS = LONS // 2
LAT = "lat"
CHIP = "chip"
CORE = "core"
LON = (CHIP, CORE)
F32 = jnp.float32
BF16 = jnp.bfloat16
VMEM_BYTES = 18 * 1024 * 1024


def call(kernel, out_shape, us, **kw):
    return pl.pallas_call(
        kernel,
        out_shape=out_shape,
        cost_estimate=pl.CostEstimate(flops=int(us * 1.1e9), bytes_accessed=int(us * 3.0e6), transcendentals=0),
        compiler_params=pltpu.CompilerParams(vmem_limit_bytes=VMEM_BYTES),
        **kw,
    )


def near(array):
    return pltpu.with_memory_space_constraint(array, pltpu.VMEM)


def shape(dims, dtype):
    return jax.ShapeDtypeStruct(dims, dtype)


def near_shape(dims, dtype):
    return pltpu.VMEM(dims, dtype)


def swap_blocks(parts):
    lane = lax.broadcasted_iota(jnp.int32, parts[0].shape, 1)
    low = lane < 64
    even = (lane & 32) == 0
    a0, a1, a2, a3 = parts
    b0 = jnp.where(low, a0, pltpu.roll(a2, 64, 1))
    b2 = jnp.where(low, pltpu.roll(a0, 64, 1), a2)
    b1 = jnp.where(low, a1, pltpu.roll(a3, 64, 1))
    b3 = jnp.where(low, pltpu.roll(a1, 64, 1), a3)
    c0 = jnp.where(even, b0, pltpu.roll(b1, 32, 1))
    c1 = jnp.where(even, pltpu.roll(b0, 96, 1), b1)
    c2 = jnp.where(even, b2, pltpu.roll(b3, 32, 1))
    c3 = jnp.where(even, pltpu.roll(b2, 96, 1), b3)
    return c0, c1, c2, c3


ROWS = QUAD * FD
INNER = TD // QUAD - 2


def widen(ext, rows, cot, left, right):
    there = slice(rows.start + 1, rows.stop + 1)
    ext[there, 0:R, :] = left[rows].astype(F32)
    ext[there, R:R + FD, :] = cot[rows].astype(F32)
    ext[there, R + FD:XW, :] = right[rows].astype(F32)


def edge_kernel(cot, left, right, first, last):
    for row, out in ((0, first), (TD - 1, last)):
        pieces = [part[row:row + 1].astype(F32) for part in (left, cot, right)]
        out[...] = jnp.concatenate(pieces, axis=1).astype(BF16)


def offsets_in_band():
    lane = lax.broadcasted_iota(jnp.int32, (FD, 256), 1)
    column = lane
    for edge in range(1, QUAD + 2):
        column = column - jnp.where(lane >= edge * XW, XW, 0)
    return (column - lax.broadcasted_iota(jnp.int32, (FD, 256), 0)).astype(F32)


def stencil_quad(quad, apart, tab, ext, band):
    zero = jnp.zeros((FD, 256), F32)
    for r in range(QUAD):
        t = quad * QUAD + r
        sums = [zero] * K
        for s in range(S):
            hit = apart == tab[t, K * S + s:K * S + s + 1, :]
            for k in range(K):
                sums[k] = sums[k] + jnp.where(hit, tab[t, k * S + s:k * S + s + 1, :], 0.0)
        for k in range(K):
            row = (k * QUAD + r) * FD
            band[row:row + FD, :] = sums[k]
    slab = ext[quad * QUAD:quad * QUAD + QUAD + 2].reshape((QUAD + 2) * XW, C).astype(BF16)
    weights = band[:, :(QUAD + 2) * XW].astype(BF16)
    return jnp.dot(weights, slab, preferred_element_type=F32).astype(BF16)


def cells_dot(field, g):
    return lax.dot_general(field, g, (((0,), (0,)), ((), ())), preferred_element_type=F32)


def weigh(g, mix):
    total = jnp.zeros((g.shape[0], C), F32)
    for k in range(K):
        total = total + lax.dot_general(
            g[:, k * C:(k + 1) * C], mix[k], (((1,), (1,)), ((), ())), preferred_element_type=F32
        )
    return total


def inner_kernel(tab, cot, left, right, field, mix, field_out, mix_out, g_out, ext, band):
    widen(ext, slice(QUAD - 1, TD - QUAD + 1), cot, left, right)
    apart = offsets_in_band()
    for n in range(INNER):
        got = stencil_quad(n + 1, apart, tab, ext, band)
        for k in range(K):
            g_out[n * ROWS:(n + 1) * ROWS, k * C:(k + 1) * C] = got[k * ROWS:(k + 1) * ROWS]
    mix_out[...] = cells_dot(field[ROWS:(INNER + 1) * ROWS, :], g_out[...])
    field_out[...] = weigh(g_out, mix)


def outer_kernel(core, tab, cot, left, right, top, bottom, field, mix_inner, g_out, mine_out, other_out, ext, band):
    widen(ext, slice(0, QUAD + 1), cot, left, right)
    widen(ext, slice(TD - QUAD - 1, TD), cot, left, right)
    ext[0:1] = top[...].astype(F32)
    ext[TD + 1:TD + 2] = bottom[...].astype(F32)
    apart = offsets_in_band()
    for n in range(2):
        got = stencil_quad(n * (INNER + 1), apart, tab, ext, band)
        for k in range(K):
            g_out[n * ROWS:(n + 1) * ROWS, k * C:(k + 1) * C] = got[k * ROWS:(k + 1) * ROWS]
    mine = jnp.concatenate([field[:ROWS, :], field[(INNER + 1) * ROWS:, :]], axis=0)
    mix = (mix_inner[...] + cells_dot(mine, g_out[...])) * (1.0 / math.sqrt(NLAT * NLON))
    first = core[0] == 0
    low, high = mix[:C // 2], mix[C // 2:]
    mine_out[...] = jnp.where(first, low, high)
    other_out[...] = jnp.where(first, high, low).astype(BF16)


def field_kernel(pos, inner, g_outer, cot, mix, pack, gf_out, send_out, flat, turned, send):
    outer = weigh(g_outer, mix)
    total = cot[...].astype(F32) + jnp.concatenate([outer[:ROWS], inner[...], outer[ROWS:]], axis=0)
    rounded = total.astype(BF16)
    gf_out[...] = rounded
    rounded = rounded.astype(F32)
    southern = pos[0] >= LATS // 2
    for t in range(TD):
        row = pl.multiple_of(jnp.where(southern, TD - 1 - t, t) * FD, FD)
        for h in range(C // 128):
            flat[h, pl.ds(row, FD), :] = rounded[t * FD:(t + 1) * FD, h * 128:(h + 1) * 128]
    pad = jnp.zeros((TP - TD, 128), F32)
    for fq in range(FD // 4):
        for h in range(C // 128):
            pieces = []
            for fr in range(4):
                pieces.append(flat[h, pl.ds(fq * 4 + fr, TD, stride=FD), :])
                pieces.append(pad)
            turned[fq, h * 128:(h + 1) * 128, :] = jnp.concatenate(pieces, axis=0).T
    for fq in range(FD // 4):
        for q in range(CD // 4):
            parts = [
                turned[fq, pl.ds(q * 4 + cr, LONS, stride=CD), :] for cr in range(4)
            ]
            for fr, part in enumerate(swap_blocks(parts)):
                send[q, pl.ds(fq * 4 + fr, LONS, stride=FD), :] = part
    padded = jnp.concatenate([send[q] for q in range(CD // 4)], axis=1).astype(BF16)
    packed = jnp.dot(padded, pack[...], preferred_element_type=F32)
    for q in range(GROUPS):
        send_out[:, q * FP:q * FP + FD, :] = packed[:, q * 128:(q + 1) * 128].reshape(LONS, FD, 128).astype(BF16)
    last = packed[:, GROUPS * 128:].reshape(LONS, FD // 8, 8, 128)
    rest = last[:, 0]
    for b in range(1, FD // 8):
        rest = rest + pltpu.roll(last[:, b], b * REST, 2)
    send_out[:, REST_ROW - 8:, :] = jnp.concatenate([jnp.zeros_like(rest), rest], axis=1).astype(BF16)


def slot_row(slot):
    return slot * FP + FD if slot < GROUPS else GROUPS * FP + (slot - GROUPS) * 8


def piece_row(piece):
    return TAIL_ROW + piece * 8


def dft_kernel(rows, columns, out):
    parts = [columns[:, q * FP:(q + 1) * FP, :].reshape(LONS * FP, 128) for q in range(GROUPS)]
    rest = columns[:, REST_ROW - 8:, :].astype(F32)[:, 8:]
    blocks = [rest if b == 0 else pltpu.roll(rest, 128 - b * REST, 2) for b in range(FD // 8)]
    blocks.append(jnp.zeros_like(rest))
    parts.append(jnp.concatenate(blocks, axis=1).reshape(LONS * FP, 128).astype(BF16))
    got = jnp.dot(rows[...], jnp.concatenate(parts, axis=1), preferred_element_type=F32)
    got = got * (1.0 / math.sqrt(NLON))
    pieces = []
    for half in range(2):
        for slot in range(SLOTS):
            first = slot_row(slot) // 16 * 16
            start = slot_row(slot) - first
            total = columns[half, first:first + 16, :].astype(F32)
            for chip in range(1, CHIPS):
                total = total + columns[2 * chip + half, first:first + 16, :].astype(F32)
            pieces.append(total[start:start + 8])
    step = 2 * MD * REST // 128
    inside = lax.broadcasted_iota(jnp.int32, (step, 128), 1) < REST
    for i in range(LATS):
        mine = got[i * 2 * MD:(i + 1) * 2 * MD]
        for q in range(GROUPS):
            out[i, q * 2 * MD:(q + 1) * 2 * MD, :] = mine[:, q * 128:(q + 1) * 128].astype(BF16)
        quarters = [
            jnp.where(inside, mine[b * step:(b + 1) * step, GROUPS * 128:], 0.0) for b in range(128 // REST)
        ]
        rest = quarters[0]
        for b in range(1, 128 // REST):
            rest = rest + pltpu.roll(quarters[b], b * REST, 1)
        out[i, GROUPS * 2 * MD:, :] = jnp.concatenate([rest] + pieces, axis=0).astype(BF16)


HALF = LATS // 2 * TP


def legendre_kernel(pos, cosines, logscale, out, coef, prev_s, early_s, scale_s, rows):
    block = pl.program_id(0)
    order = pos[0] * MD + lax.broadcasted_iota(jnp.int32, (MD, 128), 0)
    order_f = order.astype(F32)

    @pl.when(block == 0)
    def _():
        prev_s[...] = jnp.zeros_like(prev_s)
        early_s[...] = jnp.zeros_like(early_s)
        scale_s[...] = logscale[...]

    lane = lax.broadcasted_iota(jnp.int32, (MD, 128), 1)
    degree = block * LB + (lane & (LB - 1))
    deg_f = degree.astype(F32)
    higher = degree > order
    lower_a = jnp.where(higher, deg_f * deg_f - order_f * order_f, 1.0)
    factor_a = jnp.where(higher, jnp.sqrt((4.0 * deg_f * deg_f - 1.0) / lower_a), 0.0)
    before = deg_f - 1.0
    upper_b = jnp.maximum(before * before - order_f * order_f, 0.0)
    lower_b = jnp.maximum(4.0 * before * before - 1.0, 1.0)
    factor_b = jnp.sqrt(upper_b / lower_b)
    coef[...] = jnp.where(lane < LB, factor_a, factor_b)

    x = jnp.broadcast_to(cosines[...], (MD, 128))
    prev = prev_s[...]
    early = early_s[...]
    factor = jnp.exp(scale_s[...])
    for step in range(LB):
        a = jnp.broadcast_to(coef[:, step:step + 1], (MD, 128))
        b = jnp.broadcast_to(coef[:, LB + step:LB + step + 1], (MD, 128))
        seed = jnp.where(order == block * LB + step, 1.0, 0.0)
        fresh = a * (x * prev - b * early) + seed
        rows[step * MD:(step + 1) * MD, :] = fresh * factor
        early, prev = prev, fresh
    biggest = jnp.maximum(jnp.abs(prev), jnp.abs(early))
    divisor = jnp.where(biggest > 0.0, biggest, 1.0)
    prev_s[...] = prev / divisor
    early_s[...] = early / divisor
    scale_s[...] = scale_s[...] + jnp.log(divisor)
    for m in range(MD):
        side = (m % 2) * 128
        out[m // 2, :, side:side + 128] = rows[pl.ds(m, LB, stride=MD), :].astype(BF16)


MSTEP = 8


def synthesis_kernel(spec, pack, leg, out, lined, rows):
    step = pl.program_id(0)

    @pl.when(step == 0)
    def _():
        packed = []
        for i in range(LATS):
            groups = [spec[i, q * 2 * MD:(q + 1) * 2 * MD, :] for q in range(GROUPS)]
            rest = spec[i, GROUPS * 2 * MD:GROUPS * 2 * MD + 32, :].astype(F32)[:2 * MD * REST // 128]
            blocks = [rest if b == 0 else pltpu.roll(rest, 128 - b * REST, 1) for b in range(128 // REST)]
            groups.append(jnp.concatenate(blocks, axis=0).astype(BF16))
            packed.append(jnp.concatenate(groups, axis=1))
        padded = lax.dot_general(
            jnp.concatenate(packed, axis=0), pack[...], (((1,), (1,)), ((), ())), preferred_element_type=F32
        )
        padded = [padded[i * 2 * MD:(i + 1) * 2 * MD] for i in range(LATS)]
        for q in range(CD // 4):
            span = slice(q * 128, (q + 1) * 128)
            north = [padded[i][:, span] for i in range(LATS // 2)]
            south = [padded[LATS - 1 - i][:, span] for i in range(LATS // 2)]
            for odd in range(2):
                parts = [n - s if odd else n + s for n, s in zip(north, south)]
                for cr, part in enumerate(swap_blocks(parts)):
                    for p in range(2):
                        base = ((odd * 2 + p) * CD + q * 4 + cr) * MD
                        lined[base:base + MD, :] = part[p * MD:(p + 1) * MD]

    wide = 2 * CD
    odd_lane = (lax.broadcasted_iota(jnp.int32, (wide, L), 1) & 1) == 1
    zero = jnp.zeros((2 * wide, HALF), F32)
    for pair in range(MSTEP // 2):
        first = step * MSTEP + 2 * pair
        mine = [lined[pl.ds(first + side, 2 * wide, stride=MD), :] for side in range(2)]
        lhs = jnp.concatenate(
            [jnp.concatenate([mine[0], zero], axis=1), jnp.concatenate([zero, mine[1]], axis=1)], axis=0
        ).astype(BF16)
        got = lax.dot_general(
            lhs, leg[pair], (((1,), (1,)), ((), ())), preferred_element_type=F32
        ) * math.sqrt(4.0 * math.pi / NLAT)
        done = [
            jnp.where(odd_lane, got[wide:2 * wide], got[:wide]),
            jnp.where(odd_lane, got[2 * wide:3 * wide], got[3 * wide:]),
        ]
        for side in range(2):
            for h in range(L // 128):
                rows[h, pl.ds(2 * pair + side, wide, stride=MSTEP), :] = done[side][:, h * 128:(h + 1) * 128]
    for p in range(2):
        for c in range(CD):
            base = (p * CD + c) * MSTEP
            for h in range(L // 128):
                out[p, c, :, h * 128:(h + 1) * 128] = rows[h, base:base + MSTEP, :]


HALF_TILES = C // 32 * (K * C // 128)


def tiles_of(chip):
    return [(slot, *divmod(SLOTS * chip + slot, K * C // 128)) for slot in range(SLOTS) if SLOTS * chip + slot < HALF_TILES]


def chip_sum_kernel(mine, other, send, out, near_rows, far_rows, sems):
    total = (mine[...] + other[...].astype(F32)).astype(BF16)
    near_rows[...] = jnp.zeros_like(near_rows)
    far_rows[...] = jnp.zeros_like(far_rows)
    for chip in range(CHIPS):
        for slot, row, col in tiles_of(chip):
            for core in range(2):
                first = core * (C // 4) + row * 8
                tile = total[first:first + 8, col * 128:(col + 1) * 128]
                if slot < GROUPS:
                    near_rows[slot, 2 * chip + core] = tile
                else:
                    far = (slot - GROUPS) * 8
                    far_rows[2 * chip + core, far:far + 8, :] = tile
    copies = [
        pltpu.make_async_copy(near_rows.at[q], out.at[:, q * FP + FD:(q + 1) * FP, :], sems.at[q]) for q in range(GROUPS)
    ]
    copies.append(pltpu.make_async_copy(far_rows, out.at[:, GROUPS * FP:REST_ROW, :], sems.at[GROUPS]))
    for copy in copies:
        copy.start()
    for copy in copies:
        copy.wait()


def copies_kernel(spec, out):
    for piece in range(2 * SLOTS):
        row = piece_row(piece)
        first = row // 16 * 16
        total = spec[0, first:first + 16, :].astype(F32)
        for i in range(1, LATS):
            total = total + spec[i, first:first + 16, :].astype(F32)
        total = total[row - first:row - first + 8].astype(BF16)
        for chip in range(CHIPS):
            out[chip, piece * 8:(piece + 1) * 8, :] = total


def mix_kernel(held, parts, *rest):
    out, rows, sems = rest[-3:]
    copies = []
    for half in range(2):
        for chip in range(CHIPS):
            for slot, row, col in tiles_of(chip):
                k, d = divmod(col, C // 128)
                piece = (half * SLOTS + slot) * 8
                rows[half, k, row * 8:row * 8 + 8, d * 128:(d + 1) * 128] = parts[chip, piece:piece + 8, :].astype(F32)
        base = pl.multiple_of(half * (C // 2) + held[0] * (C // 4), 8)
        copies.append(pltpu.make_async_copy(rows.at[half], out.at[:, pl.ds(base, C // 4)], sems.at[half]))
        copies[-1].start()
    for copy in copies:
        copy.wait()


def dft_rows():
    order = np.arange(M).reshape(LATS, 1, MD)
    order = np.broadcast_to(order, (LATS, 2, MD)).reshape(-1)
    part = np.broadcast_to(np.arange(2).reshape(1, 2, 1), (LATS, 2, MD)).reshape(-1)
    angle = 2.0 * np.pi / NLON * ((order[:, None] * np.arange(NLON)[None, :]) % NLON)
    angle = angle.astype(np.float32)
    rows = np.where(part[:, None] == 0, np.cos(angle), -np.sin(angle))
    padded = np.zeros((2 * M, LONS, FP), np.float32)
    padded[:, :, :FD] = rows.reshape(2 * M, LONS, FD)
    return padded.reshape(2 * M, LONS * FP).astype(ml_dtypes.bfloat16)


def packing():
    pack = np.zeros((CD * TP, CD * TP), np.float32)
    for c in range(CD):
        for t in range(TD):
            pack[c * TP + t, c * TD + t] = 1.0
    return pack.astype(ml_dtypes.bfloat16)


def latitudes():
    angle = ((np.arange(NLAT) + 0.5) * (np.pi / NLAT)).reshape(LATS, TD)
    cosine = np.zeros((LATS, TP), np.float32)
    logsine = np.zeros((LATS, TP), np.float32)
    cosine[:, :TD] = np.cos(angle)
    logsine[:, :TD] = np.log(np.sin(angle))
    half = LATS // 2
    return cosine[:half].reshape(1, -1), logsine[:half].reshape(1, -1)


def seed_logs():
    degree = np.arange(M, dtype=np.float64)
    steps = np.log((2.0 * degree + 1.0) / (2.0 * degree + 2.0))
    prefix = np.concatenate([np.zeros(1), np.cumsum(steps)[:-1]])
    return (0.5 * np.log((2.0 * degree + 1.0) / (4.0 * np.pi)) + 0.5 * prefix).astype(np.float32)


def band_lanes():
    mark = np.zeros((TD, 3, 256), np.float32)
    for t in range(TD):
        for rr in range(3):
            start = (t % QUAD + rr) * XW
            mark[t, rr, start:start + XW] = 1.0
    return mark


def tap_rows(taps, offsets, counts, first_row):
    slot_ids = lax.broadcasted_iota(jnp.int32, taps.shape, 3)
    live = jnp.where(slot_ids < counts[:, None, None, None], taps, 0.0).astype(BF16).astype(F32)
    shift = (R - offsets).astype(F32)[:, None]
    both = jnp.concatenate([live, shift], axis=1)
    both = jnp.pad(both, ((1, 1), (0, 0), (0, 0), (0, 0)))
    return lax.dynamic_slice_in_dim(both, first_row, TD + 2, 0)


def tap_table(both):
    marks = band_lanes()
    table = 0.0
    for rr in range(3):
        mine = both[rr:rr + TD, :, 2 - rr, :].reshape(TD, (K + 1) * S)
        table = table + mine[:, :, None] * marks[:, rr][:, None, :]
    return table


def on_device(field, cotangent, mix_weight, taps, offsets, counts):
    lat_pos = lax.axis_index(LAT)
    up = [(i, (i + 1) % LONS) for i in range(LONS)]
    down = [(j, i) for i, j in up]
    left = lax.ppermute(cotangent[:, FD - R:], LON, up)
    right = lax.ppermute(cotangent[:, :R], LON, down)
    whole = pl.BlockSpec(memory_space=pltpu.VMEM)
    near_cot, rims = near(cotangent), (near(left), near(right))
    edge = (1, XW, C)
    edge_rows = call(
        edge_kernel,
        (near_shape(edge, BF16), near_shape(edge, BF16)),
        1,
        in_specs=[whole] * 3,
        name="edge_rows",
    )(near_cot, *rims)
    north = [(i, i + 1) for i in range(LATS - 1)]
    south = [(j, i) for i, j in north]
    top = lax.ppermute(edge_rows[1], LAT, north)
    bottom = lax.ppermute(edge_rows[0], LAT, south)

    tap_part, _ = lax.optimization_barrier((tap_rows(taps, offsets, counts, lat_pos * TD), edge_rows))
    tab = tap_table(tap_part)
    cells = TD * FD
    core = jnp.reshape(lax.axis_index(CORE), (1,)).astype(jnp.int32)
    scalar = pl.BlockSpec(memory_space=pltpu.SMEM)
    anywhere = pl.BlockSpec(memory_space=pl.ANY)
    half = (C // 2, K * C)
    near_field = near(field.reshape(cells, C))
    scratch = [pltpu.VMEM((TD + 2, XW, C), F32), pltpu.VMEM((K * ROWS, 256), F32)]
    mix_near = near(mix_weight)
    field_inner, mix_inner = call(
        inner_kernel,
        (near_shape((INNER * ROWS, C), F32), near_shape((C, K * C), F32)),
        2,
        in_specs=[whole] * 6,
        scratch_shapes=[pltpu.VMEM((INNER * ROWS, K * C), BF16)] + scratch,
        name="stencil_inner",
    )(near(tab), near_cot, *rims, near_field, mix_near)
    pack = near(jnp.asarray(packing()))
    top, bottom, pack = lax.optimization_barrier((top, bottom, pack))
    g_outer, mix_mine, mix_other = call(
        outer_kernel,
        (near_shape((2 * ROWS, K * C), BF16), near_shape(half, F32), near_shape(half, BF16)),
        2,
        in_specs=[scalar] + [whole] * 8,
        scratch_shapes=scratch,
        name="stencil_outer",
    )(core, near(tab), near_cot, *rims, near(top), near(bottom), near_field, near(mix_inner))
    swap = [(0, 1), (1, 0)]
    mix_other = lax.ppermute(mix_other, CORE, swap)

    pos = jnp.reshape(lat_pos, (1,)).astype(jnp.int32)
    grad_field, send = call(
        field_kernel,
        (shape((cells, C), BF16), shape((LONS, SENT, 128), BF16)),
        5,
        in_specs=[scalar] + [whole] * 5,
        scratch_shapes=[
            pltpu.VMEM((C // 128, cells, 128), F32),
            pltpu.VMEM((FD // 4, C, 128), F32),
            pltpu.VMEM((CD // 4, LONS * FD, 128), F32),
        ],
        name="grad_field",
    )(pos, near(field_inner), near(g_outer), near(cotangent.reshape(cells, C)), near(mix_near), near(pack))
    send = call(
        chip_sum_kernel,
        shape((LONS, SENT, 128), BF16),
        2,
        in_specs=[whole, whole, anywhere],
        out_specs=anywhere,
        scratch_shapes=[
            pltpu.VMEM((GROUPS, LONS, FP - FD, 128), BF16),
            pltpu.VMEM((LONS, REST_ROW - GROUPS * FP, 128), BF16),
            pltpu.SemaphoreType.DMA((GROUPS + 1,)),
        ],
        input_output_aliases={2: 0},
        name="mix_chip_sum",
    )(near(mix_mine), near(mix_other), send)
    columns = lax.all_to_all(send, LON, 0, 0, tiled=True)

    cosine, logsine = latitudes()
    first_order = lat_pos * MD
    seeds = lax.dynamic_slice_in_dim(jnp.asarray(seed_logs()), first_order, MD, 0)
    orders = (first_order + jnp.arange(MD, dtype=jnp.int32)).astype(F32)
    logscale = seeds[:, None] + orders[:, None] * logsine
    logscale, _ = lax.optimization_barrier((logscale, send))
    table = call(
        legendre_kernel,
        shape((MD // 2, L, 2 * HALF), BF16),
        9,
        grid_spec=pltpu.PrefetchScalarGridSpec(
            num_scalar_prefetch=1,
            grid=(L // LB,),
            in_specs=[
                pl.BlockSpec((1, HALF), lambda b, pos: (0, 0)),
                pl.BlockSpec((MD, HALF), lambda b, pos: (0, 0)),
            ],
            out_specs=pl.BlockSpec((MD // 2, LB, 2 * HALF), lambda b, pos: (0, b, 0)),
            scratch_shapes=[
                pltpu.VMEM((MD, 128), F32),
                pltpu.VMEM((MD, HALF), F32),
                pltpu.VMEM((MD, HALF), F32),
                pltpu.VMEM((MD, HALF), F32),
                pltpu.VMEM((LB * MD, HALF), F32),
            ],
        ),
        name="legendre",
    )(pos, jnp.asarray(cosine), logscale)
    columns, table = lax.optimization_barrier((columns, table))

    spectra = call(dft_kernel, near_shape((LATS, SPREAD, 128), BF16), 2, in_specs=[whole, whole], name="dft")(
        near(jnp.asarray(dft_rows())), near(columns)
    )
    spec = lax.all_to_all(spectra, LAT, 0, 0, tiled=True)
    mix_copies = call(copies_kernel, near_shape((CHIPS, 2 * SLOTS * 8, 128), BF16), 2, in_specs=[whole], name="mix_copies")(near(spec))
    mix_mine = lax.all_to_all(mix_copies, CHIP, 0, 0, tiled=True)

    grad_spectra = call(
        synthesis_kernel,
        shape((2, CD, MD, L), F32),
        6,
        grid_spec=pltpu.PrefetchScalarGridSpec(
            num_scalar_prefetch=0,
            grid=(MD // MSTEP,),
            in_specs=[
                whole,
                whole,
                pl.BlockSpec((MSTEP // 2, L, 2 * HALF), lambda b: (b, 0, 0)),
            ],
            out_specs=pl.BlockSpec((2, CD, MSTEP, L), lambda b: (0, 0, b, 0)),
            scratch_shapes=[
                pltpu.VMEM((4 * CD * MD, HALF), F32),
                pltpu.VMEM((L // 128, 2 * CD * MSTEP, 128), F32),
            ],
        ),
        name="synthesis",
    )(near(spec), near(pack), table)
    mix_mine, grad_spectra = lax.optimization_barrier((mix_mine, grad_spectra))
    mix_other = lax.ppermute(mix_mine, CORE, swap)
    grad_mix = ()
    for held, parts in ((core, mix_mine), (1 - core, mix_other)):
        grad_mix = (
            call(
                mix_kernel,
                shape((K, C, C), F32),
                1,
                in_specs=[scalar, whole] + [anywhere] * len(grad_mix),
                out_specs=anywhere,
                scratch_shapes=[pltpu.VMEM((2, K, C // 4, C), F32), pltpu.SemaphoreType.DMA((2,))],
                input_output_aliases={2: 0} if grad_mix else {},
                name="mix_out",
            )(held, near(parts), *grad_mix),
        )
    return (grad_field.reshape(TD, FD, C), jnp.transpose(grad_spectra, (0, 2, 1, 3)), grad_mix[0])


def solution(mesh):
    chips = Mesh(mesh.devices.reshape(LATS, CHIPS, 2), (LAT, CHIP, CORE))
    placed = (P(LAT, LON, None), P(LAT, LON, None), P(), P(), P(), P())
    return jax.shard_map(
        on_device,
        mesh=chips,
        in_specs=placed,
        out_specs=(P(LAT, LON, None), P(None, LAT, LON, None), P()),
        check_vma=False,
    )
```

```python
import functools
import math

import jax
import jax.numpy as jnp
import ml_dtypes
import numpy as np
from jax import lax
from jax.experimental import pallas as pl
from jax.experimental.pallas import tpu as pltpu
from jax.sharding import Mesh, PartitionSpec as P

C = 384
M = 384
L = 384
K = 3
R = 8
S = 8
LB = 32
NLAT = 192
NLON = 768
LATS = 8
LONS = 32
TD = NLAT // LATS
FD = NLON // LONS
CD = C // LONS
MD = M // LATS
XW = FD + 2 * R
TP = 32
FP = FD + 8
COLS = CD * TD
GROUPS = COLS // 128
REST = COLS - GROUPS * 128
SLOTS = 7
REST_ROW = GROUPS * FP + (SLOTS - GROUPS) * 8
SENT = REST_ROW + 8
TAIL_ROW = GROUPS * 2 * MD + 2 * MD * REST // 128
SPREAD = TAIL_ROW + 2 * SLOTS * 8
QUAD = 4
CHIPS = LONS // 2
LAT = "lat"
CHIP = "chip"
CORE = "core"
LON = (CHIP, CORE)
F32 = jnp.float32
BF16 = jnp.bfloat16
VMEM_BYTES = 18 * 1024 * 1024


def call(kernel, out_shape, us, **kw):
    return pl.pallas_call(
        kernel,
        out_shape=out_shape,
        cost_estimate=pl.CostEstimate(flops=int(us * 1.1e9), bytes_accessed=int(us * 3.0e6), transcendentals=0),
        compiler_params=pltpu.CompilerParams(vmem_limit_bytes=VMEM_BYTES),
        **kw,
    )


def near(array):
    return pltpu.with_memory_space_constraint(array, pltpu.VMEM)


def shape(dims, dtype):
    return jax.ShapeDtypeStruct(dims, dtype)


def near_shape(dims, dtype):
    return pltpu.VMEM(dims, dtype)


def swap_blocks(parts):
    lane = lax.broadcasted_iota(jnp.int32, parts[0].shape, 1)
    low = lane < 64
    even = (lane & 32) == 0
    a0, a1, a2, a3 = parts
    b0 = jnp.where(low, a0, pltpu.roll(a2, 64, 1))
    b2 = jnp.where(low, pltpu.roll(a0, 64, 1), a2)
    b1 = jnp.where(low, a1, pltpu.roll(a3, 64, 1))
    b3 = jnp.where(low, pltpu.roll(a1, 64, 1), a3)
    c0 = jnp.where(even, b0, pltpu.roll(b1, 32, 1))
    c1 = jnp.where(even, pltpu.roll(b0, 96, 1), b1)
    c2 = jnp.where(even, b2, pltpu.roll(b3, 32, 1))
    c3 = jnp.where(even, pltpu.roll(b2, 96, 1), b3)
    return c0, c1, c2, c3


ROWS = QUAD * FD
INNER = TD // QUAD - 2


def widen(ext, rows, cot, left, right):
    there = slice(rows.start + 1, rows.stop + 1)
    ext[there, 0:R, :] = left[rows].astype(F32)
    ext[there, R:R + FD, :] = cot[rows].astype(F32)
    ext[there, R + FD:XW, :] = right[rows].astype(F32)


def edge_kernel(top, bottom, left, right, first, last):
    for row, own, out in ((0, top, first), (TD - 1, bottom, last)):
        pieces = [part.astype(F32) for part in (left[row:row + 1], own[...], right[row:row + 1])]
        out[...] = jnp.concatenate(pieces, axis=1).astype(BF16)


def offsets_in_band():
    lane = lax.broadcasted_iota(jnp.int32, (FD, 256), 1)
    column = lane
    for edge in range(1, QUAD + 2):
        column = column - jnp.where(lane >= edge * XW, XW, 0)
    return (column - lax.broadcasted_iota(jnp.int32, (FD, 256), 0)).astype(F32)


def stencil_quad(quad, apart, tab, ext, band):
    zero = jnp.zeros((FD, 256), F32)
    for r in range(QUAD):
        t = quad * QUAD + r
        sums = [zero] * K
        for s in range(S):
            hit = apart == tab[t, K * S + s:K * S + s + 1, :]
            for k in range(K):
                sums[k] = sums[k] + jnp.where(hit, tab[t, k * S + s:k * S + s + 1, :], 0.0)
        for k in range(K):
            row = (k * QUAD + r) * FD
            band[row:row + FD, :] = sums[k]
    slab = ext[quad * QUAD:quad * QUAD + QUAD + 2].reshape((QUAD + 2) * XW, C).astype(BF16)
    weights = band[:, :(QUAD + 2) * XW].astype(BF16)
    return jnp.dot(weights, slab, preferred_element_type=F32).astype(BF16)


def cells_dot(field, g):
    return lax.dot_general(field, g, (((0,), (0,)), ((), ())), preferred_element_type=F32)


def weigh(g, mix):
    total = jnp.zeros((g.shape[0], C), F32)
    for k in range(K):
        total = total + lax.dot_general(
            g[:, k * C:(k + 1) * C], mix[k], (((1,), (1,)), ((), ())), preferred_element_type=F32
        )
    return total


def inner_kernel(tab, cot, left, right, field, mix, field_out, mix_out, g_out, ext, band):
    widen(ext, slice(QUAD - 1, TD - QUAD + 1), cot, left, right)
    apart = offsets_in_band()
    for n in range(INNER):
        got = stencil_quad(n + 1, apart, tab, ext, band)
        for k in range(K):
            g_out[n * ROWS:(n + 1) * ROWS, k * C:(k + 1) * C] = got[k * ROWS:(k + 1) * ROWS]
    mix_out[...] = cells_dot(field[ROWS:(INNER + 1) * ROWS, :], g_out[...])
    field_out[...] = weigh(g_out, mix)


def outer_kernel(core, tab, cot, left, right, top, bottom, field, mix_inner, g_out, mine_out, other_out, ext, band):
    widen(ext, slice(0, QUAD + 1), cot, left, right)
    widen(ext, slice(TD - QUAD - 1, TD), cot, left, right)
    ext[0:1] = top[...].astype(F32)
    ext[TD + 1:TD + 2] = bottom[...].astype(F32)
    apart = offsets_in_band()
    for n in range(2):
        got = stencil_quad(n * (INNER + 1), apart, tab, ext, band)
        for k in range(K):
            g_out[n * ROWS:(n + 1) * ROWS, k * C:(k + 1) * C] = got[k * ROWS:(k + 1) * ROWS]
    mine = jnp.concatenate([field[:ROWS, :], field[(INNER + 1) * ROWS:, :]], axis=0)
    mix = (mix_inner[...] + cells_dot(mine, g_out[...])) * (1.0 / math.sqrt(NLAT * NLON))
    first = core[0] == 0
    low, high = mix[:C // 2], mix[C // 2:]
    mine_out[...] = jnp.where(first, low, high)
    other_out[...] = jnp.where(first, high, low).astype(BF16)


def field_kernel(pos, inner, g_outer, cot, mix, pack, gf_out, send_out, flat, turned, send):
    outer = weigh(g_outer, mix)
    total = cot[...].astype(F32) + jnp.concatenate([outer[:ROWS], inner[...], outer[ROWS:]], axis=0)
    rounded = total.astype(BF16)
    gf_out[...] = rounded
    rounded = rounded.astype(F32)
    southern = pos[0] >= LATS // 2
    for t in range(TD):
        row = pl.multiple_of(jnp.where(southern, TD - 1 - t, t) * FD, FD)
        for h in range(C // 128):
            flat[h, pl.ds(row, FD), :] = rounded[t * FD:(t + 1) * FD, h * 128:(h + 1) * 128]
    pad = jnp.zeros((TP - TD, 128), F32)
    for fq in range(FD // 4):
        for h in range(C // 128):
            pieces = []
            for fr in range(4):
                pieces.append(flat[h, pl.ds(fq * 4 + fr, TD, stride=FD), :])
                pieces.append(pad)
            turned[fq, h * 128:(h + 1) * 128, :] = jnp.concatenate(pieces, axis=0).T
    for fq in range(FD // 4):
        for q in range(CD // 4):
            parts = [
                turned[fq, pl.ds(q * 4 + cr, LONS, stride=CD), :] for cr in range(4)
            ]
            for fr, part in enumerate(swap_blocks(parts)):
                send[q, pl.ds(fq * 4 + fr, LONS, stride=FD), :] = part
    padded = jnp.concatenate([send[q] for q in range(CD // 4)], axis=1).astype(BF16)
    packed = jnp.dot(padded, pack[...], preferred_element_type=F32)
    for q in range(GROUPS):
        send_out[:, q * FP:q * FP + FD, :] = packed[:, q * 128:(q + 1) * 128].reshape(LONS, FD, 128).astype(BF16)
    last = packed[:, GROUPS * 128:].reshape(LONS, FD // 8, 8, 128)
    rest = last[:, 0]
    for b in range(1, FD // 8):
        rest = rest + pltpu.roll(last[:, b], b * REST, 2)
    send_out[:, REST_ROW - 8:, :] = jnp.concatenate([jnp.zeros_like(rest), rest], axis=1).astype(BF16)


def slot_row(slot):
    return slot * FP + FD if slot < GROUPS else GROUPS * FP + (slot - GROUPS) * 8


def piece_row(piece):
    return TAIL_ROW + piece * 8


def dft_kernel(rows, columns, out):
    parts = [columns[:, q * FP:(q + 1) * FP, :].reshape(LONS * FP, 128) for q in range(GROUPS)]
    rest = columns[:, REST_ROW - 8:, :].astype(F32)[:, 8:]
    blocks = [rest if b == 0 else pltpu.roll(rest, 128 - b * REST, 2) for b in range(FD // 8)]
    blocks.append(jnp.zeros_like(rest))
    parts.append(jnp.concatenate(blocks, axis=1).reshape(LONS * FP, 128).astype(BF16))
    got = jnp.dot(rows[...], jnp.concatenate(parts, axis=1), preferred_element_type=F32)
    got = got * (1.0 / math.sqrt(NLON))
    pieces = []
    for half in range(2):
        for slot in range(SLOTS):
            first = slot_row(slot) // 16 * 16
            start = slot_row(slot) - first
            total = columns[half, first:first + 16, :].astype(F32)
            for chip in range(1, CHIPS):
                total = total + columns[2 * chip + half, first:first + 16, :].astype(F32)
            pieces.append(total[start:start + 8])
    step = 2 * MD * REST // 128
    inside = lax.broadcasted_iota(jnp.int32, (step, 128), 1) < REST
    for i in range(LATS):
        mine = got[i * 2 * MD:(i + 1) * 2 * MD]
        for q in range(GROUPS):
            out[i, q * 2 * MD:(q + 1) * 2 * MD, :] = mine[:, q * 128:(q + 1) * 128].astype(BF16)
        quarters = [
            jnp.where(inside, mine[b * step:(b + 1) * step, GROUPS * 128:], 0.0) for b in range(128 // REST)
        ]
        rest = quarters[0]
        for b in range(1, 128 // REST):
            rest = rest + pltpu.roll(quarters[b], b * REST, 1)
        out[i, GROUPS * 2 * MD:, :] = jnp.concatenate([rest] + pieces, axis=0).astype(BF16)


HALF = LATS // 2 * TP


def legendre_kernel(pos, cosines, logscale, out, coef, prev_s, early_s, scale_s, rows):
    block = pl.program_id(0)
    order = pos[0] * MD + lax.broadcasted_iota(jnp.int32, (MD, 128), 0)
    order_f = order.astype(F32)

    @pl.when(block == 0)
    def _():
        prev_s[...] = jnp.zeros_like(prev_s)
        early_s[...] = jnp.zeros_like(early_s)
        scale_s[...] = logscale[...]

    lane = lax.broadcasted_iota(jnp.int32, (MD, 128), 1)
    degree = block * LB + (lane & (LB - 1))
    deg_f = degree.astype(F32)
    higher = degree > order
    lower_a = jnp.where(higher, deg_f * deg_f - order_f * order_f, 1.0)
    factor_a = jnp.where(higher, jnp.sqrt((4.0 * deg_f * deg_f - 1.0) / lower_a), 0.0)
    before = deg_f - 1.0
    upper_b = jnp.maximum(before * before - order_f * order_f, 0.0)
    lower_b = jnp.maximum(4.0 * before * before - 1.0, 1.0)
    factor_b = jnp.sqrt(upper_b / lower_b)
    coef[...] = jnp.where(lane < LB, factor_a, factor_b)

    x = jnp.broadcast_to(cosines[...], (MD, 128))
    prev = prev_s[...]
    early = early_s[...]
    factor = jnp.exp(scale_s[...])
    for step in range(LB):
        a = jnp.broadcast_to(coef[:, step:step + 1], (MD, 128))
        b = jnp.broadcast_to(coef[:, LB + step:LB + step + 1], (MD, 128))
        seed = jnp.where(order == block * LB + step, 1.0, 0.0)
        fresh = a * (x * prev - b * early) + seed
        rows[step * MD:(step + 1) * MD, :] = fresh * factor
        early, prev = prev, fresh
    biggest = jnp.maximum(jnp.abs(prev), jnp.abs(early))
    divisor = jnp.where(biggest > 0.0, biggest, 1.0)
    prev_s[...] = prev / divisor
    early_s[...] = early / divisor
    scale_s[...] = scale_s[...] + jnp.log(divisor)
    for m in range(MD):
        side = (m % 2) * 128
        out[m // 2, :, side:side + 128] = rows[pl.ds(m, LB, stride=MD), :].astype(BF16)


MSTEP = 8


def synthesis_kernel(spec, pack, leg, out, lined, rows):
    step = pl.program_id(0)

    @pl.when(step == 0)
    def _():
        packed = []
        for i in range(LATS):
            groups = [spec[i, q * 2 * MD:(q + 1) * 2 * MD, :] for q in range(GROUPS)]
            rest = spec[i, GROUPS * 2 * MD:GROUPS * 2 * MD + 32, :].astype(F32)[:2 * MD * REST // 128]
            blocks = [rest if b == 0 else pltpu.roll(rest, 128 - b * REST, 1) for b in range(128 // REST)]
            groups.append(jnp.concatenate(blocks, axis=0).astype(BF16))
            packed.append(jnp.concatenate(groups, axis=1))
        padded = lax.dot_general(
            jnp.concatenate(packed, axis=0), pack[...], (((1,), (1,)), ((), ())), preferred_element_type=F32
        )
        padded = [padded[i * 2 * MD:(i + 1) * 2 * MD] for i in range(LATS)]
        for q in range(CD // 4):
            span = slice(q * 128, (q + 1) * 128)
            north = [padded[i][:, span] for i in range(LATS // 2)]
            south = [padded[LATS - 1 - i][:, span] for i in range(LATS // 2)]
            for odd in range(2):
                parts = [n - s if odd else n + s for n, s in zip(north, south)]
                for cr, part in enumerate(swap_blocks(parts)):
                    for p in range(2):
                        base = ((odd * 2 + p) * CD + q * 4 + cr) * MD
                        lined[base:base + MD, :] = part[p * MD:(p + 1) * MD]

    wide = 2 * CD
    odd_lane = (lax.broadcasted_iota(jnp.int32, (wide, L), 1) & 1) == 1
    zero = jnp.zeros((2 * wide, HALF), F32)
    for pair in range(MSTEP // 2):
        first = step * MSTEP + 2 * pair
        mine = [lined[pl.ds(first + side, 2 * wide, stride=MD), :] for side in range(2)]
        lhs = jnp.concatenate(
            [jnp.concatenate([mine[0], zero], axis=1), jnp.concatenate([zero, mine[1]], axis=1)], axis=0
        ).astype(BF16)
        got = lax.dot_general(
            lhs, leg[pair], (((1,), (1,)), ((), ())), preferred_element_type=F32
        ) * math.sqrt(4.0 * math.pi / NLAT)
        done = [
            jnp.where(odd_lane, got[wide:2 * wide], got[:wide]),
            jnp.where(odd_lane, got[2 * wide:3 * wide], got[3 * wide:]),
        ]
        for side in range(2):
            for h in range(L // 128):
                rows[h, pl.ds(2 * pair + side, wide, stride=MSTEP), :] = done[side][:, h * 128:(h + 1) * 128]
    for p in range(2):
        for c in range(CD):
            base = (p * CD + c) * MSTEP
            for h in range(L // 128):
                out[p, c, :, h * 128:(h + 1) * 128] = rows[h, base:base + MSTEP, :]


HALF_TILES = C // 32 * (K * C // 128)


def tiles_of(chip):
    return [(slot, *divmod(SLOTS * chip + slot, K * C // 128)) for slot in range(SLOTS) if SLOTS * chip + slot < HALF_TILES]


def chip_sum_kernel(mine, other, send, out, near_rows, far_rows, sems):
    total = (mine[...] + other[...].astype(F32)).astype(BF16)
    near_rows[...] = jnp.zeros_like(near_rows)
    far_rows[...] = jnp.zeros_like(far_rows)
    for chip in range(CHIPS):
        for slot, row, col in tiles_of(chip):
            for core in range(2):
                first = core * (C // 4) + row * 8
                tile = total[first:first + 8, col * 128:(col + 1) * 128]
                if slot < GROUPS:
                    near_rows[slot, 2 * chip + core] = tile
                else:
                    far = (slot - GROUPS) * 8
                    far_rows[2 * chip + core, far:far + 8, :] = tile
    copies = [
        pltpu.make_async_copy(near_rows.at[q], out.at[:, q * FP + FD:(q + 1) * FP, :], sems.at[q]) for q in range(GROUPS)
    ]
    copies.append(pltpu.make_async_copy(far_rows, out.at[:, GROUPS * FP:REST_ROW, :], sems.at[GROUPS]))
    for copy in copies:
        copy.start()
    for copy in copies:
        copy.wait()


def copies_kernel(spec, out):
    for piece in range(2 * SLOTS):
        row = piece_row(piece)
        first = row // 16 * 16
        total = spec[0, first:first + 16, :].astype(F32)
        for i in range(1, LATS):
            total = total + spec[i, first:first + 16, :].astype(F32)
        total = total[row - first:row - first + 8].astype(BF16)
        for chip in range(CHIPS):
            out[chip, piece * 8:(piece + 1) * 8, :] = total


def mix_kernel(held, parts, *rest):
    out, rows, sems = rest[-3:]
    copies = []
    for half in range(2):
        for chip in range(CHIPS):
            for slot, row, col in tiles_of(chip):
                k, d = divmod(col, C // 128)
                piece = (half * SLOTS + slot) * 8
                rows[half, k, row * 8:row * 8 + 8, d * 128:(d + 1) * 128] = parts[chip, piece:piece + 8, :].astype(F32)
        base = pl.multiple_of(half * (C // 2) + held[0] * (C // 4), 8)
        copies.append(pltpu.make_async_copy(rows.at[half], out.at[:, pl.ds(base, C // 4)], sems.at[half]))
        copies[-1].start()
    for copy in copies:
        copy.wait()


def dft_rows():
    order = np.arange(M).reshape(LATS, 1, MD)
    order = np.broadcast_to(order, (LATS, 2, MD)).reshape(-1)
    part = np.broadcast_to(np.arange(2).reshape(1, 2, 1), (LATS, 2, MD)).reshape(-1)
    angle = 2.0 * np.pi / NLON * ((order[:, None] * np.arange(NLON)[None, :]) % NLON)
    angle = angle.astype(np.float32)
    rows = np.where(part[:, None] == 0, np.cos(angle), -np.sin(angle))
    padded = np.zeros((2 * M, LONS, FP), np.float32)
    padded[:, :, :FD] = rows.reshape(2 * M, LONS, FD)
    return padded.reshape(2 * M, LONS * FP).astype(ml_dtypes.bfloat16)


def packing():
    pack = np.zeros((CD * TP, CD * TP), np.float32)
    for c in range(CD):
        for t in range(TD):
            pack[c * TP + t, c * TD + t] = 1.0
    return pack.astype(ml_dtypes.bfloat16)


def latitudes():
    angle = ((np.arange(NLAT) + 0.5) * (np.pi / NLAT)).reshape(LATS, TD)
    cosine = np.zeros((LATS, TP), np.float32)
    logsine = np.zeros((LATS, TP), np.float32)
    cosine[:, :TD] = np.cos(angle)
    logsine[:, :TD] = np.log(np.sin(angle))
    half = LATS // 2
    return cosine[:half].reshape(1, -1), logsine[:half].reshape(1, -1)


def seed_logs():
    degree = np.arange(M, dtype=np.float64)
    steps = np.log((2.0 * degree + 1.0) / (2.0 * degree + 2.0))
    prefix = np.concatenate([np.zeros(1), np.cumsum(steps)[:-1]])
    return (0.5 * np.log((2.0 * degree + 1.0) / (4.0 * np.pi)) + 0.5 * prefix).astype(np.float32)


def band_lanes():
    mark = np.zeros((TD, 3, 256), np.float32)
    for t in range(TD):
        for rr in range(3):
            start = (t % QUAD + rr) * XW
            mark[t, rr, start:start + XW] = 1.0
    return mark


def tap_rows(taps, offsets, counts, first_row):
    slot_ids = lax.broadcasted_iota(jnp.int32, taps.shape, 3)
    live = jnp.where(slot_ids < counts[:, None, None, None], taps, 0.0).astype(BF16).astype(F32)
    shift = (R - offsets).astype(F32)[:, None]
    both = jnp.concatenate([live, shift], axis=1)
    both = jnp.pad(both, ((1, 1), (0, 0), (0, 0), (0, 0)))
    return lax.dynamic_slice_in_dim(both, first_row, TD + 2, 0)


def tap_table(both):
    marks = band_lanes()
    table = 0.0
    for rr in range(3):
        mine = both[rr:rr + TD, :, 2 - rr, :].reshape(TD, (K + 1) * S)
        table = table + mine[:, :, None] * marks[:, rr][:, None, :]
    return table


def on_device(field, cotangent, mix_weight, taps, offsets, counts):
    lat_pos = lax.axis_index(LAT)
    up = [(i, (i + 1) % LONS) for i in range(LONS)]
    down = [(j, i) for i, j in up]
    left = lax.ppermute(cotangent[:, FD - R:], LON, up)
    right = lax.ppermute(cotangent[:, :R], LON, down)
    whole = pl.BlockSpec(memory_space=pltpu.VMEM)
    near_cot, rims = near(cotangent), (near(left), near(right))
    edge = (1, XW, C)
    edge_rows = call(
        edge_kernel,
        (near_shape(edge, BF16), near_shape(edge, BF16)),
        1,
        in_specs=[whole] * 4,
        name="edge_rows",
    )(near(cotangent[:1]), near(cotangent[TD - 1:]), *rims)
    north = [(i, i + 1) for i in range(LATS - 1)]
    south = [(j, i) for i, j in north]
    top = lax.ppermute(edge_rows[1], LAT, north)
    bottom = lax.ppermute(edge_rows[0], LAT, south)

    tap_part, _ = lax.optimization_barrier((tap_rows(taps, offsets, counts, lat_pos * TD), edge_rows))
    tab = tap_table(tap_part)
    cells = TD * FD
    core = jnp.reshape(lax.axis_index(CORE), (1,)).astype(jnp.int32)
    scalar = pl.BlockSpec(memory_space=pltpu.SMEM)
    anywhere = pl.BlockSpec(memory_space=pl.ANY)
    half = (C // 2, K * C)
    near_field = near(field.reshape(cells, C))
    scratch = [pltpu.VMEM((TD + 2, XW, C), F32), pltpu.VMEM((K * ROWS, 256), F32)]
    mix_near = near(mix_weight)
    field_inner, mix_inner = call(
        inner_kernel,
        (near_shape((INNER * ROWS, C), F32), near_shape((C, K * C), F32)),
        2,
        in_specs=[whole] * 6,
        scratch_shapes=[pltpu.VMEM((INNER * ROWS, K * C), BF16)] + scratch,
        name="stencil_inner",
    )(near(tab), near_cot, *rims, near_field, mix_near)
    pack = near(jnp.asarray(packing()))
    top, bottom, pack = lax.optimization_barrier((top, bottom, pack))
    g_outer, mix_mine, mix_other = call(
        outer_kernel,
        (near_shape((2 * ROWS, K * C), BF16), near_shape(half, F32), near_shape(half, BF16)),
        2,
        in_specs=[scalar] + [whole] * 8,
        scratch_shapes=scratch,
        name="stencil_outer",
    )(core, near(tab), near_cot, *rims, near(top), near(bottom), near_field, near(mix_inner))
    swap = [(0, 1), (1, 0)]
    mix_other = lax.ppermute(mix_other, CORE, swap)

    pos = jnp.reshape(lat_pos, (1,)).astype(jnp.int32)
    grad_field, send = call(
        field_kernel,
        (shape((cells, C), BF16), shape((LONS, SENT, 128), BF16)),
        5,
        in_specs=[scalar] + [whole] * 5,
        scratch_shapes=[
            pltpu.VMEM((C // 128, cells, 128), F32),
            pltpu.VMEM((FD // 4, C, 128), F32),
            pltpu.VMEM((CD // 4, LONS * FD, 128), F32),
        ],
        name="grad_field",
    )(pos, near(field_inner), near(g_outer), near(cotangent.reshape(cells, C)), near(mix_near), near(pack))
    send = call(
        chip_sum_kernel,
        shape((LONS, SENT, 128), BF16),
        2,
        in_specs=[whole, whole, anywhere],
        out_specs=anywhere,
        scratch_shapes=[
            pltpu.VMEM((GROUPS, LONS, FP - FD, 128), BF16),
            pltpu.VMEM((LONS, REST_ROW - GROUPS * FP, 128), BF16),
            pltpu.SemaphoreType.DMA((GROUPS + 1,)),
        ],
        input_output_aliases={2: 0},
        name="mix_chip_sum",
    )(near(mix_mine), near(mix_other), send)
    columns = lax.all_to_all(send, LON, 0, 0, tiled=True)

    cosine, logsine = latitudes()
    first_order = lat_pos * MD
    seeds = lax.dynamic_slice_in_dim(jnp.asarray(seed_logs()), first_order, MD, 0)
    orders = (first_order + jnp.arange(MD, dtype=jnp.int32)).astype(F32)
    logscale = seeds[:, None] + orders[:, None] * logsine
    logscale, _ = lax.optimization_barrier((logscale, send))
    table = call(
        legendre_kernel,
        shape((MD // 2, L, 2 * HALF), BF16),
        9,
        grid_spec=pltpu.PrefetchScalarGridSpec(
            num_scalar_prefetch=1,
            grid=(L // LB,),
            in_specs=[
                pl.BlockSpec((1, HALF), lambda b, pos: (0, 0)),
                pl.BlockSpec((MD, HALF), lambda b, pos: (0, 0)),
            ],
            out_specs=pl.BlockSpec((MD // 2, LB, 2 * HALF), lambda b, pos: (0, b, 0)),
            scratch_shapes=[
                pltpu.VMEM((MD, 128), F32),
                pltpu.VMEM((MD, HALF), F32),
                pltpu.VMEM((MD, HALF), F32),
                pltpu.VMEM((MD, HALF), F32),
                pltpu.VMEM((LB * MD, HALF), F32),
            ],
        ),
        name="legendre",
    )(pos, jnp.asarray(cosine), logscale)
    columns, table = lax.optimization_barrier((columns, table))

    spectra = call(dft_kernel, near_shape((LATS, SPREAD, 128), BF16), 2, in_specs=[whole, whole], name="dft")(
        near(jnp.asarray(dft_rows())), near(columns)
    )
    spec = lax.all_to_all(spectra, LAT, 0, 0, tiled=True)
    mix_copies = call(copies_kernel, near_shape((CHIPS, 2 * SLOTS * 8, 128), BF16), 2, in_specs=[whole], name="mix_copies")(near(spec))
    mix_mine = lax.all_to_all(mix_copies, CHIP, 0, 0, tiled=True)

    grad_spectra = call(
        synthesis_kernel,
        shape((2, CD, MD, L), F32),
        6,
        grid_spec=pltpu.PrefetchScalarGridSpec(
            num_scalar_prefetch=0,
            grid=(MD // MSTEP,),
            in_specs=[
                whole,
                whole,
                pl.BlockSpec((MSTEP // 2, L, 2 * HALF), lambda b: (b, 0, 0)),
            ],
            out_specs=pl.BlockSpec((2, CD, MSTEP, L), lambda b: (0, 0, b, 0)),
            scratch_shapes=[
                pltpu.VMEM((4 * CD * MD, HALF), F32),
                pltpu.VMEM((L // 128, 2 * CD * MSTEP, 128), F32),
            ],
        ),
        name="synthesis",
    )(near(spec), near(pack), table)
    mix_mine, grad_spectra = lax.optimization_barrier((mix_mine, grad_spectra))
    mix_other = lax.ppermute(mix_mine, CORE, swap)
    grad_mix = ()
    for held, parts in ((core, mix_mine), (1 - core, mix_other)):
        grad_mix = (
            call(
                mix_kernel,
                shape((K, C, C), F32),
                1,
                in_specs=[scalar, whole] + [anywhere] * len(grad_mix),
                out_specs=anywhere,
                scratch_shapes=[pltpu.VMEM((2, K, C // 4, C), F32), pltpu.SemaphoreType.DMA((2,))],
                input_output_aliases={2: 0} if grad_mix else {},
                name="mix_out",
            )(held, near(parts), *grad_mix),
        )
    return (grad_field.reshape(TD, FD, C), jnp.transpose(grad_spectra, (0, 2, 1, 3)), grad_mix[0])


def solution(mesh):
    chips = Mesh(mesh.devices.reshape(LATS, CHIPS, 2), (LAT, CHIP, CORE))
    placed = (P(LAT, LON, None), P(LAT, LON, None), P(), P(), P(), P())
    return jax.shard_map(
        on_device,
        mesh=chips,
        in_specs=placed,
        out_specs=(P(LAT, LON, None), P(None, LAT, LON, None), P()),
        check_vma=False,
    )
```
